32 devices in a mesh: seq: 8 (over y, x, core), wt: 4 (over z).
Axes of the slice: x: 2, y: 2, z: 4, core: 2. Of those that a mesh axis runs over, the one named last changes fastest.
Arguments:
- inputs: bfloat16 [8, 1024, 1024], P('wt', 'seq'), may hold values from -5 to 5
- cotangent: bfloat16 [8, 1024, 1024], P('wt', 'seq'), may hold values from -6 to 6
- decay: float32 [8, 1024, 8], P('wt', 'seq'), may hold values from 0.3 to 1
- w_query: bfloat16 [1024, 1024], P('wt'), may hold values from -0.1875 to 0.1875
- w_key: bfloat16 [1024, 1024], P('wt'), may hold values from -0.1875 to 0.1875
- w_value: bfloat16 [1024, 2048], P('wt'), may hold values from -0.1875 to 0.1875
- w_gate_out: bfloat16 [1024, 2048], P('wt'), may hold values from -0.1875 to 0.1875
- w_out: bfloat16 [1024, 2048], P('wt'), may hold values from -0.125 to 0.125
- w_ffn_gate: bfloat16 [1024, 2816], P('wt'), may hold values from -0.1875 to 0.1875
- w_ffn_up: bfloat16 [1024, 2816], P('wt'), may hold values from -0.1875 to 0.1875
- w_ffn_down: bfloat16 [1024, 2816], P('wt'), may hold values from -0.109375 to 0.109375
- w_beta: bfloat16 [1024, 8], replicated, may hold values from -1 to 1
- conv_weight: float32 [4, 4096], replicated, may hold values from -3 to 3
- norm_in: float32 [1024], replicated, may hold values from 0.5 to 1.5
- norm_mid: float32 [1024], replicated, may hold values from 0.5 to 1.5
- norm_head: float32 [256], replicated, may hold values from 0.5 to 1.5
Outputs:
- layer_out: bfloat16 [8, 1024, 1024], P('wt', 'seq')
- grad_input: float32 [8, 1024, 1024], P('wt', 'seq')
- grad_query: float32 [1024, 1024], P('wt')
- grad_key: float32 [1024, 1024], P('wt')
- grad_value: float32 [1024, 2048], P('wt')
- grad_gate_out: float32 [1024, 2048], P('wt')
- grad_out: float32 [1024, 2048], P('wt')
- slope_feedforward_switch: float32 [1024, 2816], P('wt')
- grad_ffn_up: float32 [1024, 2816], P('wt')
- grad_ffn_down: float32 [1024, 2816], P('wt')
- grad_beta: float32 [1024, 8], replicated
- grad_conv: float32 [4, 4096], replicated
- grad_norm_in: float32 [1024], replicated
- grad_norm_mid: float32 [1024], replicated
- grad_norm_head: float32 [256], replicated
The draws below stay inside these ranges and needn't reach their ends.
All inputs are finite; a program needn't handle non-finite values.
Results may differ from the reference program's by a relative error of at most 0.0095.
The reference program's roundings to bfloat16 on the way count: a program that leaves them out, or rounds other values in their place, can miss the bound.
Values may be sent and summed in bfloat16 or wider, within the bound.
No kernel may reach another device: no remote copies, remote signals or barrier semaphores. Data moves between devices by JAX's collectives and lax.ppermute only.
A program may use at most 320 MiB of HBM per device.

```python
import jax
import jax.numpy as jnp
from jax import lax

D = 1024
H = 8
DK = 128
DV = 256
FF = 2816
CONV = 4
GROUP = 64
TOK_BLK = 128
SEQS = 8
SEQLEN = 1024
HK = 1024
HV = 2048
CH = 4096


def shared_parts(key):
    heads_order = jax.random.permutation(jax.random.fold_in(key, 11), H)
    weak_heads = heads_order < H // 2
    sign_bits = jax.random.randint(jax.random.fold_in(key, 12), (D,), 0, 2)
    signs = (2 * sign_bits - 1).astype(jnp.float32)
    return (weak_heads, signs)


def draw_inputs(key, part):
    weak_heads, signs = shared_parts(key)
    noise_key = jax.random.fold_in(key, 13)
    noise = jnp.clip(jax.random.normal(noise_key, (SEQS, SEQLEN, D)), -4.0, 4.0)
    return (noise + signs).astype(jnp.bfloat16)


def draw_w_beta(key, part):
    weak_heads, signs = shared_parts(key)
    noise_key = jax.random.fold_in(key, 14)
    noise = jnp.clip(jax.random.normal(noise_key, (D, H)), -4.0, 4.0)
    shifted = jnp.where(weak_heads[None, :], -7.78 / D, 0.0) * signs[:, None]
    return (noise * D ** (-0.5) + shifted).astype(jnp.bfloat16)


def draw_decay(key, part):
    weak_heads, signs = shared_parts(key)
    streams = jax.random.split(jax.random.fold_in(key, 15), 5)
    share = 0.6
    picked = jax.random.uniform(streams[0], (SEQS, 1, H)) < share
    forgetful = jnp.logical_and(picked, jnp.logical_not(weak_heads)[None, None, :])
    base_rate = jnp.where(forgetful, 1.0 / 40.0, 0.2 / SEQLEN)
    blocks = SEQLEN // TOK_BLK
    block_scale = jnp.exp(jax.random.uniform(streams[1], (SEQS, blocks, 1, H), minval=-0.7, maxval=0.7))
    block_scale = jnp.broadcast_to(block_scale, (SEQS, blocks, TOK_BLK, H)).reshape(SEQS, SEQLEN, H)
    token_scale = jnp.exp(jax.random.uniform(streams[2], (SEQS, SEQLEN, H), minval=-0.4, maxval=0.4))
    descent_stepsize = base_rate * block_scale * token_scale
    symbol_locations = jax.random.randint(streams[3], (SEQS, 1, 2), 0, SEQLEN)
    symbol_indices = lax.broadcasted_iota(jnp.int32, (SEQS, SEQLEN, 2), 1)
    symbol_batches = jnp.any(symbol_indices == symbol_locations, axis=2)[:, :, None]
    multiplier_coefficient = jax.random.uniform(streams[4], (SEQS, SEQLEN, H), minval=0.5, maxval=0.8)
    return (jnp.exp(-descent_stepsize) * jnp.where(symbol_batches, multiplier_coefficient, 1.0)).astype(jnp.float32)


def levels(own_key, extent, cuts, least, largest):
    loudness, own = 1.0, jax.random.fold_in(own_key, 6)
    for position, parts in cuts:
        draws = jnp.exp(jax.random.uniform(jax.random.fold_in(own, position), (parts,), jnp.float32, least / len(cuts), largest / len(cuts)))
        loudness = loudness * jnp.repeat(draws, extent[position] // parts).reshape([-1 if axis == position else 1 for axis in range(len(extent))])
    return loudness


def normal_values(rng, shape, scale, reach, shards=(), kind=jnp.bfloat16):
    values = jax.random.normal(rng, shape, jnp.float32) * scale
    if len(shards) > 0:
        values = levels(rng, shape, shards, -0.22, 0.18) * values
    return jnp.clip(values, min=-reach, max=reach).astype(kind)


def setup_inputs(seed: int = 0) -> dict:
    key_list = jax.random.split(jax.random.key(seed), 17)
    inputs = draw_inputs(jax.random.fold_in(key_list[16], 71), 0)
    cotangent = normal_values(key_list[1], (SEQS, SEQLEN, D), 1.0, 6.0, ((0, 4), (1, 8)))
    decay = draw_decay(jax.random.fold_in(key_list[16], 71), 0)
    w_query = normal_values(key_list[3], (D, HK), D ** -0.5, 0.1875, ((0, 4),))
    w_key = normal_values(key_list[4], (D, HK), D ** -0.5, 0.1875, ((0, 4),))
    w_value = normal_values(key_list[5], (D, HV), D ** -0.5, 0.1875, ((0, 4),))
    w_gate_out = normal_values(key_list[6], (D, HV), D ** -0.5, 0.1875, ((0, 4),))
    w_out = normal_values(key_list[7], (D, HV), HV ** -0.5, 0.125, ((0, 4),))
    w_ffn_gate = normal_values(key_list[8], (D, FF), D ** -0.5, 0.1875, ((0, 4),))
    w_ffn_up = normal_values(key_list[9], (D, FF), D ** -0.5, 0.1875, ((0, 4),))
    w_ffn_down = normal_values(key_list[10], (D, FF), FF ** -0.5, 0.109375, ((0, 4),))
    w_beta = draw_w_beta(jax.random.fold_in(key_list[16], 71), 0)
    conv_weight = normal_values(key_list[12], (CONV, CH), 0.5, 3.0, (), jnp.float32)
    norm_in = jnp.clip(1.0 + 0.1 * jax.random.normal(key_list[13], (D,), jnp.float32), 0.5, 1.5)
    norm_mid = jnp.clip(1.0 + 0.1 * jax.random.normal(key_list[14], (D,), jnp.float32), 0.5, 1.5)
    norm_head = jnp.clip(1.0 + 0.1 * jax.random.normal(key_list[15], (DV,), jnp.float32), 0.5, 1.5)
    return dict(inputs=inputs, cotangent=cotangent, decay=decay, w_query=w_query, w_key=w_key, w_value=w_value, w_gate_out=w_gate_out, w_out=w_out, w_ffn_gate=w_ffn_gate, w_ffn_up=w_ffn_up, w_ffn_down=w_ffn_down, w_beta=w_beta, conv_weight=conv_weight, norm_in=norm_in, norm_mid=norm_mid, norm_head=norm_head)


highest = lax.Precision.HIGHEST

@jax.custom_vjp
def low(v):
    return lax.optimization_barrier(v.astype(jnp.bfloat16)).astype(jnp.float32)

@jax.custom_vjp
def low_back(v):
    return v

def low_keep(v):
    return (low(v), None)

def low_pass(kept, grad):
    return (grad,)

def back_keep(v):
    return (v, None)

def back_low(kept, grad):
    return (low(grad),)
low.defvjp(low_keep, low_pass)
low_back.defvjp(back_keep, back_low)

def project(left, right):
    return jnp.dot(left.astype(jnp.float32), right.astype(jnp.float32), precision=highest, preferred_element_type=jnp.float32)

def project_back(left, right):
    return lax.dot_general(left.astype(jnp.float32), right.astype(jnp.float32), (((1,), (1,)), ((), ())), precision=highest, preferred_element_type=jnp.float32)

def rms_norm(values, scaling):
    return values * lax.rsqrt(lax.optimization_barrier(jnp.mean(values * values, axis=-1, keepdims=True)) + 1e-05) * scaling

def head_norm(mixed, out_gate, scaling):
    multiplier_coefficient = lax.rsqrt(lax.optimization_barrier(jnp.mean(mixed * mixed, axis=-1, keepdims=True)) + 1e-05)
    gate_heads = out_gate.reshape(mixed.shape)
    return (mixed * multiplier_coefficient * scaling * jax.nn.silu(gate_heads)).reshape(out_gate.shape)

def pre_mix(padded, conv_weight, beta_logit):
    length = padded.shape[1] - (CONV - 1)
    summed = padded[:, 0:length] * conv_weight[0]
    for tap_index in range(1, CONV):
        summed = summed + padded[:, tap_index:tap_index + length] * conv_weight[tap_index]
    active = jax.nn.silu(summed)
    leading = active.shape[:2]
    queries = active[..., :H * DK].reshape(leading + (H, DK))
    keys_raw = active[..., H * DK:2 * H * DK].reshape(leading + (H, DK))
    keys_unit = keys_raw * lax.rsqrt(lax.optimization_barrier(jnp.sum(keys_raw * keys_raw, axis=-1, keepdims=True)) + 1e-06)
    values = active[..., 2 * H * DK:].reshape(leading + (H, DV))
    return (queries, keys_unit, values, jax.nn.sigmoid(beta_logit))

def group_step(state, pieces):
    queries, keys_unit, values, betas, log_decay = pieces
    length = queries.shape[1]
    row_ids = lax.broadcasted_iota(jnp.int32, (length, length), 0)
    col_ids = lax.broadcasted_iota(jnp.int32, (length, length), 1)
    causal = row_ids >= col_ids
    strict = row_ids > col_ids
    running = jnp.cumsum(log_decay, axis=1)
    value_spread = jnp.where(causal, running[:, :, None] - running[:, None, :], 0.0)
    decay_mat = jnp.where(causal, jnp.exp(value_spread), 0.0)
    key_gram = jnp.einsum('hid,hjd->hij', keys_unit, keys_unit, precision=highest)
    system = jnp.eye(length, dtype=state.dtype) + jnp.where(strict, betas[:, :, None] * key_gram * decay_mat, 0.0)
    growth = jnp.exp(running)
    recalled = jnp.einsum('hid,hde->hie', keys_unit, state, precision=highest)
    target = betas[:, :, None] * (values - growth[:, :, None] * recalled)
    deltas = jax.scipy.linalg.solve_triangular(system, target, lower=True, unit_diagonal=True)
    scores = jnp.einsum('hid,hjd->hij', queries, keys_unit, precision=highest) * decay_mat
    read_out = growth[:, :, None] * jnp.einsum('hid,hde->hie', queries, state, precision=highest)
    read_out = read_out + jnp.einsum('hij,hje->hie', scores, deltas, precision=highest)
    final_log = running[:, -1:]
    weights_in = jnp.exp(final_log - running)
    new_state = jnp.exp(final_log)[:, :, None] * state + jnp.einsum('hid,hie->hde', keys_unit * weights_in[:, :, None], deltas, precision=highest)
    return (new_state, read_out)

def delta_rule(state, queries, keys_unit, values, betas, log_decay):
    length = queries.shape[0]
    blocks = length // GROUP

    def arrange(array):
        return jnp.swapaxes(array.reshape((blocks, GROUP) + array.shape[1:]), 1, 2)
    final_state, read_out = lax.scan(jax.checkpoint(group_step), state, (arrange(queries), arrange(keys_unit), arrange(values), arrange(betas), arrange(log_decay)))
    ordered = jnp.swapaxes(read_out, 1, 2)
    return (ordered.reshape((length,) + ordered.shape[2:]), final_state)

def forward(rows_in, decay_seq, query_w, key_w, value_w, gate_w, out_w, ffn_gate_w, ffn_up_w, ffn_down_w, beta_w, conv_w, gain_in, gain_mid, gain_head):
    length = rows_in.shape[0]
    normed_in = low(rms_norm(rows_in, gain_in))
    conv_in = low(low_back(jnp.concatenate([project(normed_in, query_w), project(normed_in, key_w), project(normed_in, value_w)], axis=1)))
    out_gate = low_back(project(normed_in, gate_w))
    beta_logit = low_back(project(normed_in, beta_w))
    padded = jnp.pad(conv_in, ((CONV - 1, 0), (0, 0)))[None]
    queries, keys_unit, values, betas = pre_mix(padded, conv_w, beta_logit.reshape(1, length, H))
    state = jnp.zeros((H, DK, DV), rows_in.dtype)
    mixed = delta_rule(state, queries[0], keys_unit[0], values[0], betas[0], jnp.log(decay_seq))[0]
    headed = low(head_norm(mixed[None], out_gate[None], gain_head)[0])
    residual = rows_in + low_back(project_back(headed, out_w))
    normed_mid = low(rms_norm(residual, gain_mid))
    gate_pre = low_back(project(normed_mid, ffn_gate_w))
    up_pre = low_back(project(normed_mid, ffn_up_w))
    hidden = low(jax.nn.silu(gate_pre) * up_pre)
    return residual + low_back(project_back(hidden, ffn_down_w))

def reference(inputs, cotangent, decay, w_query, w_key, w_value, w_gate_out, w_out, w_ffn_gate, w_ffn_up, w_ffn_down, w_beta, conv_weight, norm_in, norm_mid, norm_head):
    params = tuple((p.astype(jnp.float32) for p in (w_query, w_key, w_value, w_gate_out, w_out, w_ffn_gate, w_ffn_up, w_ffn_down, w_beta, conv_weight, norm_in, norm_mid, norm_head)))

    def one_sequence(totals, items):
        rows_in, rows_cot, decay_seq = items

        def apply_layer(rows_val, *weights):
            return forward(rows_val, decay_seq, *weights)
        result, pullback = jax.vjp(apply_layer, rows_in, *params)
        grads = pullback(rows_cot)
        updated = tuple((a + b for a, b in zip(totals, grads[1:])))
        return (updated, (result, grads[0]))
    zeros_init = tuple((jnp.zeros_like(p) for p in params))
    totals, (results, d_inputs) = lax.scan(one_sequence, zeros_init, (inputs.astype(jnp.float32), cotangent.astype(jnp.float32), decay))
    return (results.astype(jnp.bfloat16), d_inputs, totals[0], totals[1], totals[2], totals[3], totals[4], totals[5], totals[6], totals[7], totals[8], totals[9], totals[10], totals[11], totals[12])
```

```python
import jax
import jax.numpy as jnp
from jax import lax
from jax.experimental import pallas as pl
from jax.experimental.pallas import tpu as pltpu
from jax.sharding import PartitionSpec as P

H = 8
DK = 128
DV = 256
CONV = 4
HALO = 16
bf16 = jnp.bfloat16
f32 = jnp.float32


def parts(values):
    high = values.astype(bf16)
    low = (values - high.astype(f32)).astype(bf16)
    return high, low


def dot(left, right, dims):
    return lax.dot_general(left, right, (dims, ((), ())), preferred_element_type=f32)


def mul(left, right):
    (lh, ll), (rh, rl) = left, right
    wide = dot(jnp.concatenate([lh, ll], 1), jnp.concatenate([rh, rh], 0), ((1,), (0,)))
    return wide + dot(lh, rl, ((1,), (0,)))


def mul_t(left, right):
    (lh, ll), (rh, rl) = left, right
    wide = dot(jnp.concatenate([lh, ll], 1), jnp.concatenate([rh, rh], 1), ((1,), (1,)))
    return wide + dot(lh, rl, ((1,), (1,)))


def cat_parts(values):
    return jnp.concatenate(parts(values), 1)


def from_cat(both):
    half = both.shape[1] // 2
    return both[:, :half], both[:, half:]


def iotas(size):
    return (
        lax.broadcasted_iota(jnp.int32, (size, size), 0),
        lax.broadcasted_iota(jnp.int32, (size, size), 1),
    )


def column(row, rows, cols):
    return jnp.sum(jnp.where(rows == cols, row, 0.0), axis=1, keepdims=True)


def unit_inverse(lower, rows, cols):
    size = lower.shape[0]
    level = 0
    inverse = jnp.where(rows == cols, 1.0, 0.0)
    while (1 << level) < size:
        pair_up = (rows >> (level + 1)) == (cols >> (level + 1))
        corner = pair_up & (((rows >> level) & 1) == 1) & (((cols >> level) & 1) == 0)
        block = jnp.where(corner, lower, 0.0)
        if level == 0:
            inverse = inverse - block
        else:
            whole = parts(inverse)
            inverse = inverse - mul(whole, parts(mul(parts(block), whole)))
        level += 1
    return inverse


def conv_rows(conv_ref, halo_ref, rows_ref, taps_ref, chunk, seq, slot):
    size = conv_ref.shape[2]
    before = conv_ref[jnp.maximum(chunk - 1, 0), seq, size - HALO :, :]
    before = jnp.where(chunk == 0, halo_ref[seq], before)
    rows_ref[slot, :HALO, :] = before.astype(f32)
    rows_ref[slot, HALO:, :] = conv_ref[chunk, seq].astype(f32)
    total = None
    for tap in range(CONV):
        start = HALO - (CONV - 1) + tap
        term = rows_ref[slot, start : start + size, :] * taps_ref[tap : tap + 1, :]
        total = term if total is None else total + term
    return total


def decays(run_ref, chunk, seq, rows, cols):
    size = rows.shape[0]
    run_row = run_ref[chunk, seq][0:1, :]
    run_col = column(run_row, rows, cols)
    spread = jnp.where(rows >= cols, run_col - run_row, 0.0)
    decay_mat = jnp.where(rows >= cols, jnp.exp(spread), 0.0)
    last = run_row[:, size - 1 : size]
    return decay_mat, jnp.exp(run_col), jnp.exp(last - run_col), jnp.exp(last)


def forward_kernel(
    conv_ref, gate_ref, run_ref, taps_ref, gain_ref, state_ref, halo_ref,
    headed_ref, mixed_ref, inverse_ref, scores_ref, delta_ref, starts_ref, end_ref,
    rows_ref, recall_ref, target_ref, query_ref, write_ref, plain_ref,
):
    chunks, seqs, size, _ = conv_ref.shape
    rows, cols = iotas(size)

    def prepare(chunk, _):
        for seq in range(seqs):
            summed = conv_rows(conv_ref, halo_ref, rows_ref, taps_ref, chunk, seq, seq)
            active = summed * jax.nn.sigmoid(summed)
            query = active[:, :DK]
            key = active[:, DK : 2 * DK]
            key = key * lax.rsqrt(jnp.sum(key * key, axis=1, keepdims=True) + 1e-06)
            value = active[:, 2 * DK :]
            beta = jax.nn.sigmoid(gate_ref[chunk, seq, :, DV : DV + 1])
            decay_mat, growth, fade, _ = decays(run_ref, chunk, seq, rows, cols)
            key_parts = parts(key)
            gram = mul_t(key_parts, key_parts)
            lower = jnp.where(rows > cols, beta * gram * decay_mat, 0.0)
            inverse = unit_inverse(lower, rows, cols)
            scores = mul_t(parts(query), key_parts) * decay_mat
            inverse_parts = parts(inverse)
            recall_ref[chunk, seq] = cat_parts(mul(inverse_parts, parts(beta * growth * key)))
            target_ref[chunk, seq] = mul(inverse_parts, parts(beta * value))
            query_ref[chunk, seq] = cat_parts(growth * query)
            write_ref[chunk, seq] = cat_parts((fade * key).T)
            plain_ref[chunk, seq] = cat_parts(scores)
            inverse_ref[chunk, seq] = cat_parts(inverse.T)
            scores_ref[chunk, seq] = cat_parts(scores.T)
        return 0

    lax.fori_loop(0, chunks, prepare, 0)

    def advance(chunk, states):
        following = []
        for seq in range(seqs):
            state = states[seq]
            starts_ref[chunk, seq] = state
            state_parts = parts(state)
            delta = target_ref[chunk, seq] - mul(from_cat(recall_ref[chunk, seq]), state_parts)
            delta_parts = parts(delta)
            read = mul(from_cat(query_ref[chunk, seq]), state_parts)
            read = read + mul(from_cat(plain_ref[chunk, seq]), delta_parts)
            total = jnp.exp(run_ref[chunk, seq][0:1, size - 1 : size])
            following.append(
                total * state + mul(from_cat(write_ref[chunk, seq]), delta_parts)
            )
            delta_ref[chunk, seq] = delta
            mixed_ref[chunk, seq] = read
            scale = lax.rsqrt(jnp.mean(read * read, axis=1, keepdims=True) + 1e-05)
            gate = gate_ref[chunk, seq, :, :DV]
            headed = read * scale * gain_ref[...] * (gate * jax.nn.sigmoid(gate))
            headed_ref[chunk, seq] = headed.astype(bf16)
        return tuple(following)

    final = lax.fori_loop(0, chunks, advance, tuple(state_ref[seq] for seq in range(seqs)))
    for seq in range(seqs):
        end_ref[seq] = final[seq]


def backward_kernel(
    conv_ref, gate_ref, run_ref, taps_ref, gain_ref, halo_ref, d_headed_ref, mixed_ref,
    inverse_ref, scores_ref, delta_ref, starts_ref, d_end_ref, d_after_ref,
    d_all_ref, grad_taps_ref, grad_gain_ref, d_start_ref, d_before_ref,
    rows_ref, d_mixed_ref, hold_ref, carry_ref, base_ref, back_ref, d_target_ref, d_state_ref,
    d_conv_ref,
):
    chunks, seqs, size, _ = conv_ref.shape
    rows, cols = iotas(size)

    def pieces(chunk, seq, slot):
        summed = conv_rows(conv_ref, halo_ref, rows_ref, taps_ref, chunk, seq, slot)
        logistic = jax.nn.sigmoid(summed)
        active = summed * logistic
        query = active[:, :DK]
        raw = active[:, DK : 2 * DK]
        shrink = lax.rsqrt(jnp.sum(raw * raw, axis=1, keepdims=True) + 1e-06)
        value = active[:, 2 * DK :]
        beta = jax.nn.sigmoid(gate_ref[chunk, seq, :, DV : DV + 1])
        slope = logistic * (1.0 + summed * (1.0 - logistic))
        return slope, query, raw * shrink, shrink, value, beta

    grad_gain_ref[...] = jnp.zeros_like(grad_gain_ref)
    grad_taps_ref[...] = jnp.zeros_like(grad_taps_ref)

    def prepare(chunk, _):
        for seq in range(seqs):
            _, query, key, _, _, beta = pieces(chunk, seq, seq)
            _, growth, fade, _ = decays(run_ref, chunk, seq, rows, cols)
            mixed = mixed_ref[chunk, seq]
            d_headed = d_headed_ref[chunk, seq]
            gate = gate_ref[chunk, seq, :, :DV]
            logistic = jax.nn.sigmoid(gate)
            scale = lax.rsqrt(jnp.mean(mixed * mixed, axis=1, keepdims=True) + 1e-05)
            normed = mixed * scale
            swish = gate * logistic
            inner = d_headed * gain_ref[...] * swish
            d_mixed = scale * (inner - normed * jnp.mean(normed * inner, axis=1, keepdims=True))
            grad_gain_ref[...] += jnp.sum(d_headed * normed * swish, axis=0, keepdims=True)
            d_gate = d_headed * gain_ref[...] * normed * logistic * (1.0 + gate * (1.0 - logistic))
            d_all_ref[chunk, seq, :, 2 * DK + DV : 2 * DK + 2 * DV] = d_gate.astype(bf16)
            d_mixed_ref[chunk, seq] = d_mixed
            d_mixed_parts = parts(d_mixed)
            inverse_parts = from_cat(inverse_ref[chunk, seq])
            scored = mul(from_cat(scores_ref[chunk, seq]), d_mixed_parts)
            base_ref[chunk, seq] = mul(inverse_parts, parts(scored))
            hold_ref[chunk, seq] = cat_parts(mul(inverse_parts, parts(fade * key)))
            back_ref[chunk, seq] = mul(parts((growth * query).T), d_mixed_parts)
            carry_ref[chunk, seq] = cat_parts((beta * growth * key).T)
        return 0

    lax.fori_loop(0, chunks, prepare, 0)

    def advance(step, d_states):
        chunk = chunks - 1 - step
        following = []
        for seq in range(seqs):
            d_state = d_states[seq]
            d_state_ref[chunk, seq] = d_state
            d_target = base_ref[chunk, seq] + mul(from_cat(hold_ref[chunk, seq]), parts(d_state))
            d_target_ref[chunk, seq] = d_target
            total = jnp.exp(run_ref[chunk, seq][0:1, size - 1 : size])
            back = mul(from_cat(carry_ref[chunk, seq]), parts(d_target))
            following.append(total * d_state + back_ref[chunk, seq] - back)
        return tuple(following)

    first = lax.fori_loop(0, chunks, advance, tuple(d_end_ref[seq] for seq in range(seqs)))
    for seq in range(seqs):
        d_start_ref[seq] = first[seq]
        d_conv_ref[seq, size:, :] = d_after_ref[seq]

    def finish(step, _):
        chunk = chunks - 1 - step
        for seq in range(seqs):
            slope, query, key, shrink, value, beta = pieces(chunk, seq, seq)
            decay_mat, growth, fade, _ = decays(run_ref, chunk, seq, rows, cols)
            key_parts = parts(key)
            query_parts = parts(query)
            gram = mul_t(key_parts, key_parts) * decay_mat
            d_target = d_target_ref[chunk, seq]
            delta_parts = parts(delta_ref[chunk, seq])
            start_parts = parts(starts_ref[chunk, seq])
            both = parts(jnp.concatenate([d_target, d_mixed_ref[chunk, seq]], 0))
            on_delta = mul_t(both, delta_parts)
            on_state = mul_t(both, start_parts)
            d_lower = jnp.where(rows > cols, -on_delta[:size], 0.0)
            d_scores = on_delta[size:] * decay_mat
            through = on_state[:size]
            d_gram = d_lower * decay_mat * beta
            d_query = growth * on_state[size:] + mul(parts(d_scores), key_parts)
            d_key = mul(parts(d_scores.T), query_parts)
            d_key = d_key + mul(parts(d_gram + d_gram.T), key_parts)
            d_key = d_key + fade * mul_t(delta_parts, parts(d_state_ref[chunk, seq]))
            d_key = d_key - (beta * growth) * through
            d_beta = (
                jnp.sum(d_target * value, axis=1, keepdims=True)
                - growth * jnp.sum(key * through, axis=1, keepdims=True)
                + jnp.sum(d_lower * gram, axis=1, keepdims=True)
            )
            d_raw = shrink * (d_key - key * jnp.sum(key * d_key, axis=1, keepdims=True))
            d_conv = jnp.concatenate([d_query, d_raw, beta * d_target], 1) * slope
            d_conv_ref[seq, :size, :] = d_conv
            d_in = None
            for tap in range(CONV):
                start = HALO - (CONV - 1) + tap
                grad_taps_ref[tap : tap + 1, :] += jnp.sum(
                    d_conv * rows_ref[seq, start : start + size, :], axis=0, keepdims=True
                )
                shift = CONV - 1 - tap
                term = d_conv_ref[seq, shift : shift + size, :] * taps_ref[tap : tap + 1, :]
                d_in = term if d_in is None else d_in + term
            d_conv_ref[seq, size:, :] = d_conv[:8, :]
            d_all_ref[chunk, seq, :, : 2 * DK + DV] = d_in.astype(bf16)
            d_logit = d_beta * beta * (1.0 - beta)
            lane = lax.broadcasted_iota(jnp.int32, (size, 128), 1)
            d_all_ref[chunk, seq, :, 2 * DK + 2 * DV :] = jnp.where(
                lane == 0, d_logit, 0.0
            ).astype(bf16)
        return 0

    lax.fori_loop(0, chunks, finish, 0)
    for seq in range(seqs):
        d_before_ref[seq] = d_conv_ref[seq, size:, :]


VMEM_LIMIT = 60 * 1024 * 1024


def whole(count):
    return [pl.BlockSpec(memory_space=pltpu.VMEM)] * count


def forward_rule(conv_in, gate_beta, run, taps, gain, state, halo):
    chunks, seqs, size, width = conv_in.shape
    lead = (chunks, seqs)
    shape = jax.ShapeDtypeStruct
    return pl.pallas_call(
        forward_kernel,
        name="delta_forward",
        out_shape=(
            shape(lead + (size, DV), bf16),
            shape(lead + (size, DV), f32),
            shape(lead + (size, 2 * size), bf16),
            shape(lead + (size, 2 * size), bf16),
            shape(lead + (size, DV), f32),
            shape(lead + (DK, DV), f32),
            shape((seqs, DK, DV), f32),
        ),
        in_specs=whole(7),
        out_specs=tuple(whole(7)),
        scratch_shapes=[
            pltpu.VMEM((seqs, HALO + size, width), f32),
            pltpu.VMEM(lead + (size, 2 * DK), bf16),
            pltpu.VMEM(lead + (size, DV), f32),
            pltpu.VMEM(lead + (size, 2 * DK), bf16),
            pltpu.VMEM(lead + (DK, 2 * size), bf16),
            pltpu.VMEM(lead + (size, 2 * size), bf16),
        ],
        compiler_params=pltpu.CompilerParams(vmem_limit_bytes=VMEM_LIMIT),
    )(conv_in, gate_beta, run, taps, gain, state, halo)


def backward_rule(conv_in, gate_beta, run, taps, gain, halo, d_headed, saved, d_end, d_after):
    chunks, seqs, size, width = conv_in.shape
    lead = (chunks, seqs)
    shape = jax.ShapeDtypeStruct
    return pl.pallas_call(
        backward_kernel,
        name="delta_backward",
        out_shape=(
            shape(lead + (size, 2 * DK + 2 * DV + 128), bf16),
            shape((8, width), f32),
            shape((1, DV), f32),
            shape((seqs, DK, DV), f32),
            shape((seqs, 8, width), f32),
        ),
        in_specs=whole(14),
        out_specs=tuple(whole(5)),
        scratch_shapes=[
            pltpu.VMEM((seqs, HALO + size, width), f32),
            pltpu.VMEM(lead + (size, DV), f32),
            pltpu.VMEM(lead + (size, 2 * DK), bf16),
            pltpu.VMEM(lead + (DK, 2 * size), bf16),
            pltpu.VMEM(lead + (size, DV), f32),
            pltpu.VMEM(lead + (DK, DV), f32),
            pltpu.VMEM(lead + (size, DV), f32),
            pltpu.VMEM(lead + (DK, DV), f32),
            pltpu.VMEM((seqs, size + 8, width), f32),
        ],
        compiler_params=pltpu.CompilerParams(vmem_limit_bytes=VMEM_LIMIT),
    )(conv_in, gate_beta, run, taps, gain, halo, d_headed, *saved, d_end, d_after)


def product(left, right):
    return jnp.dot(left, right, preferred_element_type=f32)


def contract_rows(left, right):
    return dot(left, right, ((0,), (0,)))


def contract_cols(left, right):
    return dot(left, right, ((1,), (1,)))


def passed_along(array, axis, by):
    peers = lax.axis_size(axis)
    pairs = [(i, i + by) for i in range(peers) if 0 <= i + by < peers]
    return lax.ppermute(array, axis, pairs)


def rms_scale(values):
    return lax.rsqrt(jnp.mean(values * values, axis=-1, keepdims=True) + 1e-05)


def rms_back(values, scale, gain, d_normed):
    normed = values * scale
    pulled = d_normed * gain
    d_values = scale * (pulled - normed * jnp.mean(normed * pulled, axis=-1, keepdims=True))
    return d_values, jnp.sum(d_normed * normed, axis=0)


def shards(
    inputs,
    cotangent,
    decay,
    w_query,
    w_key,
    w_value,
    w_gate_out,
    w_out,
    w_ffn_gate,
    w_ffn_up,
    w_ffn_down,
    w_beta,
    conv_weight,
    norm_in,
    norm_mid,
    norm_head,
):
    seqs, size, model = inputs.shape
    rows = seqs * size
    peers = lax.axis_size("seq")
    stages = peers // H
    groups = None
    if stages > 1:
        groups = [[stage * H + head for head in range(H)] for stage in range(stages)]
    head = lax.rem(lax.axis_index("seq"), H)
    all_rows = H * rows
    hidden_all = w_ffn_gate.shape[1]
    share = -(-hidden_all // (H * 128)) * 128

    def gather_rows(local):
        return lax.all_gather(local, "seq", axis_index_groups=groups).reshape(
            (all_rows,) + local.shape[1:]
        )

    def scatter_rows(partial):
        blocks = partial.astype(bf16).reshape(H, rows, model)
        swapped = lax.all_to_all(blocks, "seq", 0, 0, axis_index_groups=groups, tiled=True)
        return jnp.sum(swapped.astype(f32), axis=0)

    def own_columns(weight, width):
        return lax.dynamic_slice_in_dim(weight, head * width, width, axis=1)

    def own_hidden(weight):
        start = jnp.minimum(head * share, hidden_all - share)
        piece = lax.dynamic_slice_in_dim(weight, start, share, axis=1)
        lane = lax.broadcasted_iota(jnp.int32, piece.shape, 1)
        return jnp.where(lane + start >= head * share, piece, jnp.zeros_like(piece))

    def gather_weight(local):
        return lax.all_gather(local, "wt", axis=0, tiled=True)

    flat_in = inputs.reshape(rows, model).astype(f32)
    scale_in = rms_scale(flat_in)
    normed_in = gather_rows((flat_in * scale_in * norm_in).astype(bf16))

    mixer_w = gather_weight(
        jnp.concatenate(
            [
                own_columns(w_query, DK),
                own_columns(w_key, DK),
                own_columns(w_value, DV),
                own_columns(w_gate_out, DV),
            ],
            axis=1,
        )
    )
    beta_w = jnp.pad(own_columns(w_beta, 1), ((0, 0), (0, 127)))
    mixer_w = jnp.concatenate([mixer_w, beta_w], axis=1)
    full_out = gather_weight(w_out)
    ffn_w = gather_weight(
        jnp.concatenate(
            [own_hidden(w_ffn_gate), own_hidden(w_ffn_up), own_hidden(w_ffn_down)], axis=1
        )
    )
    gate_w, up_w, down_w = ffn_w[:, :share], ffn_w[:, share : 2 * share], ffn_w[:, 2 * share :]
    upstream_own = cotangent.reshape(rows, model)
    upstream = gather_rows(upstream_own)

    own_decay = lax.all_gather(decay, "seq", axis_index_groups=groups)
    own_decay = lax.dynamic_index_in_dim(own_decay, head, axis=3, keepdims=False)
    run = jnp.cumsum(jnp.log(own_decay), axis=-1)
    run = jnp.broadcast_to(run[:, :, None, :], (H, seqs, 8, size))
    taps = jnp.concatenate(
        [
            own_columns(conv_weight[:, : H * DK], DK),
            own_columns(conv_weight[:, H * DK : 2 * H * DK], DK),
            own_columns(conv_weight[:, 2 * H * DK :], DV),
        ],
        axis=1,
    )
    taps = jnp.pad(taps, ((0, 8 - CONV), (0, 0)))
    gain = norm_head[None, :]

    conv_width = 2 * DK + DV
    lead = (H, seqs, size)
    conv_in = product(normed_in, mixer_w[:, :conv_width]).astype(bf16).reshape(lead + (-1,))
    gate_beta = product(normed_in, mixer_w[:, conv_width:]).reshape(lead + (-1,))

    state = jnp.zeros((seqs, DK, DV), f32)
    halo = jnp.zeros((seqs, HALO, conv_width), bf16)
    if stages > 1:
        halo = passed_along(conv_in[H - 1, :, size - HALO :], "seq", H)
    for stage in range(stages):
        headed, *saved, ending = forward_rule(conv_in, gate_beta, run, taps, gain, state, halo)
        if stage < stages - 1:
            state = passed_along(ending, "seq", H)

    own_headed = lax.all_to_all(
        headed.reshape(H, rows, DV), "seq", 0, 0, axis_index_groups=groups, tiled=True
    )
    own_headed = jnp.swapaxes(own_headed, 0, 1).reshape(rows, H * DV)
    residual = flat_in + contract_cols(own_headed, full_out)
    scale_mid = rms_scale(residual)
    normed_mid = gather_rows((residual * scale_mid * norm_mid).astype(bf16))

    gate_pre = product(normed_mid, gate_w)
    up_pre = product(normed_mid, up_w)
    logistic = jax.nn.sigmoid(gate_pre)
    swish = gate_pre * logistic
    hidden = (swish * up_pre).astype(bf16)
    d_hidden = product(upstream, down_w)
    d_gate = (d_hidden * up_pre * logistic * (1.0 + gate_pre * (1.0 - logistic))).astype(bf16)
    d_up = (d_hidden * swish).astype(bf16)
    d_normed_mid = scatter_rows(contract_cols(d_gate, gate_w) + contract_cols(d_up, up_w))
    ffn_out = lax.psum_scatter(
        contract_cols(hidden, down_w).astype(bf16),
        "seq",
        scatter_dimension=0,
        axis_index_groups=groups,
        tiled=True,
    )
    layer_out = (residual + ffn_out.astype(f32)).astype(bf16).reshape(inputs.shape)

    d_from_mid, grad_mid = rms_back(residual, scale_mid, norm_mid, d_normed_mid)
    d_residual = upstream_own.astype(f32) + d_from_mid
    d_branch = gather_rows(d_residual.astype(bf16))
    out_w = lax.dynamic_slice_in_dim(full_out, head * DV, DV, axis=1)
    d_headed = product(d_branch, out_w).reshape(lead + (DV,))

    d_end = jnp.zeros((seqs, DK, DV), f32)
    d_after = jnp.zeros((seqs, 8, conv_width), f32)
    for stage in range(stages):
        d_all, grad_taps, grad_gain, d_start, d_before = backward_rule(
            conv_in, gate_beta, run, taps, gain, halo, d_headed, saved, d_end, d_after
        )
        if stage < stages - 1:
            d_end = passed_along(d_start, "seq", -H)
            d_after = passed_along(d_before, "seq", -H)
    d_all = d_all.reshape(all_rows, -1)

    def reduce_grads(partial):
        summed = lax.psum_scatter(
            partial.astype(bf16), "wt", scatter_dimension=0, tiled=True
        )
        spread = lax.all_gather(summed, "seq")
        spread = spread.reshape((stages, H) + summed.shape).astype(f32)
        return jnp.sum(spread, axis=0)

    def joined(spread):
        return jnp.swapaxes(spread, 0, 1).reshape(spread.shape[1], -1)

    def joined_hidden(spread):
        flat = joined(spread)
        kept = (H - 1) * share
        return jnp.concatenate([flat[:, :kept], flat[:, kept + H * share - hidden_all :]], axis=1)

    ffn_grads = reduce_grads(
        jnp.concatenate(
            [
                contract_rows(normed_mid, d_gate),
                contract_rows(normed_mid, d_up),
                contract_rows(upstream, hidden),
            ],
            axis=1,
        )
    )
    mixer_partial = contract_rows(normed_in, d_all)
    out_partial = contract_rows(d_branch, headed.reshape(all_rows, DV))
    width = conv_width + DV
    mixer_grads = reduce_grads(jnp.concatenate([mixer_partial[:, :width], out_partial], axis=1))

    d_normed_in = scatter_rows(contract_cols(d_all, mixer_w))
    d_from_in, _ = rms_back(flat_in, scale_in, norm_in, d_normed_in)
    grad_input = (d_residual + d_from_in).reshape(inputs.shape)

    grad_in_part = jnp.sum(mixer_partial * mixer_w.astype(f32), axis=1) / norm_in
    small = jnp.concatenate(
        [
            grad_taps[:CONV].reshape(-1),
            mixer_partial[:, width],
            grad_gain[0],
            grad_mid,
            grad_in_part,
        ]
    )
    small = lax.all_gather(small.reshape(-1, 128), ("seq", "wt")).reshape(
        stages, H, lax.axis_size("wt"), -1
    )
    small = jnp.sum(small, axis=(0, 2))
    bounds = [CONV * conv_width, model, DV, model, model]
    ends = []
    for bound in bounds:
        ends.append(bound + (ends[-1] if ends else 0))
    taps_part = small[:, : ends[0]].reshape(H, CONV, conv_width)
    grad_conv = jnp.concatenate(
        [
            joined(taps_part[:, :, :DK]),
            joined(taps_part[:, :, DK : 2 * DK]),
            joined(taps_part[:, :, 2 * DK :]),
        ],
        axis=1,
    )
    grad_beta = small[:, ends[0] : ends[1]].T
    shared = jnp.sum(small[:, ends[1] :], axis=0)
    grad_head, grad_mid, grad_in = (
        shared[:DV],
        shared[DV : DV + model],
        shared[DV + model :],
    )
    return (
        layer_out,
        grad_input,
        joined(mixer_grads[:, :, :DK]),
        joined(mixer_grads[:, :, DK : 2 * DK]),
        joined(mixer_grads[:, :, 2 * DK : conv_width]),
        joined(mixer_grads[:, :, conv_width:width]),
        joined(mixer_grads[:, :, width:]),
        joined_hidden(ffn_grads[:, :, :share]),
        joined_hidden(ffn_grads[:, :, share : 2 * share]),
        joined_hidden(ffn_grads[:, :, 2 * share :]),
        grad_beta,
        grad_conv,
        grad_in,
        grad_mid,
        grad_head,
    )


def solution(mesh):
    rows = P("wt", "seq", None)
    cut = P("wt", None)
    in_specs = (rows,) * 3 + (cut,) * 8 + (P(),) * 5
    out_specs = (rows,) * 2 + (cut,) * 8 + (P(),) * 5
    return jax.shard_map(shards, mesh=mesh, in_specs=in_specs, out_specs=out_specs, check_vma=False)
```

```python
import jax
import jax.numpy as jnp
from jax import lax
from jax.experimental import pallas as pl
from jax.experimental.pallas import tpu as pltpu
from jax.sharding import PartitionSpec as P

H = 8
DK = 128
DV = 256
CONV = 4
HALO = 16
WIDTH = 2 * DK + DV
VMEM_LIMIT = 60 * 1024 * 1024
bf16 = jnp.bfloat16
f32 = jnp.float32


def dot(left, right, dims):
    return lax.dot_general(left, right, (dims, ((), ())), preferred_element_type=f32)


def product(left, right):
    return dot(left, right, ((1,), (0,)))


def contract_rows(left, right):
    return dot(left, right, ((0,), (0,)))


def contract_cols(left, right):
    return dot(left, right, ((1,), (1,)))


def parts(values):
    high = values.astype(bf16)
    return high, (values - high.astype(f32)).astype(bf16)


def mul(left, right):
    (lh, ll), (rh, rl) = left, right
    wide = product(jnp.concatenate([lh, ll], 1), jnp.concatenate([rh, rh], 0))
    return wide + product(lh, rl)


def mul_t(left, right):
    (lh, ll), (rh, rl) = left, right
    wide = contract_cols(jnp.concatenate([lh, ll], 1), jnp.concatenate([rh, rh], 1))
    return wide + contract_cols(lh, rl)


def cat_parts(values):
    return jnp.concatenate(parts(values), 1)


def from_cat(both):
    half = both.shape[1] // 2
    return both[:, :half], both[:, half:]


def iotas(size):
    return (
        lax.broadcasted_iota(jnp.int32, (size, size), 0),
        lax.broadcasted_iota(jnp.int32, (size, size), 1),
    )


def unit_inverses(lowers, rows, cols):
    size = rows.shape[0]
    level = 0
    eye = jnp.where(rows == cols, 1.0, 0.0)
    inverses = [eye] * len(lowers)
    while (1 << level) < size:
        together = (rows >> (level + 1)) == (cols >> (level + 1))
        corner = together & (((rows >> level) & 1) == 1) & (((cols >> level) & 1) == 0)
        blocks = [jnp.where(corner, lower, 0.0) for lower in lowers]
        if level == 0:
            inverses = [inverse - block for inverse, block in zip(inverses, blocks)]
        else:
            wholes = [parts(inverse) for inverse in inverses]
            steps = [mul(parts(block), whole) for block, whole in zip(blocks, wholes)]
            steps = [mul(whole, parts(step)) for step, whole in zip(steps, wholes)]
            inverses = [inverse - step for inverse, step in zip(inverses, steps)]
        level += 1
    return inverses


def conv_rows(conv_ref, halo_ref, rows_ref, taps_ref, chunk, seq, slot):
    size = conv_ref.shape[2]
    before = conv_ref[jnp.maximum(chunk - 1, 0), seq, size - HALO :, :]
    before = jnp.where(chunk == 0, halo_ref[seq], before)
    rows_ref[slot, :HALO, :] = before.astype(f32)
    rows_ref[slot, HALO:, :] = conv_ref[chunk, seq].astype(f32)
    total = None
    for tap in range(CONV):
        start = HALO - (CONV - 1) + tap
        term = rows_ref[slot, start : start + size, :] * taps_ref[tap : tap + 1, :]
        total = term if total is None else total + term
    return total


def decays(run_ref, chunk, seq, rows, cols):
    size = rows.shape[0]
    run_row = run_ref[chunk, seq][0:1, :]
    run_col = jnp.sum(jnp.where(rows == cols, run_row, 0.0), axis=1, keepdims=True)
    spread = jnp.where(rows >= cols, run_col - run_row, 0.0)
    decay_mat = jnp.where(rows >= cols, jnp.exp(spread), 0.0)
    last = run_row[:, size - 1 : size]
    return decay_mat, jnp.exp(run_col), jnp.exp(last - run_col)


def units_of(first, count, seqs):
    return [(first + chunk, seq) for chunk in range(count) for seq in range(seqs)]


FORWARD_CHUNKS = 4


def forward_kernel(head_ref, *refs):
    block_refs, refs = refs[:H], refs[H:]
    (
        weight_ref, beta_ref, run_ref, taps_ref, gain_ref, state_ref, halo_ref,
        headed_ref, conv_ref, gate_ref, mixed_ref, inverse_ref, scores_ref, delta_ref, starts_ref,
        end_ref,
        rows_ref, recall_ref, target_ref, query_ref, write_ref, plain_ref,
    ) = refs
    chunks, seqs, size, _ = conv_ref.shape
    rows, cols = iotas(size)
    head = head_ref[0]

    for slot in range(H):
        chunk = slot ^ head
        block = block_refs[slot][...]
        conv = product(block, weight_ref[:, :WIDTH]).astype(bf16)
        gate = product(block, weight_ref[:, WIDTH : WIDTH + DV])
        beta = product(block, beta_ref[...])
        for seq in range(seqs):
            span = slice(seq * size, (seq + 1) * size)
            conv_ref[chunk, seq] = conv[span]
            gate_ref[chunk, seq, :, :DV] = gate[span]
            gate_ref[chunk, seq, :, DV:] = beta[span]

    def prepare(turn, _):
        units = units_of(turn * FORWARD_CHUNKS, FORWARD_CHUNKS, seqs)
        keys, betas, growths, lowers, mats = [], [], [], [], []
        for slot, (chunk, seq) in enumerate(units):
            summed = conv_rows(conv_ref, halo_ref, rows_ref, taps_ref, chunk, seq, slot)
            active = summed * jax.nn.sigmoid(summed)
            query = active[:, :DK]
            key = active[:, DK : 2 * DK]
            key = key * lax.rsqrt(jnp.sum(key * key, axis=1, keepdims=True) + 1e-06)
            beta = jax.nn.sigmoid(gate_ref[chunk, seq, :, DV : DV + 1])
            decay_mat, growth, fade = decays(run_ref, chunk, seq, rows, cols)
            target_ref[chunk, seq] = beta * active[:, 2 * DK :]
            query_ref[chunk, seq] = cat_parts(growth * query)
            write_ref[chunk, seq] = cat_parts((fade * key).T)
            recall_ref[chunk, seq] = cat_parts(beta * growth * key)
            key_parts = parts(key)
            gram = mul_t(key_parts, key_parts)
            lowers.append(jnp.where(rows > cols, beta * gram * decay_mat, 0.0))
            scores = mul_t(parts(query), key_parts) * decay_mat
            plain_ref[chunk, seq] = cat_parts(scores)
            scores_ref[chunk, seq] = cat_parts(scores.T)
        inverses = unit_inverses(lowers, rows, cols)
        for (chunk, seq), inverse in zip(units, inverses):
            inverse_parts = parts(inverse)
            recall = mul(inverse_parts, from_cat(recall_ref[chunk, seq]))
            recall_ref[chunk, seq] = cat_parts(recall)
            target_ref[chunk, seq] = mul(inverse_parts, parts(target_ref[chunk, seq]))
            inverse_ref[chunk, seq] = cat_parts(inverse.T)
        return 0

    lax.fori_loop(0, chunks // FORWARD_CHUNKS, prepare, 0)

    def advance(chunk, states):
        following = []
        for seq in range(seqs):
            state = states[seq]
            starts_ref[chunk, seq] = state
            state_parts = parts(state)
            delta = target_ref[chunk, seq] - mul(from_cat(recall_ref[chunk, seq]), state_parts)
            delta_parts = parts(delta)
            total = jnp.exp(run_ref[chunk, seq][0:1, size - 1 : size])
            following.append(
                total * state + mul(from_cat(write_ref[chunk, seq]), delta_parts)
            )
            delta_ref[chunk, seq] = delta
            read = mul(from_cat(query_ref[chunk, seq]), state_parts)
            read = read + mul(from_cat(plain_ref[chunk, seq]), delta_parts)
            mixed_ref[chunk, seq] = read
            scale = lax.rsqrt(jnp.mean(read * read, axis=1, keepdims=True) + 1e-05)
            gate = gate_ref[chunk, seq, :, :DV]
            headed = read * scale * gain_ref[...] * (gate * jax.nn.sigmoid(gate))
            headed_ref[chunk, seq] = headed.astype(bf16)
        return tuple(following)

    final = lax.fori_loop(0, chunks, advance, tuple(state_ref[seq] for seq in range(seqs)))
    for seq in range(seqs):
        end_ref[seq] = final[seq]


BACKWARD_CHUNKS = 2


def backward_kernel(
    head_ref,
    branch_ref, out_ref, conv_ref, gate_ref, run_ref, taps_ref, gain_ref, halo_ref, mixed_ref,
    inverse_ref, scores_ref, delta_ref, starts_ref, d_end_ref, d_after_ref,
    d_all_ref, grad_taps_ref, grad_gain_ref, d_start_ref, d_before_ref,
    rows_ref, d_headed_ref, hold_ref, carry_ref, base_ref, back_ref, d_target_ref, d_state_ref,
    d_conv_ref,
):
    chunks, seqs, size, _ = conv_ref.shape
    rows, cols = iotas(size)
    head = head_ref[0]

    def pieces(chunk, seq, slot):
        summed = conv_rows(conv_ref, halo_ref, rows_ref, taps_ref, chunk, seq, slot)
        logistic = jax.nn.sigmoid(summed)
        active = summed * logistic
        query = active[:, :DK]
        raw = active[:, DK : 2 * DK]
        shrink = lax.rsqrt(jnp.sum(raw * raw, axis=1, keepdims=True) + 1e-06)
        value = active[:, 2 * DK :]
        beta = jax.nn.sigmoid(gate_ref[chunk, seq, :, DV : DV + 1])
        slope = logistic * (1.0 + summed * (1.0 - logistic))
        return slope, query, raw * shrink, shrink, value, beta

    grad_gain_ref[...] = jnp.zeros_like(grad_gain_ref)
    grad_taps_ref[...] = jnp.zeros_like(grad_taps_ref)

    for chunk in range(H):
        d_headed = product(branch_ref[chunk], out_ref[...])
        for seq in range(seqs):
            d_headed_ref[chunk, seq] = d_headed[seq * size : (seq + 1) * size]

    def prepare(turn, _):
        units = units_of(turn * BACKWARD_CHUNKS, BACKWARD_CHUNKS, seqs)
        for slot, (chunk, seq) in enumerate(units):
            _, query, key, _, _, beta = pieces(chunk, seq, slot)
            _, growth, fade = decays(run_ref, chunk, seq, rows, cols)
            mixed = mixed_ref[chunk, seq]
            d_headed = d_headed_ref[chunk, seq]
            gate = gate_ref[chunk, seq, :, :DV]
            logistic = jax.nn.sigmoid(gate)
            scale = lax.rsqrt(jnp.mean(mixed * mixed, axis=1, keepdims=True) + 1e-05)
            normed = mixed * scale
            swish = gate * logistic
            inner = d_headed * gain_ref[...] * swish
            d_mixed = scale * (inner - normed * jnp.mean(normed * inner, axis=1, keepdims=True))
            grad_gain_ref[...] += jnp.sum(d_headed * normed * swish, axis=0, keepdims=True)
            d_gate = d_headed * gain_ref[...] * normed * logistic * (1.0 + gate * (1.0 - logistic))
            d_all_ref[chunk ^ head, seq, :, WIDTH : WIDTH + DV] = d_gate.astype(bf16)
            d_headed_ref[chunk, seq] = d_mixed
            d_mixed_parts = parts(d_mixed)
            inverse_parts = from_cat(inverse_ref[chunk, seq])
            scored = mul(from_cat(scores_ref[chunk, seq]), d_mixed_parts)
            base_ref[chunk, seq] = mul(inverse_parts, parts(scored))
            hold_ref[chunk, seq] = cat_parts(mul(inverse_parts, parts(fade * key)))
            back_ref[chunk, seq] = mul(parts((growth * query).T), d_mixed_parts)
            carry_ref[chunk, seq] = cat_parts((beta * growth * key).T)
        return 0

    lax.fori_loop(0, chunks // BACKWARD_CHUNKS, prepare, 0)

    def advance(step, d_states):
        chunk = chunks - 1 - step
        following = []
        for seq in range(seqs):
            d_state = d_states[seq]
            d_state_ref[chunk, seq] = d_state
            d_target = base_ref[chunk, seq] + mul(from_cat(hold_ref[chunk, seq]), parts(d_state))
            d_target_ref[chunk, seq] = d_target
            total = jnp.exp(run_ref[chunk, seq][0:1, size - 1 : size])
            back = mul(from_cat(carry_ref[chunk, seq]), parts(d_target))
            following.append(total * d_state + back_ref[chunk, seq] - back)
        return tuple(following)

    first = lax.fori_loop(0, chunks, advance, tuple(d_end_ref[seq] for seq in range(seqs)))
    for seq in range(seqs):
        d_start_ref[seq] = first[seq]
        d_conv_ref[seq, size:, :] = d_after_ref[seq]

    def finish(turn, _):
        units = [
            (chunks - 1 - turn * BACKWARD_CHUNKS - back, seq)
            for back in range(BACKWARD_CHUNKS)
            for seq in range(seqs)
        ]
        for slot, (chunk, seq) in enumerate(units):
            slope, query, key, shrink, value, beta = pieces(chunk, seq, slot)
            decay_mat, growth, fade = decays(run_ref, chunk, seq, rows, cols)
            key_parts = parts(key)
            gram = mul_t(key_parts, key_parts) * decay_mat
            d_target = d_target_ref[chunk, seq]
            delta_parts = parts(delta_ref[chunk, seq])
            start_parts = parts(starts_ref[chunk, seq])
            both = parts(jnp.concatenate([d_target, d_headed_ref[chunk, seq]], 0))
            on_delta = mul_t(both, delta_parts)
            on_state = mul_t(both, start_parts)
            d_lower = jnp.where(rows > cols, -on_delta[:size], 0.0)
            d_scores = on_delta[size:] * decay_mat
            through = on_state[:size]
            d_gram = d_lower * decay_mat * beta
            d_query = growth * on_state[size:] + mul(parts(d_scores), key_parts)
            d_key = mul(parts(d_scores.T), parts(query))
            d_key = d_key + mul(parts(d_gram + d_gram.T), key_parts)
            d_key = d_key + fade * mul_t(delta_parts, parts(d_state_ref[chunk, seq]))
            d_key = d_key - (beta * growth) * through
            d_beta = (
                jnp.sum(d_target * value, axis=1, keepdims=True)
                - growth * jnp.sum(key * through, axis=1, keepdims=True)
                + jnp.sum(d_lower * gram, axis=1, keepdims=True)
            )
            d_raw = shrink * (d_key - key * jnp.sum(key * d_key, axis=1, keepdims=True))
            d_conv = jnp.concatenate([d_query, d_raw, beta * d_target], 1) * slope
            d_conv_ref[seq, :size, :] = d_conv
            d_in = None
            for tap in range(CONV):
                start = HALO - (CONV - 1) + tap
                grad_taps_ref[tap : tap + 1, :] += jnp.sum(
                    d_conv * rows_ref[slot, start : start + size, :], axis=0, keepdims=True
                )
                shift = CONV - 1 - tap
                term = d_conv_ref[seq, shift : shift + size, :] * taps_ref[tap : tap + 1, :]
                d_in = term if d_in is None else d_in + term
            d_conv_ref[seq, size:, :] = d_conv[:8, :]
            d_all_ref[chunk ^ head, seq, :, :WIDTH] = d_in.astype(bf16)
            d_logit = d_beta * beta * (1.0 - beta)
            lane = lax.broadcasted_iota(jnp.int32, (size, 128), 1)
            d_all_ref[chunk ^ head, seq, :, WIDTH + DV :] = jnp.where(
                lane == 0, d_logit, 0.0
            ).astype(bf16)
        return 0

    lax.fori_loop(0, chunks // BACKWARD_CHUNKS, finish, 0)
    for seq in range(seqs):
        d_before_ref[seq] = d_conv_ref[seq, size:, :]


def whole(count):
    return [pl.BlockSpec(memory_space=pltpu.VMEM)] * count


def scalar():
    return [pl.BlockSpec(memory_space=pltpu.SMEM)]


shaped = jax.ShapeDtypeStruct


def kernel_params():
    return pltpu.CompilerParams(vmem_limit_bytes=VMEM_LIMIT)


def forward_rule(head, blocks, weight, beta_w, run, taps, gain, state, halo):
    chunks, seqs, _, size = run.shape
    lead = (chunks, seqs)
    return pl.pallas_call(
        forward_kernel,
        name="mixer_forward",
        out_shape=(
            shaped(lead + (size, DV), bf16),
            shaped(lead + (size, WIDTH), bf16),
            shaped(lead + (size, DV + 128), f32),
            shaped(lead + (size, DV), f32),
            shaped(lead + (size, 2 * size), bf16),
            shaped(lead + (size, 2 * size), bf16),
            shaped(lead + (size, DV), f32),
            shaped(lead + (DK, DV), f32),
            shaped((seqs, DK, DV), f32),
        ),
        in_specs=scalar() + whole(H + 7),
        out_specs=tuple(whole(9)),
        scratch_shapes=[
            pltpu.VMEM((FORWARD_CHUNKS * seqs, HALO + size, WIDTH), f32),
            pltpu.VMEM(lead + (size, 2 * DK), bf16),
            pltpu.VMEM(lead + (size, DV), f32),
            pltpu.VMEM(lead + (size, 2 * DK), bf16),
            pltpu.VMEM(lead + (DK, 2 * size), bf16),
            pltpu.VMEM(lead + (size, 2 * size), bf16),
        ],
        compiler_params=kernel_params(),
    )(head, *blocks, weight, beta_w, run, taps, gain, state, halo)


def backward_rule(head, branch, out_w, run, taps, gain, halo, saved, d_end, d_after):
    chunks, seqs, _, size = run.shape
    lead = (chunks, seqs)
    conv_in, gate_beta, mixed, inverse, scores, delta, starts = saved
    return pl.pallas_call(
        backward_kernel,
        name="mixer_backward",
        out_shape=(
            shaped(lead + (size, WIDTH + DV + 128), bf16),
            shaped((8, WIDTH), f32),
            shaped((1, DV), f32),
            shaped((seqs, DK, DV), f32),
            shaped((seqs, 8, WIDTH), f32),
        ),
        in_specs=scalar() + whole(15),
        out_specs=tuple(whole(5)),
        scratch_shapes=[
            pltpu.VMEM((BACKWARD_CHUNKS * seqs, HALO + size, WIDTH), f32),
            pltpu.VMEM(lead + (size, DV), f32),
            pltpu.VMEM(lead + (size, 2 * DK), bf16),
            pltpu.VMEM(lead + (DK, 2 * size), bf16),
            pltpu.VMEM(lead + (size, DV), f32),
            pltpu.VMEM(lead + (DK, DV), f32),
            pltpu.VMEM(lead + (size, DV), f32),
            pltpu.VMEM(lead + (DK, DV), f32),
            pltpu.VMEM((seqs, size + 8, WIDTH), f32),
        ],
        compiler_params=kernel_params(),
    )(
        head, branch, out_w, conv_in, gate_beta, run, taps, gain, halo, mixed, inverse, scores,
        delta, starts, d_end, d_after,
    )


def out_kernel(head_ref, *refs):
    block_refs, (headed_ref, inputs_ref, gain_ref, residual_ref, normed_ref) = refs[:H], refs[H:]
    head = head_ref[0]
    total = inputs_ref[...].astype(f32)
    for slot in range(H):
        total = total + contract_cols(headed_ref[slot ^ head], block_refs[slot][...])
    residual_ref[...] = total
    scale = lax.rsqrt(jnp.mean(total * total, axis=1, keepdims=True) + 1e-05)
    normed_ref[...] = (total * scale * gain_ref[...]).astype(bf16)


def out_rule(head, blocks, headed, inputs, gain):
    return pl.pallas_call(
        out_kernel,
        name="out_projection",
        out_shape=(shaped(inputs.shape, f32), shaped(inputs.shape, bf16)),
        in_specs=scalar() + whole(H + 3),
        out_specs=tuple(whole(2)),
        compiler_params=kernel_params(),
    )(head, *blocks, headed, inputs, gain)


def ffn_kernel(head_ref, normed_ref, up_ref, weight_ref, d_both_ref, hidden_ref, d_in_ref, out_ref):
    share = weight_ref.shape[1] // 3
    both = product(normed_ref[0], weight_ref[:, : 2 * share])
    d_hidden = product(up_ref[0], weight_ref[:, 2 * share :])
    gate, up = both[:, :share], both[:, share:]
    logistic = jax.nn.sigmoid(gate)
    swish = gate * logistic
    hidden = (swish * up).astype(bf16)
    hidden_ref[0] = hidden
    d_gate = (d_hidden * up * logistic * (1.0 + gate * (1.0 - logistic))).astype(bf16)
    d_up = (d_hidden * swish).astype(bf16)
    d_both = jnp.concatenate([d_gate, d_up], 1)
    d_both_ref[0] = d_both
    d_in_ref[0] = contract_cols(d_both, weight_ref[:, : 2 * share]).astype(bf16)
    out_ref[0] = contract_cols(hidden, weight_ref[:, 2 * share :]).astype(bf16)


def ffn_rule(head, normed, upstream, weight):
    count, rows, model = normed.shape
    share = weight.shape[1] // 3

    def same(step, head_ref):
        return (step, 0, 0)

    def moved(step, head_ref):
        return (step ^ head_ref[0], 0, 0)

    return pl.pallas_call(
        ffn_kernel,
        name="feed_forward",
        grid_spec=pltpu.PrefetchScalarGridSpec(
            num_scalar_prefetch=1,
            grid=(count,),
            in_specs=[
                pl.BlockSpec((1, rows, model), same),
                pl.BlockSpec((1, rows, model), moved),
                pl.BlockSpec(weight.shape, lambda step, head_ref: (0, 0)),
            ],
            out_specs=[
                pl.BlockSpec((1, rows, 2 * share), same),
                pl.BlockSpec((1, rows, share), moved),
                pl.BlockSpec((1, rows, model), moved),
                pl.BlockSpec((1, rows, model), moved),
            ],
        ),
        out_shape=(
            shaped((count, rows, 2 * share), bf16),
            shaped((count, rows, share), bf16),
            shaped((count, rows, model), bf16),
            shaped((count, rows, model), bf16),
        ),
        compiler_params=kernel_params(),
    )(head, normed, upstream, weight)


def join_kernel(spread_ref, *out_refs):
    start = 0
    for out_ref in out_refs:
        width = out_ref.shape[1]
        out_ref[...] = spread_ref[0, :, start : start + width].astype(f32)
        start += width


def join_rule(spread, widths):
    count, rows, width = spread.shape
    return pl.pallas_call(
        join_kernel,
        name="join_heads",
        grid=(count,),
        in_specs=[pl.BlockSpec((1, rows, width), lambda step: (step, 0, 0))],
        out_specs=[pl.BlockSpec((rows, width), lambda step: (0, step)) for width in widths],
        out_shape=[shaped((rows, count * width), f32) for width in widths],
        compiler_params=kernel_params(),
    )(spread)


def join_hidden_kernel(total, spread_ref, *out_refs):
    count, _, width = spread_ref.shape
    share = width // len(out_refs)
    for index, out_ref in enumerate(out_refs):
        for peer in range(count):
            start = min(peer * share, total - share)
            skip = peer * share - start
            piece = spread_ref[peer, :, index * share + skip : (index + 1) * share]
            out_ref[:, start + skip : start + share] = piece.astype(f32)


def join_hidden_rule(spread, total, pieces):
    count, rows, width = spread.shape
    return pl.pallas_call(
        lambda *refs: join_hidden_kernel(total, *refs),
        name="join_hidden",
        in_specs=whole(1),
        out_specs=whole(pieces),
        out_shape=[shaped((rows, total), f32)] * pieces,
        compiler_params=kernel_params(),
    )(spread)


def passed_along(array, axis, by):
    peers = lax.axis_size(axis)
    pairs = [(i, i + by) for i in range(peers) if 0 <= i + by < peers]
    return lax.ppermute(array, axis, pairs)


def swapped(array, axis, bits):
    return lax.ppermute(array, axis, [(i, i ^ bits) for i in range(lax.axis_size(axis))])


def gather_blocks(own):
    near, far, across = (swapped(own, "seq", bits) for bits in (2, 4, 6))
    blocks = [own, None, near, None, far, None, across, None]
    for slot in range(0, H, 2):
        blocks[slot + 1] = swapped(blocks[slot], "seq", 1)
    return blocks


def scatter_blocks(partial):
    handed = [swapped(partial[slot + 1], "seq", 1) for slot in range(0, H, 2)]
    sums = [partial[2 * i].astype(f32) + handed[i].astype(f32) for i in range(H // 2)]
    total = sums[0]
    for i in range(H // 2 - 1, 0, -1):
        total = total + swapped(sums[i].astype(bf16), "seq", 2 * i).astype(f32)
    return total


def rms_scale(values):
    return lax.rsqrt(jnp.mean(values * values, axis=-1, keepdims=True) + 1e-05)


def rms_back(values, gain, d_normed):
    scale = rms_scale(values)
    normed = values * scale
    pulled = d_normed * gain
    d_values = scale * (pulled - normed * jnp.mean(normed * pulled, axis=-1, keepdims=True))
    return d_values, jnp.sum(d_normed * normed, axis=0)


def shards(
    inputs,
    cotangent,
    decay,
    w_query,
    w_key,
    w_value,
    w_gate_out,
    w_out,
    w_ffn_gate,
    w_ffn_up,
    w_ffn_down,
    w_beta,
    conv_weight,
    norm_in,
    norm_mid,
    norm_head,
):
    seqs, size, model = inputs.shape
    rows = seqs * size
    peers = lax.axis_size("seq")
    stages = peers // H
    groups = None
    if stages > 1:
        groups = [[stage * H + head for head in range(H)] for stage in range(stages)]
    place = lax.axis_index("seq")
    head = lax.rem(place, H)
    head_arg = head.reshape(1)
    all_rows = H * rows
    hidden_all = w_ffn_gate.shape[1]
    share = -(-hidden_all // (H * 128)) * 128

    def gather_rows(local):
        return lax.all_gather(local, "seq", axis_index_groups=groups)

    def own_columns(weight, width):
        return lax.dynamic_slice_in_dim(weight, head * width, width, axis=1)

    def own_hidden(weight):
        start = jnp.minimum(head * share, hidden_all - share)
        piece = lax.dynamic_slice_in_dim(weight, start, share, axis=1)
        lane = lax.broadcasted_iota(jnp.int32, piece.shape, 1)
        return jnp.where(lane + start >= head * share, piece, jnp.zeros_like(piece))

    def gather_weight(local):
        return lax.all_gather(local, "wt", axis=0, tiled=True)

    mixer_w = gather_weight(
        jnp.concatenate(
            [
                own_columns(w_query, DK),
                own_columns(w_key, DK),
                own_columns(w_value, DV),
                own_columns(w_gate_out, DV),
                own_columns(w_out, DV),
            ],
            axis=1,
        )
    )
    ffn_w = gather_weight(
        jnp.concatenate(
            [own_hidden(w_ffn_gate), own_hidden(w_ffn_up), own_hidden(w_ffn_down)], axis=1
        )
    )
    own_in = inputs.reshape(rows, model)
    flat_in = own_in.astype(f32)
    normed_own = (flat_in * rms_scale(flat_in) * norm_in).astype(bf16)
    normed_in = gather_blocks(normed_own)
    upstream_own = cotangent.reshape(rows, model)
    upstream = jnp.stack(gather_blocks(upstream_own))
    beta_w = jnp.pad(own_columns(w_beta, 1), ((0, 0), (0, 127)))
    in_width = WIDTH + DV
    out_w = mixer_w[:, in_width:]
    out_blocks = gather_blocks(out_w)

    own_decay = gather_rows(decay)
    own_decay = lax.dynamic_index_in_dim(own_decay, head, axis=3, keepdims=False)
    run = jnp.cumsum(jnp.log(own_decay), axis=-1)
    run = jnp.broadcast_to(run[:, :, None, :], (H, seqs, 8, size))
    taps = jnp.concatenate(
        [
            own_columns(conv_weight[:, : H * DK], DK),
            own_columns(conv_weight[:, H * DK : 2 * H * DK], DK),
            own_columns(conv_weight[:, 2 * H * DK :], DV),
        ],
        axis=1,
    )
    taps = jnp.pad(taps, ((0, 8 - CONV), (0, 0)))
    gain = norm_head[None, :]

    state = jnp.zeros((seqs, DK, DV), f32)
    halo = jnp.zeros((seqs, HALO, WIDTH), bf16)
    if stages > 1:
        edges = lax.all_gather(normed_own.reshape(seqs, size, model)[:, size - HALO :], "seq")
        before = lax.dynamic_index_in_dim(edges, jnp.maximum(place - head - 1, 0), keepdims=False)
        rolled = product(before.reshape(seqs * HALO, model), mixer_w[:, :WIDTH]).astype(bf16)
        halo = jnp.where(place >= H, rolled.reshape(halo.shape), halo)
    for stage in range(stages):
        headed, *saved, ending = forward_rule(
            head_arg, normed_in, mixer_w, beta_w, run, taps, gain, state, halo
        )
        if stage < stages - 1:
            state = passed_along(ending, "seq", H)

    headed = headed.reshape(H, rows, DV)
    own_headed = lax.all_to_all(headed, "seq", 0, 0, axis_index_groups=groups, tiled=True)
    residual, normed_mid = out_rule(head_arg, out_blocks, own_headed, own_in, norm_mid[None, :])
    normed_mid = gather_rows(normed_mid)

    d_both, hidden, d_mid_blocks, ffn_blocks = ffn_rule(head_arg, normed_mid, upstream, ffn_w)
    d_normed_mid = scatter_blocks(d_mid_blocks)
    d_from_mid, grad_mid = rms_back(residual, norm_mid, d_normed_mid)
    d_residual = upstream_own.astype(f32) + d_from_mid
    branch = gather_rows(d_residual.astype(bf16))

    d_end = jnp.zeros((seqs, DK, DV), f32)
    d_after = jnp.zeros((seqs, 8, WIDTH), f32)
    for stage in range(stages):
        d_all, grad_taps, grad_gain, d_start, d_before = backward_rule(
            head_arg, branch, out_w, run, taps, gain, halo, saved, d_end, d_after
        )
        if stage < stages - 1:
            d_end = passed_along(d_start, "seq", -H)
            d_after = passed_along(d_before, "seq", -H)
    d_all = d_all.reshape(all_rows, -1)

    layer_out = (residual + scatter_blocks(ffn_blocks)).astype(bf16).reshape(inputs.shape)

    def reduce_grads(partial):
        summed = lax.psum_scatter(partial.astype(bf16), "wt", scatter_dimension=0, tiled=True)
        spread = lax.all_gather(summed, "seq")
        if stages > 1:
            spread = spread.reshape((stages, H) + summed.shape).astype(f32)
            spread = jnp.sum(spread, axis=0)
        return spread

    def flat(blocks):
        return blocks.reshape(all_rows, -1)

    ffn_partial = jnp.concatenate(
        [
            contract_rows(flat(normed_mid), flat(d_both)),
            contract_rows(flat(upstream), flat(hidden)),
        ],
        axis=1,
    )
    ffn_grads = join_hidden_rule(reduce_grads(ffn_partial), hidden_all, 3)

    mixer_partial = contract_rows(jnp.concatenate(normed_in, axis=0), d_all)
    out_partial = contract_rows(flat(branch), flat(headed))
    mixer_grads = join_rule(
        reduce_grads(jnp.concatenate([mixer_partial[:, :in_width], out_partial], axis=1)),
        [DK, DK, DV, DV, DV],
    )

    in_w = jnp.concatenate([mixer_w[:, :in_width], beta_w], axis=1)
    d_in_blocks = contract_cols(d_all, in_w).astype(bf16).reshape(H, rows, model)
    d_from_in, _ = rms_back(flat_in, norm_in, scatter_blocks(d_in_blocks))
    grad_input = (d_residual + d_from_in).reshape(inputs.shape)

    grad_in_part = jnp.sum(mixer_partial * in_w.astype(f32), axis=1) / norm_in
    small = jnp.concatenate(
        [
            grad_taps[:CONV].reshape(-1),
            mixer_partial[:, in_width],
            grad_gain[0],
            grad_mid,
            grad_in_part,
        ]
    ).reshape(-1, 128)
    step = 1
    while step < lax.axis_size("wt"):
        small = small + swapped(small, "wt", step)
        step *= 2
    step = H
    while step < peers:
        small = small + swapped(small, "seq", step)
        step *= 2
    small = small[None]
    for bits in (1, 2, 4):
        small = jnp.concatenate([small, swapped(small, "seq", bits)], axis=0)
    small = small[jnp.arange(H) ^ head].reshape(H, -1)
    ends = []
    for bound in (CONV * WIDTH, model, DV, model, model):
        ends.append(bound + (ends[-1] if ends else 0))
    taps_part = small[:, : ends[0]].reshape(H, CONV, WIDTH)

    def joined(pieces):
        return jnp.swapaxes(pieces, 0, 1).reshape(CONV, -1)

    grad_conv = jnp.concatenate(
        [
            joined(taps_part[:, :, :DK]),
            joined(taps_part[:, :, DK : 2 * DK]),
            joined(taps_part[:, :, 2 * DK :]),
        ],
        axis=1,
    )
    grad_beta = small[:, ends[0] : ends[1]].T
    shared = jnp.sum(small[:, ends[1] :], axis=0)
    return (
        layer_out,
        grad_input,
        *mixer_grads,
        *ffn_grads,
        grad_beta,
        grad_conv,
        shared[DV + model :],
        shared[DV : DV + model],
        shared[:DV],
    )


def solution(mesh):
    rows = P("wt", "seq", None)
    cut = P("wt", None)
    in_specs = (rows,) * 3 + (cut,) * 8 + (P(),) * 5
    out_specs = (rows,) * 2 + (cut,) * 8 + (P(),) * 5
    return jax.shard_map(shards, mesh=mesh, in_specs=in_specs, out_specs=out_specs, check_vma=False)
```

```python
import jax
import jax.numpy as jnp
from jax import lax
from jax.experimental import pallas as pl
from jax.experimental.pallas import tpu as pltpu
from jax.sharding import PartitionSpec as P

H = 8
DK = 128
DV = 256
CONV = 4
HALO = 16
WIDTH = 2 * DK + DV
VMEM_LIMIT = 60 * 1024 * 1024
bf16 = jnp.bfloat16
f32 = jnp.float32


def dot(left, right, dims):
    return lax.dot_general(left, right, (dims, ((), ())), preferred_element_type=f32)


def product(left, right):
    return dot(left, right, ((1,), (0,)))


def contract_rows(left, right):
    return dot(left, right, ((0,), (0,)))


def contract_cols(left, right):
    return dot(left, right, ((1,), (1,)))


def parts(values):
    high = values.astype(bf16)
    return high, (values - high.astype(f32)).astype(bf16)


def mul(left, right):
    (lh, ll), (rh, rl) = left, right
    wide = product(jnp.concatenate([lh, ll], 1), jnp.concatenate([rh, rh], 0))
    return wide + product(lh, rl)


def mul_t(left, right):
    (lh, ll), (rh, rl) = left, right
    wide = contract_cols(jnp.concatenate([lh, ll], 1), jnp.concatenate([rh, rh], 1))
    return wide + contract_cols(lh, rl)


def cat_parts(values):
    return jnp.concatenate(parts(values), 1)


def from_cat(both):
    half = both.shape[1] // 2
    return both[:, :half], both[:, half:]


def iotas(size):
    return (
        lax.broadcasted_iota(jnp.int32, (size, size), 0),
        lax.broadcasted_iota(jnp.int32, (size, size), 1),
    )


def unit_inverses(lowers, rows, cols):
    size = rows.shape[0]
    level = 0
    eye = jnp.where(rows == cols, 1.0, 0.0)
    inverses = [eye] * len(lowers)
    while (1 << level) < size:
        together = (rows >> (level + 1)) == (cols >> (level + 1))
        corner = together & (((rows >> level) & 1) == 1) & (((cols >> level) & 1) == 0)
        blocks = [jnp.where(corner, lower, 0.0) for lower in lowers]
        if level == 0:
            inverses = [inverse - block for inverse, block in zip(inverses, blocks)]
        else:
            wholes = [parts(inverse) for inverse in inverses]
            steps = [mul(parts(block), whole) for block, whole in zip(blocks, wholes)]
            steps = [mul(whole, parts(step)) for step, whole in zip(steps, wholes)]
            inverses = [inverse - step for inverse, step in zip(inverses, steps)]
        level += 1
    return inverses


def conv_rows(conv_ref, halo_ref, rows_ref, taps_ref, chunk, seq, slot):
    size = conv_ref.shape[2]
    before = conv_ref[jnp.maximum(chunk - 1, 0), seq, size - HALO :, :]
    before = jnp.where(chunk == 0, halo_ref[seq], before)
    rows_ref[slot, :HALO, :] = before.astype(f32)
    rows_ref[slot, HALO:, :] = conv_ref[chunk, seq].astype(f32)
    total = None
    for tap in range(CONV):
        start = HALO - (CONV - 1) + tap
        term = rows_ref[slot, start : start + size, :] * taps_ref[tap : tap + 1, :]
        total = term if total is None else total + term
    return total


def run_row_of(run_ref, chunk, seq, seqs):
    return run_ref[pl.ds(chunk * seqs + seq, 1), :]


def decays(run_row, rows, cols):
    size = rows.shape[0]
    run_col = jnp.sum(jnp.where(rows == cols, run_row, 0.0), axis=1, keepdims=True)
    spread = jnp.where(rows >= cols, run_col - run_row, 0.0)
    decay_mat = jnp.where(rows >= cols, jnp.exp(spread), 0.0)
    last = run_row[:, size - 1 : size]
    return decay_mat, jnp.exp(run_col), jnp.exp(last - run_col)


def running_sums(values, rows, cols):
    upper = jnp.where(rows <= cols, 1.0, 0.0).astype(bf16)
    total = None
    for _ in range(3):
        part = values.astype(bf16)
        values = values - part.astype(f32)
        term = product(part, upper)
        total = term if total is None else total + term
    return total


def units_of(first, count, seqs):
    return [(first + chunk, seq) for chunk in range(count) for seq in range(seqs)]


FORWARD_CHUNKS = 4


def forward_kernel(head_ref, *refs):
    block_refs, decay_refs, refs = refs[:H], refs[H : 2 * H], refs[2 * H :]
    weight_in, beta_ref, taps_ref, gain_ref, state_ref, halo_ref = refs[:6]
    outs, (run_ref, end_ref), held, refs = refs[6:14], refs[14:16], refs[16:24], refs[24:]
    headed_ref, conv_ref, gate_ref, mixed_ref, inverse_ref, scores_ref, delta_ref, starts_ref = held
    (
        block_ref, weight_ref, log_ref, rows_ref, recall_ref, target_ref, query_ref, write_ref,
        plain_ref, block_sems, weight_sem, out_sems,
    ) = refs
    chunks, seqs, size, _ = conv_ref.shape
    rows, cols = iotas(size)
    head = head_ref[0]

    weight_copy = pltpu.make_async_copy(
        weight_in.at[:, pl.ds(0, WIDTH + DV)], weight_ref, weight_sem
    )
    weight_copy.start()
    block_copies = [
        pltpu.make_async_copy(block_refs[slot], block_ref.at[slot], block_sems.at[slot])
        for slot in range(H)
    ]
    for copy in block_copies[:2]:
        copy.start()
    for slot in range(H):
        logs = jnp.log(decay_refs[slot][pl.ds(head, 1), :])
        for seq in range(seqs):
            log_ref[pl.ds((slot ^ head) * seqs + seq, 1), :] = logs[:, seq * size : (seq + 1) * size]
    run_ref[...] = running_sums(log_ref[...], rows, cols)

    weight_copy.wait()
    for slot in range(H):
        chunk = slot ^ head
        if slot + 2 < H:
            block_copies[slot + 2].start()
        block_copies[slot].wait()
        block = block_ref[slot]
        conv = product(block, weight_ref[:, :WIDTH]).astype(bf16)
        gate = product(block, weight_ref[:, WIDTH:])
        beta = product(block, beta_ref[...])
        for seq in range(seqs):
            span = slice(seq * size, (seq + 1) * size)
            conv_ref[chunk, seq] = conv[span]
            gate_ref[chunk, seq, :, :DV] = gate[span]
            gate_ref[chunk, seq, :, DV:] = beta[span]

    def send(index, first, count):
        span = pl.ds(first, count)
        pltpu.make_async_copy(
            held[index].at[span], outs[index].at[span], out_sems.at[index]
        ).start()

    def prepare(turn, _):
        units = units_of(turn * FORWARD_CHUNKS, FORWARD_CHUNKS, seqs)
        lowers = []

        @pl.when(turn > 0)
        def _():
            for index in (1, 2, 4, 5):
                send(index, (turn - 1) * FORWARD_CHUNKS, FORWARD_CHUNKS)

        for slot, (chunk, seq) in enumerate(units):
            summed = conv_rows(conv_ref, halo_ref, rows_ref, taps_ref, chunk, seq, slot)
            active = summed * jax.nn.sigmoid(summed)
            query = active[:, :DK]
            key = active[:, DK : 2 * DK]
            key = key * lax.rsqrt(jnp.sum(key * key, axis=1, keepdims=True) + 1e-06)
            beta = jax.nn.sigmoid(gate_ref[chunk, seq, :, DV : DV + 1])
            decay_mat, growth, fade = decays(run_row_of(run_ref, chunk, seq, seqs), rows, cols)
            target_ref[chunk, seq] = beta * active[:, 2 * DK :]
            query_ref[chunk, seq] = cat_parts(growth * query)
            write_ref[chunk, seq] = cat_parts((fade * key).T)
            recall_ref[chunk, seq] = cat_parts(beta * growth * key)
            key_parts = parts(key)
            gram = mul_t(key_parts, key_parts)
            lowers.append(jnp.where(rows > cols, beta * gram * decay_mat, 0.0))
            scores = mul_t(parts(query), key_parts) * decay_mat
            plain_ref[chunk, seq] = cat_parts(scores)
            scores_ref[chunk, seq] = cat_parts(scores.T)
        inverses = unit_inverses(lowers, rows, cols)
        for (chunk, seq), inverse in zip(units, inverses):
            inverse_parts = parts(inverse)
            recall = mul(inverse_parts, from_cat(recall_ref[chunk, seq]))
            recall_ref[chunk, seq] = cat_parts(recall)
            target_ref[chunk, seq] = mul(inverse_parts, parts(target_ref[chunk, seq]))
            inverse_ref[chunk, seq] = cat_parts(inverse.T)
        return 0

    lax.fori_loop(0, chunks // FORWARD_CHUNKS, prepare, 0)

    def advance(chunk, states):
        following = []

        @pl.when(chunk == 0)
        def _():
            for index in (1, 2, 4, 5):
                send(index, chunks - FORWARD_CHUNKS, FORWARD_CHUNKS)

        @pl.when(chunk > 0)
        def _():
            for index in (0, 3, 6, 7):
                send(index, chunk - 1, 1)

        for seq in range(seqs):
            state = states[seq]
            starts_ref[chunk, seq] = state
            state_parts = parts(state)
            delta = target_ref[chunk, seq] - mul(from_cat(recall_ref[chunk, seq]), state_parts)
            delta_parts = parts(delta)
            total = jnp.exp(run_row_of(run_ref, chunk, seq, seqs)[:, size - 1 : size])
            following.append(
                total * state + mul(from_cat(write_ref[chunk, seq]), delta_parts)
            )
            delta_ref[chunk, seq] = delta
            read = mul(from_cat(query_ref[chunk, seq]), state_parts)
            read = read + mul(from_cat(plain_ref[chunk, seq]), delta_parts)
            mixed_ref[chunk, seq] = read
            scale = lax.rsqrt(jnp.mean(read * read, axis=1, keepdims=True) + 1e-05)
            gate = gate_ref[chunk, seq, :, :DV]
            headed = read * scale * gain_ref[...] * (gate * jax.nn.sigmoid(gate))
            headed_ref[chunk, seq] = headed.astype(bf16)
        return tuple(following)

    final = lax.fori_loop(0, chunks, advance, tuple(state_ref[seq] for seq in range(seqs)))
    for seq in range(seqs):
        end_ref[seq] = final[seq]
    for index in (0, 3, 6, 7):
        send(index, chunks - 1, 1)
    for index in range(len(held)):
        pltpu.make_async_copy(held[index], outs[index], out_sems.at[index]).wait()


BACKWARD_CHUNKS = 2


def backward_kernel(head_ref, *refs):
    branch_refs, weight_in, refs = refs[:H], refs[H], refs[H + 1 :]
    saved, refs = refs[:7], refs[7:]
    run_ref, taps_ref, gain_ref, halo_ref, d_end_ref, d_after_ref = refs[:6]
    d_all_out, grad_taps_ref, grad_gain_ref, d_start_ref, d_before_ref = refs[6:11]
    branch_ref, weight_ref, held, refs = refs[11], refs[12], refs[13:20], refs[20:]
    conv_ref, gate_ref, mixed_ref, inverse_ref, scores_ref, delta_ref, starts_ref = held
    (
        rows_ref, d_headed_ref, hold_ref, carry_ref, base_ref, back_ref, d_target_ref, d_state_ref,
        d_conv_ref, d_all_ref, slope_ref, active_ref, column_ref,
        block_sems, weight_sem, saved_sems, out_sem,
    ) = refs
    chunks, seqs, size, _ = conv_ref.shape
    rows, cols = iotas(size)
    head = head_ref[0]

    weight_copy = pltpu.make_async_copy(
        weight_in.at[:, pl.ds(WIDTH + DV, DV)], weight_ref, weight_sem
    )
    weight_copy.start()
    block_copies = [
        pltpu.make_async_copy(branch_refs[slot], branch_ref.at[slot], block_sems.at[slot])
        for slot in range(H)
    ]
    for copy in block_copies[:2]:
        copy.start()
    saved_copies = [
        pltpu.make_async_copy(saved[index], held[index], saved_sems.at[index])
        for index in range(len(saved))
    ]

    lane = lax.broadcasted_iota(jnp.int32, (size, 128), 1)
    grad_gain_ref[...] = jnp.zeros_like(grad_gain_ref)
    grad_taps_ref[...] = jnp.zeros_like(grad_taps_ref)

    weight_copy.wait()
    for slot in range(H):
        if slot + 2 < H:
            block_copies[slot + 2].start()
        if 1 < slot < len(saved_copies):
            saved_copies[slot - 2].start()
        block_copies[slot].wait()
        d_headed = product(branch_ref[slot], weight_ref[...])
        for seq in range(seqs):
            d_headed_ref[slot ^ head, seq] = d_headed[seq * size : (seq + 1) * size]
    for copy in saved_copies[:5]:
        copy.wait()
    for copy in saved_copies[5:]:
        copy.start()

    def prepare(turn, _):
        units = units_of(turn * BACKWARD_CHUNKS, BACKWARD_CHUNKS, seqs)
        for chunk, seq in units:
            unit = chunk * seqs + seq
            summed = conv_rows(conv_ref, halo_ref, rows_ref, taps_ref, chunk, seq, unit)
            logistic = jax.nn.sigmoid(summed)
            active = summed * logistic
            slope_ref[unit] = logistic * (1.0 + summed * (1.0 - logistic))
            query = active[:, :DK]
            raw = active[:, DK : 2 * DK]
            shrink = lax.rsqrt(jnp.sum(raw * raw, axis=1, keepdims=True) + 1e-06)
            key = raw * shrink
            active_ref[unit, :, :DK] = query
            active_ref[unit, :, DK : 2 * DK] = key
            active_ref[unit, :, 2 * DK :] = active[:, 2 * DK :]
            beta = jax.nn.sigmoid(gate_ref[chunk, seq, :, DV : DV + 1])
            column_ref[unit] = jnp.where(lane == 0, shrink, beta)
            _, growth, fade = decays(run_row_of(run_ref, chunk, seq, seqs), rows, cols)
            mixed = mixed_ref[chunk, seq]
            d_headed = d_headed_ref[chunk, seq]
            gate = gate_ref[chunk, seq, :, :DV]
            logistic = jax.nn.sigmoid(gate)
            scale = lax.rsqrt(jnp.mean(mixed * mixed, axis=1, keepdims=True) + 1e-05)
            normed = mixed * scale
            swish = gate * logistic
            inner = d_headed * gain_ref[...] * swish
            d_mixed = scale * (inner - normed * jnp.mean(normed * inner, axis=1, keepdims=True))
            grad_gain_ref[...] += jnp.sum(d_headed * normed * swish, axis=0, keepdims=True)
            d_gate = d_headed * gain_ref[...] * normed * logistic * (1.0 + gate * (1.0 - logistic))
            d_all_ref[chunk ^ head, seq, :, WIDTH : WIDTH + DV] = d_gate.astype(bf16)
            d_headed_ref[chunk, seq] = d_mixed
            d_mixed_parts = parts(d_mixed)
            inverse_parts = from_cat(inverse_ref[chunk, seq])
            scored = mul(from_cat(scores_ref[chunk, seq]), d_mixed_parts)
            base_ref[chunk, seq] = mul(inverse_parts, parts(scored))
            hold_ref[chunk, seq] = cat_parts(mul(inverse_parts, parts(fade * key)))
            back_ref[chunk, seq] = mul(parts((growth * query).T), d_mixed_parts)
            carry_ref[chunk, seq] = cat_parts((beta * growth * key).T)
        return 0

    lax.fori_loop(0, chunks // BACKWARD_CHUNKS, prepare, 0)

    def advance(step, d_states):
        chunk = chunks - 1 - step
        following = []
        for seq in range(seqs):
            d_state = d_states[seq]
            d_state_ref[chunk, seq] = d_state
            d_target = base_ref[chunk, seq] + mul(from_cat(hold_ref[chunk, seq]), parts(d_state))
            d_target_ref[chunk, seq] = d_target
            total = jnp.exp(run_row_of(run_ref, chunk, seq, seqs)[:, size - 1 : size])
            back = mul(from_cat(carry_ref[chunk, seq]), parts(d_target))
            following.append(total * d_state + back_ref[chunk, seq] - back)
        return tuple(following)

    first = lax.fori_loop(0, chunks, advance, tuple(d_end_ref[seq] for seq in range(seqs)))
    for seq in range(seqs):
        d_start_ref[seq] = first[seq]
        d_conv_ref[seq, size:, :] = d_after_ref[seq]
    for copy in saved_copies[5:]:
        copy.wait()

    def send(chunk):
        slot = chunk ^ head
        pltpu.make_async_copy(d_all_ref.at[slot], d_all_out.at[slot], out_sem).start()

    def finish(turn, _):
        units = [
            (chunks - 1 - turn * BACKWARD_CHUNKS - back, seq)
            for back in range(BACKWARD_CHUNKS)
            for seq in range(seqs)
        ]

        @pl.when(turn > 0)
        def _():
            for back in range(BACKWARD_CHUNKS):
                send(chunks - 1 - (turn - 1) * BACKWARD_CHUNKS - back)

        for chunk, seq in units:
            unit = chunk * seqs + seq
            slope = slope_ref[unit]
            query = active_ref[unit, :, :DK]
            key = active_ref[unit, :, DK : 2 * DK]
            value = active_ref[unit, :, 2 * DK :]
            shrink = column_ref[unit, :, 0:1]
            beta = column_ref[unit, :, 1:2]
            decay_mat, growth, fade = decays(run_row_of(run_ref, chunk, seq, seqs), rows, cols)
            key_parts = parts(key)
            gram = mul_t(key_parts, key_parts) * decay_mat
            d_target = d_target_ref[chunk, seq]
            delta_parts = parts(delta_ref[chunk, seq])
            start_parts = parts(starts_ref[chunk, seq])
            both = parts(jnp.concatenate([d_target, d_headed_ref[chunk, seq]], 0))
            on_delta = mul_t(both, delta_parts)
            on_state = mul_t(both, start_parts)
            d_lower = jnp.where(rows > cols, -on_delta[:size], 0.0)
            d_scores = on_delta[size:] * decay_mat
            through = on_state[:size]
            d_gram = d_lower * decay_mat * beta
            d_query = growth * on_state[size:] + mul(parts(d_scores), key_parts)
            d_key = mul(parts(d_scores.T), parts(query))
            d_key = d_key + mul(parts(d_gram + d_gram.T), key_parts)
            d_key = d_key + fade * mul_t(delta_parts, parts(d_state_ref[chunk, seq]))
            d_key = d_key - (beta * growth) * through
            d_beta = (
                jnp.sum(d_target * value, axis=1, keepdims=True)
                - growth * jnp.sum(key * through, axis=1, keepdims=True)
                + jnp.sum(d_lower * gram, axis=1, keepdims=True)
            )
            d_raw = shrink * (d_key - key * jnp.sum(key * d_key, axis=1, keepdims=True))
            d_conv = jnp.concatenate([d_query, d_raw, beta * d_target], 1) * slope
            d_conv_ref[seq, :size, :] = d_conv
            d_in = None
            for tap in range(CONV):
                start = HALO - (CONV - 1) + tap
                grad_taps_ref[tap : tap + 1, :] += jnp.sum(
                    d_conv * rows_ref[unit, start : start + size, :], axis=0, keepdims=True
                )
                shift = CONV - 1 - tap
                term = d_conv_ref[seq, shift : shift + size, :] * taps_ref[tap : tap + 1, :]
                d_in = term if d_in is None else d_in + term
            d_conv_ref[seq, size:, :] = d_conv[:8, :]
            d_all_ref[chunk ^ head, seq, :, :WIDTH] = d_in.astype(bf16)
            d_logit = d_beta * beta * (1.0 - beta)
            d_all_ref[chunk ^ head, seq, :, WIDTH + DV :] = jnp.where(
                lane == 0, d_logit, 0.0
            ).astype(bf16)
        return 0

    lax.fori_loop(0, chunks // BACKWARD_CHUNKS, finish, 0)
    for seq in range(seqs):
        d_before_ref[seq] = d_conv_ref[seq, size:, :]
    for chunk in range(BACKWARD_CHUNKS):
        send(chunk)
    pltpu.make_async_copy(d_all_ref, d_all_out, out_sem).wait()


def whole(count):
    return [pl.BlockSpec(memory_space=pltpu.VMEM)] * count


def scalar():
    return [pl.BlockSpec(memory_space=pltpu.SMEM)]


shaped = jax.ShapeDtypeStruct


def cost(flops):
    return pl.CostEstimate(flops=flops, bytes_accessed=0, transcendentals=0)


def kernel_params():
    return pltpu.CompilerParams(vmem_limit_bytes=VMEM_LIMIT)


def anywhere(count):
    return [pl.BlockSpec(memory_space=pltpu.HBM)] * count


def forward_rule(head, blocks, decay_blocks, weight, beta_w, taps, gain, state, halo):
    rows, model = blocks[0].shape
    seqs = state.shape[0]
    size = rows // seqs
    lead = (H, seqs)
    held = [
        (lead + (size, DV), bf16),
        (lead + (size, WIDTH), bf16),
        (lead + (size, DV + 128), f32),
        (lead + (size, DV), f32),
        (lead + (size, 2 * size), bf16),
        (lead + (size, 2 * size), bf16),
        (lead + (size, DV), f32),
        (lead + (DK, DV), f32),
    ]
    return pl.pallas_call(
        forward_kernel,
        name="mixer_forward",
        out_shape=[shaped(*item) for item in held]
        + [shaped((H * seqs, size), f32), shaped((seqs, DK, DV), f32)],
        in_specs=scalar() + anywhere(H) + whole(H) + anywhere(1) + whole(5),
        out_specs=anywhere(8) + whole(2),
        scratch_shapes=[pltpu.VMEM(*item) for item in held]
        + [
            pltpu.VMEM((H, rows, model), bf16),
            pltpu.VMEM((model, WIDTH + DV), bf16),
            pltpu.VMEM((H * seqs, size), f32),
            pltpu.VMEM((FORWARD_CHUNKS * seqs, HALO + size, WIDTH), f32),
            pltpu.VMEM(lead + (size, 2 * DK), bf16),
            pltpu.VMEM(lead + (size, DV), f32),
            pltpu.VMEM(lead + (size, 2 * DK), bf16),
            pltpu.VMEM(lead + (DK, 2 * size), bf16),
            pltpu.VMEM(lead + (size, 2 * size), bf16),
            pltpu.SemaphoreType.DMA((H,)),
            pltpu.SemaphoreType.DMA,
            pltpu.SemaphoreType.DMA((8,)),
        ],
        compiler_params=kernel_params(),
    )(head, *blocks, *decay_blocks, weight, beta_w, taps, gain, state, halo)


def backward_rule(head, branch, weight, saved, run, taps, gain, halo, d_end, d_after):
    rows, model = branch[0].shape
    seqs = d_end.shape[0]
    size = rows // seqs
    lead = (H, seqs)
    return pl.pallas_call(
        backward_kernel,
        name="mixer_backward",
        out_shape=(
            shaped(lead + (size, WIDTH + DV + 128), bf16),
            shaped((8, WIDTH), f32),
            shaped((1, DV), f32),
            shaped((seqs, DK, DV), f32),
            shaped((seqs, 8, WIDTH), f32),
        ),
        in_specs=scalar() + anywhere(H + 8) + whole(6),
        out_specs=tuple(anywhere(1) + whole(4)),
        scratch_shapes=[
            pltpu.VMEM((H, rows, model), bf16),
            pltpu.VMEM((model, DV), bf16),
        ]
        + [pltpu.VMEM(item.shape, item.dtype) for item in saved]
        + [
            pltpu.VMEM((H * seqs, HALO + size, WIDTH), f32),
            pltpu.VMEM(lead + (size, DV), f32),
            pltpu.VMEM(lead + (size, 2 * DK), bf16),
            pltpu.VMEM(lead + (DK, 2 * size), bf16),
            pltpu.VMEM(lead + (size, DV), f32),
            pltpu.VMEM(lead + (DK, DV), f32),
            pltpu.VMEM(lead + (size, DV), f32),
            pltpu.VMEM(lead + (DK, DV), f32),
            pltpu.VMEM((seqs, size + 8, WIDTH), f32),
            pltpu.VMEM(lead + (size, WIDTH + DV + 128), bf16),
            pltpu.VMEM((H * seqs, size, WIDTH), f32),
            pltpu.VMEM((H * seqs, size, WIDTH), f32),
            pltpu.VMEM((H * seqs, size, 128), f32),
            pltpu.SemaphoreType.DMA((H,)),
            pltpu.SemaphoreType.DMA,
            pltpu.SemaphoreType.DMA((7,)),
            pltpu.SemaphoreType.DMA,
        ],
        compiler_params=kernel_params(),
    )(head, *branch, weight, *saved, run, taps, gain, halo, d_end, d_after)


def out_kernel(
    weight_in, headed_ref, inputs_ref, gain_ref, residual_ref, normed_ref, weight_ref, sems
):
    copies = [
        pltpu.make_async_copy(weight_in.at[peer], weight_ref.at[peer], sems.at[peer])
        for peer in range(H)
    ]
    for copy in copies:
        copy.start()
    total = inputs_ref[...].astype(f32)
    for peer in range(H):
        copies[peer].wait()
        total = total + contract_cols(headed_ref[peer], weight_ref[peer])
    residual_ref[...] = total
    scale = lax.rsqrt(jnp.mean(total * total, axis=1, keepdims=True) + 1e-05)
    normed_ref[...] = (total * scale * gain_ref[...]).astype(bf16)


def out_rule(weight, headed, inputs, gain):
    return pl.pallas_call(
        out_kernel,
        name="out_projection",
        out_shape=(shaped(inputs.shape, f32), shaped(inputs.shape, bf16)),
        in_specs=anywhere(1) + whole(3),
        out_specs=tuple(whole(2)),
        scratch_shapes=[pltpu.VMEM(weight.shape, bf16), pltpu.SemaphoreType.DMA((H,))],
        compiler_params=kernel_params(),
    )(weight, headed, inputs, gain)


def ffn_kernel(*refs):
    normed_refs, up_refs, refs = refs[:H], refs[H : 2 * H], refs[2 * H :]
    weight_in, d_both_ref, hidden_ref, d_even_ref, d_odd_ref, even_ref, odd_ref = refs[:7]
    normed_all_ref, up_all_ref, weight_ref, normed_sems, up_sems, weight_sem = refs[7:]
    share = weight_ref.shape[1] // 3
    step = pl.program_id(0)

    def copy_of(source, target, sems, slot):
        return pltpu.make_async_copy(source, target.at[slot], sems.at[slot])

    def start_pair(pair):
        for slot in (2 * pair, 2 * pair + 1):
            copy_of(normed_refs[slot], normed_all_ref, normed_sems, slot).start()
            copy_of(up_refs[slot], up_all_ref, up_sems, slot).start()

    @pl.when(step == 0)
    def _():
        weight_copy = pltpu.make_async_copy(weight_in, weight_ref, weight_sem)
        weight_copy.start()
        start_pair(0)
        weight_copy.wait()

    for later in range(1, H // 2):

        @pl.when(step == later - 1)
        def _():
            start_pair(later)

    for side, d_in_ref, out_ref in ((0, d_even_ref, even_ref), (1, d_odd_ref, odd_ref)):
        slot = 2 * step + side
        copy_of(normed_refs[0], normed_all_ref, normed_sems, slot).wait()
        copy_of(up_refs[0], up_all_ref, up_sems, slot).wait()
        both = product(normed_all_ref[slot], weight_ref[:, : 2 * share])
        d_hidden = product(up_all_ref[slot], weight_ref[:, 2 * share :])
        gate, up = both[:, :share], both[:, share:]
        logistic = jax.nn.sigmoid(gate)
        swish = gate * logistic
        hidden = (swish * up).astype(bf16)
        hidden_ref[side] = hidden
        d_gate = (d_hidden * up * logistic * (1.0 + gate * (1.0 - logistic))).astype(bf16)
        d_up = (d_hidden * swish).astype(bf16)
        d_both = jnp.concatenate([d_gate, d_up], 1)
        d_both_ref[side] = d_both
        d_in_ref[0] = contract_cols(d_both, weight_ref[:, : 2 * share]).astype(bf16)
        out_ref[0] = contract_cols(hidden, weight_ref[:, 2 * share :]).astype(bf16)


def ffn_rule(normed, upstream, weight):
    rows, model = normed[0].shape
    share = weight.shape[1] // 3

    def moving(count, width):
        return pl.BlockSpec((count, rows, width), lambda step: (step, 0, 0))

    return pl.pallas_call(
        ffn_kernel,
        name="feed_forward",
        grid=(H // 2,),
        in_specs=anywhere(2 * H + 1),
        out_specs=[moving(2, 2 * share), moving(2, share)] + [moving(1, model)] * 4,
        out_shape=[shaped((H, rows, 2 * share), bf16), shaped((H, rows, share), bf16)]
        + [shaped((H // 2, rows, model), bf16)] * 4,
        scratch_shapes=[pltpu.VMEM((H, rows, model), bf16)] * 2
        + [
            pltpu.VMEM(weight.shape, bf16),
            pltpu.SemaphoreType.DMA((H,)),
            pltpu.SemaphoreType.DMA((H,)),
            pltpu.SemaphoreType.DMA,
        ],
        compiler_params=kernel_params(),
    )(*normed, *upstream, weight)


GRAD_TILE = 256


def ffn_grads_kernel(*refs):
    normed_refs, up_refs, (d_both_ref, hidden_ref, out_ref) = refs[:H], refs[H : 2 * H], refs[2 * H :]
    wide = d_both_ref.shape[1]
    normed = jnp.concatenate([ref[...] for ref in normed_refs], 0)
    out_ref[:, :wide] = contract_rows(normed, d_both_ref[...]).astype(bf16)
    upstream = jnp.concatenate([ref[...] for ref in up_refs], 0)
    out_ref[:, wide:] = contract_rows(upstream, hidden_ref[...]).astype(bf16)


def ffn_grads_rule(normed, upstream, d_both, hidden):
    rows, model = normed[0].shape
    width = d_both.shape[1] + hidden.shape[1]
    columns = pl.BlockSpec((rows, GRAD_TILE), lambda step: (0, step))
    return pl.pallas_call(
        ffn_grads_kernel,
        name="feed_forward_grads",
        grid=(model // GRAD_TILE,),
        in_specs=[columns] * (2 * H)
        + [
            pl.BlockSpec(d_both.shape, lambda step: (0, 0)),
            pl.BlockSpec(hidden.shape, lambda step: (0, 0)),
        ],
        out_specs=pl.BlockSpec((GRAD_TILE, width), lambda step: (step, 0)),
        out_shape=shaped((model, width), bf16),
        cost_estimate=cost(4 * H * rows * model * width),
        compiler_params=kernel_params(),
    )(*normed, *upstream, d_both, hidden)


def mixer_grads_kernel(head_ref, *refs):
    normed_refs, branch_refs, refs = refs[:H], refs[H : 2 * H], refs[2 * H :]
    d_all_ref, headed_ref, weight_ref, beta_ref, out_ref, small_ref = refs
    head = head_ref[0]
    width = WIDTH + DV
    normed = jnp.concatenate([ref[...] for ref in normed_refs], 0)
    partial = contract_rows(normed, d_all_ref[:, :width])
    out_ref[:, :width] = partial.astype(bf16)
    beta = contract_rows(normed, d_all_ref[:, width:])
    branch = jnp.concatenate([ref[...] for ref in branch_refs], 0)
    headed = jnp.concatenate([headed_ref[slot ^ head] for slot in range(H)], 0)
    out_ref[:, width:] = contract_rows(branch, headed).astype(bf16)
    weighed = jnp.sum(partial * weight_ref[:, :width].astype(f32), axis=1, keepdims=True)
    weighed = weighed + beta[:, :1] * beta_ref[:, :1].astype(f32)
    lane = lax.broadcasted_iota(jnp.int32, beta.shape, 1)
    small_ref[...] = jnp.where(lane == 0, beta, jnp.where(lane == 1, weighed, 0.0))


def mixer_grads_rule(head, normed, branch, d_all, headed, weight, beta_w):
    rows, model = normed[0].shape
    width = WIDTH + 2 * DV
    columns = pl.BlockSpec((rows, GRAD_TILE), lambda step: (0, step))
    return pl.pallas_call(
        mixer_grads_kernel,
        name="mixer_grads",
        grid=(model // GRAD_TILE,),
        in_specs=scalar()
        + [columns] * (2 * H)
        + [
            pl.BlockSpec(d_all.shape, lambda step: (0, 0)),
            pl.BlockSpec(headed.shape, lambda step: (0, 0, 0)),
            pl.BlockSpec((GRAD_TILE, width), lambda step: (step, 0)),
            pl.BlockSpec((GRAD_TILE, 128), lambda step: (step, 0)),
        ],
        out_specs=[
            pl.BlockSpec((GRAD_TILE, width), lambda step: (step, 0)),
            pl.BlockSpec((GRAD_TILE, 128), lambda step: (step, 0)),
        ],
        out_shape=[shaped((model, width), bf16), shaped((model, 128), f32)],
        compiler_params=kernel_params(),
    )(head, *normed, *branch, d_all, headed, weight, beta_w)


def d_in_kernel(d_all_ref, weight_ref, beta_ref, even_ref, odd_ref):
    width = WIDTH + DV
    for side, out_ref in ((0, even_ref), (1, odd_ref)):
        d_all = d_all_ref[side]
        total = contract_cols(d_all[:, :width], weight_ref[:, :width])
        total = total + contract_cols(d_all[:, width:], beta_ref[...])
        out_ref[0] = total.astype(bf16)


def d_in_rule(d_all, weight, beta_w):
    _, rows, width = d_all.shape
    model = weight.shape[0]
    out = pl.BlockSpec((1, rows, model), lambda step: (step, 0, 0))
    return pl.pallas_call(
        d_in_kernel,
        name="mixer_d_in",
        grid=(H // 2,),
        in_specs=[
            pl.BlockSpec((2, rows, width), lambda step: (step, 0, 0)),
            pl.BlockSpec(weight.shape, lambda step: (0, 0)),
            pl.BlockSpec(beta_w.shape, lambda step: (0, 0)),
        ],
        out_specs=[out, out],
        out_shape=[shaped((H // 2, rows, model), bf16)] * 2,
        compiler_params=kernel_params(),
    )(d_all, weight, beta_w)


JOIN_ROWS = 32


def join_kernel(spread_ref, *out_refs):
    start = 0
    for out_ref in out_refs:
        width = out_ref.shape[1] // H
        for peer in range(H):
            piece = spread_ref[peer, :, start : start + width]
            out_ref[:, peer * width : (peer + 1) * width] = piece.astype(f32)
        start += width


def join_rule(spread, widths):
    count, rows, width = spread.shape
    return pl.pallas_call(
        join_kernel,
        name="join_heads",
        grid=(rows // JOIN_ROWS,),
        in_specs=[pl.BlockSpec((count, JOIN_ROWS, width), lambda step: (0, step, 0))],
        out_specs=[pl.BlockSpec((JOIN_ROWS, count * width), lambda step: (step, 0)) for width in widths],
        out_shape=[shaped((rows, count * width), f32) for width in widths],
        compiler_params=kernel_params(),
    )(spread)


def join_hidden_kernel(spread_ref, *out_refs):
    count, _, width = spread_ref.shape
    share = width // len(out_refs)
    total = out_refs[0].shape[1]
    for index, out_ref in enumerate(out_refs):
        for peer in range(count):
            first = peer * share
            skip = first - min(first, total - share)
            piece = spread_ref[peer, :, index * share + skip : (index + 1) * share]
            out_ref[:, first : first + share - skip] = piece.astype(f32)


def join_hidden_rule(spread, total, pieces):
    count, rows, width = spread.shape
    return pl.pallas_call(
        join_hidden_kernel,
        name="join_hidden",
        grid=(rows // JOIN_ROWS,),
        in_specs=[pl.BlockSpec((count, JOIN_ROWS, width), lambda step: (0, step, 0))],
        out_specs=[pl.BlockSpec((JOIN_ROWS, total), lambda step: (step, 0))] * pieces,
        out_shape=[shaped((rows, total), f32)] * pieces,
        compiler_params=kernel_params(),
    )(spread)


def passed_along(array, axis, by):
    peers = lax.axis_size(axis)
    pairs = [(i, i + by) for i in range(peers) if 0 <= i + by < peers]
    return lax.ppermute(array, axis, pairs)


def swapped(array, axis, bits):
    return lax.ppermute(array, axis, [(i, i ^ bits) for i in range(lax.axis_size(axis))])


def neighbours(own):
    return [own] + [swapped(own, "seq", bits) for bits in range(2, H, 2)]


def with_siblings(blocks):
    return [each for block in blocks for each in (block, swapped(block, "seq", 1))]


def gather_blocks(own):
    return with_siblings(neighbours(own))


def pair_sums(even, handed):
    sums = [even[i].astype(f32) + handed[i].astype(f32) for i in range(H // 2)]
    return sums[0], [each.astype(bf16) for each in sums[1:]]


def exchanged(sums):
    return [swapped(sums[i - 1], "seq", 2 * i) for i in range(1, H // 2)]


def total_of(own, received):
    for piece in received:
        own = own + piece.astype(f32)
    return own


def rms_scale(values):
    return lax.rsqrt(jnp.mean(values * values, axis=-1, keepdims=True) + 1e-05)


def rms_back(values, gain, d_normed):
    scale = rms_scale(values)
    normed = values * scale
    pulled = d_normed * gain
    d_values = scale * (pulled - normed * jnp.mean(normed * pulled, axis=-1, keepdims=True))
    return d_values, jnp.sum(d_normed * normed, axis=0)


def shards(
    inputs,
    cotangent,
    decay,
    w_query,
    w_key,
    w_value,
    w_gate_out,
    w_out,
    w_ffn_gate,
    w_ffn_up,
    w_ffn_down,
    w_beta,
    conv_weight,
    norm_in,
    norm_mid,
    norm_head,
):
    seqs, size, model = inputs.shape
    rows = seqs * size
    peers = lax.axis_size("seq")
    stages = peers // H
    groups = None
    if stages > 1:
        groups = [[stage * H + head for head in range(H)] for stage in range(stages)]
    place = lax.axis_index("seq")
    head = lax.rem(place, H)
    head_arg = head.reshape(1)
    all_rows = H * rows
    hidden_all = w_ffn_gate.shape[1]
    share = -(-hidden_all // (H * 128)) * 128

    def gather_rows(local):
        return lax.all_gather(local, "seq", axis_index_groups=groups)

    def own_columns(weight, width):
        return lax.dynamic_slice_in_dim(weight, head * width, width, axis=1)

    def own_hidden(weight):
        start = jnp.minimum(head * share, hidden_all - share)
        piece = lax.dynamic_slice_in_dim(weight, start, share, axis=1)
        lane = lax.broadcasted_iota(jnp.int32, piece.shape, 1)
        return jnp.where(lane + start >= head * share, piece, jnp.zeros_like(piece))

    def gather_weight(local):
        return lax.all_gather(local, "wt", axis=0, tiled=True)

    mixer_w = gather_weight(
        jnp.concatenate(
            [
                own_columns(w_query, DK),
                own_columns(w_key, DK),
                own_columns(w_value, DV),
                own_columns(w_gate_out, DV),
                own_columns(w_out, DV),
            ],
            axis=1,
        )
    )
    ffn_w_own = jnp.concatenate(
        [own_hidden(w_ffn_gate), own_hidden(w_ffn_up), own_hidden(w_ffn_down)], axis=1
    )

    def reduce_weight(partial):
        return lax.psum_scatter(partial, "wt", scatter_dimension=0, tiled=True)

    def spread_grads(summed):
        spread = lax.all_gather(summed, "seq")
        if stages > 1:
            spread = spread.reshape((stages, H) + summed.shape).astype(f32)
            spread = jnp.sum(spread, axis=0)
        return spread

    own_in = inputs.reshape(rows, model)
    flat_in = own_in.astype(f32)
    normed_own = (flat_in * rms_scale(flat_in) * norm_in).astype(bf16)
    upstream_own = cotangent.reshape(rows, model)
    decay_rows = decay.reshape(rows, H).T
    near_in = neighbours(normed_own)
    near_in, late_upstream, ffn_w_own = lax.optimization_barrier(
        (near_in, upstream_own, ffn_w_own)
    )
    up_near = neighbours(late_upstream)
    normed_in, decay_blocks, mixer_w = lax.optimization_barrier(
        (with_siblings(near_in), gather_blocks(decay_rows), mixer_w)
    )
    ffn_w = gather_weight(ffn_w_own)
    beta_w = jnp.pad(own_columns(w_beta, 1), ((0, 0), (0, 127)))
    in_width = WIDTH + DV
    out_w = gather_rows(mixer_w[:, in_width:])

    taps = jnp.concatenate(
        [
            own_columns(conv_weight[:, : H * DK], DK),
            own_columns(conv_weight[:, H * DK : 2 * H * DK], DK),
            own_columns(conv_weight[:, 2 * H * DK :], DV),
        ],
        axis=1,
    )
    taps = jnp.pad(taps, ((0, 8 - CONV), (0, 0)))
    gain = norm_head[None, :]

    state = jnp.zeros((seqs, DK, DV), f32)
    halo = jnp.zeros((seqs, HALO, WIDTH), bf16)
    if stages > 1:
        edges = lax.all_gather(normed_own.reshape(seqs, size, model)[:, size - HALO :], "seq")
        before = lax.dynamic_index_in_dim(edges, jnp.maximum(place - head - 1, 0), keepdims=False)
        rolled = product(before.reshape(seqs * HALO, model), mixer_w[:, :WIDTH]).astype(bf16)
        halo = jnp.where(place >= H, rolled.reshape(halo.shape), halo)
    for stage in range(stages):
        headed, *saved, ending = forward_rule(
            head_arg, normed_in, decay_blocks, mixer_w, beta_w, taps, gain, state, halo
        )
        run = saved.pop()
        if stage < stages - 1:
            state = passed_along(ending, "seq", H)

    headed = headed.reshape(H, rows, DV)
    headed, up_near = lax.optimization_barrier((headed, up_near))
    upstream = with_siblings(up_near)
    own_headed = lax.all_to_all(headed, "seq", 0, 0, axis_index_groups=groups, tiled=True)
    residual, normed_own = out_rule(out_w, own_headed, own_in, norm_mid[None, :])
    normed_mid = gather_blocks(normed_own)

    d_both, hidden, d_even, d_odd, even, odd = ffn_rule(normed_mid, upstream, ffn_w)
    ffn_partial = ffn_grads_rule(
        normed_mid, upstream, d_both.reshape(all_rows, -1), hidden.reshape(all_rows, -1)
    )
    ffn_summed = reduce_weight(ffn_partial)
    handed, _ = lax.optimization_barrier((swapped(d_odd, "seq", 1), ffn_partial))
    own_sum, sums = pair_sums(d_even, handed)
    received = exchanged(sums)
    ffn_own, ffn_sums = pair_sums(even, swapped(odd, "seq", 1))
    received, ffn_own, ffn_sums = lax.optimization_barrier((received, ffn_own, ffn_sums))
    d_normed_mid = total_of(own_sum, received)
    d_from_mid, grad_mid = rms_back(residual, norm_mid, d_normed_mid)
    d_residual = upstream_own.astype(f32) + d_from_mid
    branch, ffn_sums, ffn_summed = lax.optimization_barrier(
        (gather_blocks(d_residual.astype(bf16)), ffn_sums, ffn_summed)
    )
    ffn_spread = spread_grads(ffn_summed)
    ffn_received = exchanged(ffn_sums)

    d_end = jnp.zeros((seqs, DK, DV), f32)
    d_after = jnp.zeros((seqs, 8, WIDTH), f32)
    for stage in range(stages):
        d_all, grad_taps, grad_gain, d_start, d_before = backward_rule(
            head_arg, branch, mixer_w, saved, run, taps, gain, halo, d_end, d_after
        )
        if stage < stages - 1:
            d_end = passed_along(d_start, "seq", -H)
            d_after = passed_along(d_before, "seq", -H)
    d_all = d_all.reshape(H, rows, -1)

    layer_out = (residual + total_of(ffn_own, ffn_received)).astype(bf16).reshape(inputs.shape)

    mixer_partial, narrow = mixer_grads_rule(
        head_arg, normed_in, branch, d_all.reshape(all_rows, -1), headed, mixer_w, beta_w
    )
    mixer_partial, ffn_spread = lax.optimization_barrier((mixer_partial, ffn_spread))
    mixer_summed = reduce_weight(mixer_partial)
    ffn_grads = join_hidden_rule(ffn_spread, hidden_all, 3)

    d_even, d_odd = d_in_rule(d_all, mixer_w, beta_w)
    own_sum, sums = pair_sums(d_even, swapped(d_odd, "seq", 1))
    received, mixer_summed, narrow, ffn_grads = lax.optimization_barrier(
        (exchanged(sums), mixer_summed, narrow, ffn_grads)
    )
    mixer_grads = join_rule(spread_grads(mixer_summed), [DK, DK, DV, DV, DV])
    d_normed_in = total_of(own_sum, received)
    d_from_in, _ = rms_back(flat_in, norm_in, d_normed_in)
    grad_input = (d_residual + d_from_in).reshape(inputs.shape)

    small = jnp.concatenate(
        [
            grad_taps[:CONV].reshape(-1),
            narrow[:, 0],
            grad_gain[0],
            grad_mid,
            narrow[:, 1] / norm_in,
        ]
    ).reshape(-1, 128)
    step = 1
    while step < lax.axis_size("wt"):
        small = small + swapped(small, "wt", step)
        step *= 2
    step = H
    while step < peers:
        small = small + swapped(small, "seq", step)
        step *= 2
    small = small[None]
    for bits in (1, 2, 4):
        small = jnp.concatenate([small, swapped(small, "seq", bits)], axis=0)
    small = small[jnp.arange(H) ^ head].reshape(H, -1)
    ends = []
    for bound in (CONV * WIDTH, model, DV, model, model):
        ends.append(bound + (ends[-1] if ends else 0))
    taps_part = small[:, : ends[0]].reshape(H, CONV, WIDTH)

    def joined(pieces):
        return jnp.swapaxes(pieces, 0, 1).reshape(CONV, -1)

    grad_conv = jnp.concatenate(
        [
            joined(taps_part[:, :, :DK]),
            joined(taps_part[:, :, DK : 2 * DK]),
            joined(taps_part[:, :, 2 * DK :]),
        ],
        axis=1,
    )
    grad_beta = small[:, ends[0] : ends[1]].T
    shared = jnp.sum(small[:, ends[1] :], axis=0)
    return (
        layer_out,
        grad_input,
        *mixer_grads,
        *ffn_grads,
        grad_beta,
        grad_conv,
        shared[DV + model :],
        shared[DV : DV + model],
        shared[:DV],
    )


def solution(mesh):
    rows = P("wt", "seq", None)
    cut = P("wt", None)
    in_specs = (rows,) * 3 + (cut,) * 8 + (P(),) * 5
    out_specs = (rows,) * 2 + (cut,) * 8 + (P(),) * 5
    return jax.shard_map(shards, mesh=mesh, in_specs=in_specs, out_specs=out_specs, check_vma=False)
```

```python
import jax
import jax.numpy as jnp
from jax import lax
from jax.experimental import pallas as pl
from jax.experimental.pallas import tpu as pltpu
from jax.sharding import PartitionSpec as P

H = 8
DK = 128
DV = 256
CONV = 4
HALO = 16
WIDTH = 2 * DK + DV
VMEM_LIMIT = 60 * 1024 * 1024
bf16 = jnp.bfloat16
f32 = jnp.float32


def dot(left, right, dims):
    return lax.dot_general(left, right, (dims, ((), ())), preferred_element_type=f32)


def product(left, right):
    return dot(left, right, ((1,), (0,)))


def contract_rows(left, right):
    return dot(left, right, ((0,), (0,)))


def contract_cols(left, right):
    return dot(left, right, ((1,), (1,)))


def parts(values):
    high = values.astype(bf16)
    return high, (values - high.astype(f32)).astype(bf16)


def mul(left, right):
    (lh, ll), (rh, rl) = left, right
    wide = product(jnp.concatenate([lh, ll], 1), jnp.concatenate([rh, rh], 0))
    return wide + product(lh, rl)


def mul_t(left, right):
    (lh, ll), (rh, rl) = left, right
    wide = contract_cols(jnp.concatenate([lh, ll], 1), jnp.concatenate([rh, rh], 1))
    return wide + contract_cols(lh, rl)


def cat_parts(values):
    return jnp.concatenate(parts(values), 1)


def from_cat(both):
    half = both.shape[1] // 2
    return both[:, :half], both[:, half:]


def iotas(size):
    return (
        lax.broadcasted_iota(jnp.int32, (size, size), 0),
        lax.broadcasted_iota(jnp.int32, (size, size), 1),
    )


def unit_inverses(lowers, rows, cols):
    size = rows.shape[0]
    level = 0
    eye = jnp.where(rows == cols, 1.0, 0.0)
    inverses = [eye] * len(lowers)
    while (1 << level) < size:
        together = (rows >> (level + 1)) == (cols >> (level + 1))
        corner = together & (((rows >> level) & 1) == 1) & (((cols >> level) & 1) == 0)
        blocks = [jnp.where(corner, lower, 0.0) for lower in lowers]
        if level == 0:
            inverses = [inverse - block for inverse, block in zip(inverses, blocks)]
        else:
            wholes = [parts(inverse) for inverse in inverses]
            steps = [mul(parts(block), whole) for block, whole in zip(blocks, wholes)]
            steps = [mul(whole, parts(step)) for step, whole in zip(steps, wholes)]
            inverses = [inverse - step for inverse, step in zip(inverses, steps)]
        level += 1
    return inverses


def conv_rows(conv_ref, halo_ref, rows_ref, taps_ref, chunk, seq, slot):
    size = conv_ref.shape[2]
    before = conv_ref[jnp.maximum(chunk - 1, 0), seq, size - HALO :, :]
    before = jnp.where(chunk == 0, halo_ref[seq], before)
    rows_ref[slot, :HALO, :] = before.astype(f32)
    rows_ref[slot, HALO:, :] = conv_ref[chunk, seq].astype(f32)
    total = None
    for tap in range(CONV):
        start = HALO - (CONV - 1) + tap
        term = rows_ref[slot, start : start + size, :] * taps_ref[tap : tap + 1, :]
        total = term if total is None else total + term
    return total


def run_row_of(run_ref, chunk, seq, seqs):
    return run_ref[pl.ds(chunk * seqs + seq, 1), :]


def decays(run_row, rows, cols):
    size = rows.shape[0]
    run_col = jnp.sum(jnp.where(rows == cols, run_row, 0.0), axis=1, keepdims=True)
    spread = jnp.where(rows >= cols, run_col - run_row, 0.0)
    decay_mat = jnp.where(rows >= cols, jnp.exp(spread), 0.0)
    last = run_row[:, size - 1 : size]
    return decay_mat, jnp.exp(run_col), jnp.exp(last - run_col)


def running_sums(values, rows, cols):
    upper = jnp.where(rows <= cols, 1.0, 0.0).astype(bf16)
    total = None
    for _ in range(3):
        part = values.astype(bf16)
        values = values - part.astype(f32)
        term = product(part, upper)
        total = term if total is None else total + term
    return total


def units_of(first, count, seqs):
    return [(first + chunk, seq) for chunk in range(count) for seq in range(seqs)]


FORWARD_CHUNKS = 4


def forward_kernel(head_ref, *refs):
    block_refs, decay_refs, refs = refs[:H], refs[H : 2 * H], refs[2 * H :]
    weight_in, beta_ref, taps_ref, gain_ref, state_ref, halo_ref = refs[:6]
    outs, (run_ref, end_ref), held, refs = refs[6:14], refs[14:16], refs[16:24], refs[24:]
    headed_ref, conv_ref, gate_ref, mixed_ref, inverse_ref, scores_ref, delta_ref, starts_ref = held
    (
        block_ref, weight_ref, log_ref, rows_ref, recall_ref, target_ref, query_ref, write_ref,
        plain_ref, block_sems, weight_sem, out_sems,
    ) = refs
    chunks, seqs, size, _ = conv_ref.shape
    rows, cols = iotas(size)
    head = head_ref[0]

    weight_copy = pltpu.make_async_copy(
        weight_in.at[:, pl.ds(0, WIDTH + DV)], weight_ref, weight_sem
    )
    weight_copy.start()
    def block_copy(source, slot):
        return pltpu.make_async_copy(source, block_ref.at[slot], block_sems.at[slot])

    for slot in range(H):
        block_copy(block_refs[slot], slot).start()
    for slot in range(H):
        logs = jnp.log(decay_refs[slot][pl.ds(head, 1), :])
        for seq in range(seqs):
            log_ref[pl.ds((slot ^ head) * seqs + seq, 1), :] = logs[:, seq * size : (seq + 1) * size]
    run_ref[...] = running_sums(log_ref[...], rows, cols)

    weight_copy.wait()

    def project(slot, _):
        chunk = slot ^ head
        block_copy(block_refs[0], slot).wait()
        block = block_ref[slot]
        conv = product(block, weight_ref[:, :WIDTH]).astype(bf16)
        gate = product(block, weight_ref[:, WIDTH:])
        beta = product(block, beta_ref[...])
        for seq in range(seqs):
            span = slice(seq * size, (seq + 1) * size)
            conv_ref[chunk, seq] = conv[span]
            gate_ref[chunk, seq, :, :DV] = gate[span]
            gate_ref[chunk, seq, :, DV:] = beta[span]
        return 0

    lax.fori_loop(0, H, project, 0)

    def send(index, first, count):
        span = pl.ds(first, count)
        pltpu.make_async_copy(
            held[index].at[span], outs[index].at[span], out_sems.at[index]
        ).start()

    def prepare(turn, _):
        units = units_of(turn * FORWARD_CHUNKS, FORWARD_CHUNKS, seqs)
        lowers = []

        @pl.when(turn > 0)
        def _():
            for index in (1, 2, 4, 5):
                send(index, (turn - 1) * FORWARD_CHUNKS, FORWARD_CHUNKS)

        for slot, (chunk, seq) in enumerate(units):
            summed = conv_rows(conv_ref, halo_ref, rows_ref, taps_ref, chunk, seq, slot)
            active = summed * jax.nn.sigmoid(summed)
            query = active[:, :DK]
            key = active[:, DK : 2 * DK]
            key = key * lax.rsqrt(jnp.sum(key * key, axis=1, keepdims=True) + 1e-06)
            beta = jax.nn.sigmoid(gate_ref[chunk, seq, :, DV : DV + 1])
            decay_mat, growth, fade = decays(run_row_of(run_ref, chunk, seq, seqs), rows, cols)
            target_ref[chunk, seq] = beta * active[:, 2 * DK :]
            query_ref[chunk, seq] = cat_parts(growth * query)
            write_ref[chunk, seq] = cat_parts((fade * key).T)
            recall_ref[chunk, seq] = cat_parts(beta * growth * key)
            key_parts = parts(key)
            gram = mul_t(key_parts, key_parts)
            lowers.append(jnp.where(rows > cols, beta * gram * decay_mat, 0.0))
            scores = mul_t(parts(query), key_parts) * decay_mat
            plain_ref[chunk, seq] = cat_parts(scores)
            scores_ref[chunk, seq] = cat_parts(scores.T)
        inverses = unit_inverses(lowers, rows, cols)
        for (chunk, seq), inverse in zip(units, inverses):
            inverse_parts = parts(inverse)
            recall = mul(inverse_parts, from_cat(recall_ref[chunk, seq]))
            recall_ref[chunk, seq] = cat_parts(recall)
            target_ref[chunk, seq] = mul(inverse_parts, parts(target_ref[chunk, seq]))
            inverse_ref[chunk, seq] = cat_parts(inverse.T)
        return 0

    lax.fori_loop(0, chunks // FORWARD_CHUNKS, prepare, 0)

    def advance(chunk, states):
        following = []

        @pl.when(chunk == 0)
        def _():
            for index in (1, 2, 4, 5):
                send(index, chunks - FORWARD_CHUNKS, FORWARD_CHUNKS)

        @pl.when(chunk > 0)
        def _():
            for index in (0, 3, 6, 7):
                send(index, chunk - 1, 1)

        for seq in range(seqs):
            state = states[seq]
            starts_ref[chunk, seq] = state
            state_parts = parts(state)
            delta = target_ref[chunk, seq] - mul(from_cat(recall_ref[chunk, seq]), state_parts)
            delta_parts = parts(delta)
            total = jnp.exp(run_row_of(run_ref, chunk, seq, seqs)[:, size - 1 : size])
            following.append(
                total * state + mul(from_cat(write_ref[chunk, seq]), delta_parts)
            )
            delta_ref[chunk, seq] = delta
            read = mul(from_cat(query_ref[chunk, seq]), state_parts)
            read = read + mul(from_cat(plain_ref[chunk, seq]), delta_parts)
            mixed_ref[chunk, seq] = read
            scale = lax.rsqrt(jnp.mean(read * read, axis=1, keepdims=True) + 1e-05)
            gate = gate_ref[chunk, seq, :, :DV]
            headed = read * scale * gain_ref[...] * (gate * jax.nn.sigmoid(gate))
            headed_ref[chunk, seq] = headed.astype(bf16)
        return tuple(following)

    final = lax.fori_loop(0, chunks, advance, tuple(state_ref[seq] for seq in range(seqs)))
    for seq in range(seqs):
        end_ref[seq] = final[seq]
    for index in (0, 3, 6, 7):
        send(index, chunks - 1, 1)
    for index in range(len(held)):
        pltpu.make_async_copy(held[index], outs[index], out_sems.at[index]).wait()


BACKWARD_CHUNKS = 2


def backward_kernel(head_ref, *refs):
    branch_refs, weight_in, refs = refs[:H], refs[H], refs[H + 1 :]
    saved, refs = refs[:7], refs[7:]
    run_ref, taps_ref, gain_ref, halo_ref, d_end_ref, d_after_ref = refs[:6]
    d_all_out, grad_taps_ref, grad_gain_ref, d_start_ref, d_before_ref = refs[6:11]
    branch_ref, weight_ref, held, refs = refs[11], refs[12], refs[13:20], refs[20:]
    conv_ref, gate_ref, mixed_ref, inverse_ref, scores_ref, delta_ref, starts_ref = held
    (
        rows_ref, d_headed_ref, hold_ref, carry_ref, base_ref, back_ref, d_target_ref, d_state_ref,
        d_conv_ref, d_all_ref, slope_ref, active_ref, column_ref,
        block_sems, weight_sem, saved_sems, out_sem,
    ) = refs
    chunks, seqs, size, _ = conv_ref.shape
    rows, cols = iotas(size)
    head = head_ref[0]

    weight_copy = pltpu.make_async_copy(
        weight_in.at[:, pl.ds(WIDTH + DV, DV)], weight_ref, weight_sem
    )
    weight_copy.start()

    def block_copy(source, slot):
        return pltpu.make_async_copy(source, branch_ref.at[slot], block_sems.at[slot])

    for slot in range(H):
        block_copy(branch_refs[slot], slot).start()
    saved_copies = [
        pltpu.make_async_copy(saved[index], held[index], saved_sems.at[index])
        for index in range(len(saved))
    ]

    lane = lax.broadcasted_iota(jnp.int32, (size, 128), 1)
    grad_gain_ref[...] = jnp.zeros_like(grad_gain_ref)
    grad_taps_ref[...] = jnp.zeros_like(grad_taps_ref)

    weight_copy.wait()

    def project(slot, _):
        @pl.when(slot == 1)
        def _():
            for copy in saved_copies[:5]:
                copy.start()

        block_copy(branch_refs[0], slot).wait()
        d_headed = product(branch_ref[slot], weight_ref[...])
        for seq in range(seqs):
            d_headed_ref[slot ^ head, seq] = d_headed[seq * size : (seq + 1) * size]
        return 0

    lax.fori_loop(0, H, project, 0)
    for copy in saved_copies[:5]:
        copy.wait()
    for copy in saved_copies[5:]:
        copy.start()

    def prepare(turn, _):
        units = units_of(turn * BACKWARD_CHUNKS, BACKWARD_CHUNKS, seqs)
        for chunk, seq in units:
            unit = chunk * seqs + seq
            summed = conv_rows(conv_ref, halo_ref, rows_ref, taps_ref, chunk, seq, unit)
            logistic = jax.nn.sigmoid(summed)
            active = summed * logistic
            slope_ref[unit] = logistic * (1.0 + summed * (1.0 - logistic))
            query = active[:, :DK]
            raw = active[:, DK : 2 * DK]
            shrink = lax.rsqrt(jnp.sum(raw * raw, axis=1, keepdims=True) + 1e-06)
            key = raw * shrink
            active_ref[unit, :, :DK] = query
            active_ref[unit, :, DK : 2 * DK] = key
            active_ref[unit, :, 2 * DK :] = active[:, 2 * DK :]
            beta = jax.nn.sigmoid(gate_ref[chunk, seq, :, DV : DV + 1])
            column_ref[unit] = jnp.where(lane == 0, shrink, beta)
            _, growth, fade = decays(run_row_of(run_ref, chunk, seq, seqs), rows, cols)
            mixed = mixed_ref[chunk, seq]
            d_headed = d_headed_ref[chunk, seq]
            gate = gate_ref[chunk, seq, :, :DV]
            logistic = jax.nn.sigmoid(gate)
            scale = lax.rsqrt(jnp.mean(mixed * mixed, axis=1, keepdims=True) + 1e-05)
            normed = mixed * scale
            swish = gate * logistic
            inner = d_headed * gain_ref[...] * swish
            d_mixed = scale * (inner - normed * jnp.mean(normed * inner, axis=1, keepdims=True))
            grad_gain_ref[...] += jnp.sum(d_headed * normed * swish, axis=0, keepdims=True)
            d_gate = d_headed * gain_ref[...] * normed * logistic * (1.0 + gate * (1.0 - logistic))
            d_all_ref[chunk ^ head, seq, :, WIDTH : WIDTH + DV] = d_gate.astype(bf16)
            d_headed_ref[chunk, seq] = d_mixed
            d_mixed_parts = parts(d_mixed)
            inverse_parts = from_cat(inverse_ref[chunk, seq])
            scored = mul(from_cat(scores_ref[chunk, seq]), d_mixed_parts)
            base_ref[chunk, seq] = mul(inverse_parts, parts(scored))
            hold_ref[chunk, seq] = cat_parts(mul(inverse_parts, parts(fade * key)))
            back_ref[chunk, seq] = mul(parts((growth * query).T), d_mixed_parts)
            carry_ref[chunk, seq] = cat_parts((beta * growth * key).T)
        return 0

    lax.fori_loop(0, chunks // BACKWARD_CHUNKS, prepare, 0)

    def advance(step, d_states):
        chunk = chunks - 1 - step
        following = []
        for seq in range(seqs):
            d_state = d_states[seq]
            d_state_ref[chunk, seq] = d_state
            d_target = base_ref[chunk, seq] + mul(from_cat(hold_ref[chunk, seq]), parts(d_state))
            d_target_ref[chunk, seq] = d_target
            total = jnp.exp(run_row_of(run_ref, chunk, seq, seqs)[:, size - 1 : size])
            back = mul(from_cat(carry_ref[chunk, seq]), parts(d_target))
            following.append(total * d_state + back_ref[chunk, seq] - back)
        return tuple(following)

    first = lax.fori_loop(0, chunks, advance, tuple(d_end_ref[seq] for seq in range(seqs)))
    for seq in range(seqs):
        d_start_ref[seq] = first[seq]
        d_conv_ref[seq, size:, :] = d_after_ref[seq]
    for copy in saved_copies[5:]:
        copy.wait()

    def send(chunk):
        slot = chunk ^ head
        pltpu.make_async_copy(d_all_ref.at[slot], d_all_out.at[slot], out_sem).start()

    def finish(turn, _):
        units = [
            (chunks - 1 - turn * BACKWARD_CHUNKS - back, seq)
            for back in range(BACKWARD_CHUNKS)
            for seq in range(seqs)
        ]

        @pl.when(turn > 0)
        def _():
            for back in range(BACKWARD_CHUNKS):
                send(chunks - 1 - (turn - 1) * BACKWARD_CHUNKS - back)

        for chunk, seq in units:
            unit = chunk * seqs + seq
            slope = slope_ref[unit]
            query = active_ref[unit, :, :DK]
            key = active_ref[unit, :, DK : 2 * DK]
            value = active_ref[unit, :, 2 * DK :]
            shrink = column_ref[unit, :, 0:1]
            beta = column_ref[unit, :, 1:2]
            decay_mat, growth, fade = decays(run_row_of(run_ref, chunk, seq, seqs), rows, cols)
            key_parts = parts(key)
            gram = mul_t(key_parts, key_parts) * decay_mat
            d_target = d_target_ref[chunk, seq]
            delta_parts = parts(delta_ref[chunk, seq])
            start_parts = parts(starts_ref[chunk, seq])
            both = parts(jnp.concatenate([d_target, d_headed_ref[chunk, seq]], 0))
            on_delta = mul_t(both, delta_parts)
            on_state = mul_t(both, start_parts)
            d_lower = jnp.where(rows > cols, -on_delta[:size], 0.0)
            d_scores = on_delta[size:] * decay_mat
            through = on_state[:size]
            d_gram = d_lower * decay_mat * beta
            d_query = growth * on_state[size:] + mul(parts(d_scores), key_parts)
            d_key = mul(parts(d_scores.T), parts(query))
            d_key = d_key + mul(parts(d_gram + d_gram.T), key_parts)
            d_key = d_key + fade * mul_t(delta_parts, parts(d_state_ref[chunk, seq]))
            d_key = d_key - (beta * growth) * through
            d_beta = (
                jnp.sum(d_target * value, axis=1, keepdims=True)
                - growth * jnp.sum(key * through, axis=1, keepdims=True)
                + jnp.sum(d_lower * gram, axis=1, keepdims=True)
            )
            d_raw = shrink * (d_key - key * jnp.sum(key * d_key, axis=1, keepdims=True))
            d_conv = jnp.concatenate([d_query, d_raw, beta * d_target], 1) * slope
            d_conv_ref[seq, :size, :] = d_conv
            d_in = None
            for tap in range(CONV):
                start = HALO - (CONV - 1) + tap
                grad_taps_ref[tap : tap + 1, :] += jnp.sum(
                    d_conv * rows_ref[unit, start : start + size, :], axis=0, keepdims=True
                )
                shift = CONV - 1 - tap
                term = d_conv_ref[seq, shift : shift + size, :] * taps_ref[tap : tap + 1, :]
                d_in = term if d_in is None else d_in + term
            d_conv_ref[seq, size:, :] = d_conv[:8, :]
            d_all_ref[chunk ^ head, seq, :, :WIDTH] = d_in.astype(bf16)
            d_logit = d_beta * beta * (1.0 - beta)
            d_all_ref[chunk ^ head, seq, :, WIDTH + DV :] = jnp.where(
                lane == 0, d_logit, 0.0
            ).astype(bf16)
        return 0

    lax.fori_loop(0, chunks // BACKWARD_CHUNKS, finish, 0)
    for seq in range(seqs):
        d_before_ref[seq] = d_conv_ref[seq, size:, :]
    for chunk in range(BACKWARD_CHUNKS):
        send(chunk)
    pltpu.make_async_copy(d_all_ref, d_all_out, out_sem).wait()


def whole(count):
    return [pl.BlockSpec(memory_space=pltpu.VMEM)] * count


def scalar():
    return [pl.BlockSpec(memory_space=pltpu.SMEM)]


shaped = jax.ShapeDtypeStruct


def cost(flops):
    return pl.CostEstimate(flops=flops, bytes_accessed=0, transcendentals=0)


def kernel_params():
    return pltpu.CompilerParams(vmem_limit_bytes=VMEM_LIMIT)


def anywhere(count):
    return [pl.BlockSpec(memory_space=pltpu.HBM)] * count


def forward_rule(head, blocks, decay_blocks, weight, beta_w, taps, gain, state, halo):
    rows, model = blocks[0].shape
    seqs = state.shape[0]
    size = rows // seqs
    lead = (H, seqs)
    held = [
        (lead + (size, DV), bf16),
        (lead + (size, WIDTH), bf16),
        (lead + (size, DV + 128), f32),
        (lead + (size, DV), f32),
        (lead + (size, 2 * size), bf16),
        (lead + (size, 2 * size), bf16),
        (lead + (size, DV), f32),
        (lead + (DK, DV), f32),
    ]
    return pl.pallas_call(
        forward_kernel,
        name="mixer_forward",
        out_shape=[shaped(*item) for item in held]
        + [shaped((H * seqs, size), f32), shaped((seqs, DK, DV), f32)],
        in_specs=scalar() + anywhere(H) + whole(H) + anywhere(1) + whole(5),
        out_specs=anywhere(8) + whole(2),
        scratch_shapes=[pltpu.VMEM(*item) for item in held]
        + [
            pltpu.VMEM((H, rows, model), bf16),
            pltpu.VMEM((model, WIDTH + DV), bf16),
            pltpu.VMEM((H * seqs, size), f32),
            pltpu.VMEM((FORWARD_CHUNKS * seqs, HALO + size, WIDTH), f32),
            pltpu.VMEM(lead + (size, 2 * DK), bf16),
            pltpu.VMEM(lead + (size, DV), f32),
            pltpu.VMEM(lead + (size, 2 * DK), bf16),
            pltpu.VMEM(lead + (DK, 2 * size), bf16),
            pltpu.VMEM(lead + (size, 2 * size), bf16),
            pltpu.SemaphoreType.DMA((H,)),
            pltpu.SemaphoreType.DMA,
            pltpu.SemaphoreType.DMA((8,)),
        ],
        compiler_params=kernel_params(),
    )(head, *blocks, *decay_blocks, weight, beta_w, taps, gain, state, halo)


def backward_rule(head, branch, weight, saved, run, taps, gain, halo, d_end, d_after):
    rows, model = branch[0].shape
    seqs = d_end.shape[0]
    size = rows // seqs
    lead = (H, seqs)
    return pl.pallas_call(
        backward_kernel,
        name="mixer_backward",
        out_shape=(
            shaped(lead + (size, WIDTH + DV + 128), bf16),
            shaped((8, WIDTH), f32),
            shaped((1, DV), f32),
            shaped((seqs, DK, DV), f32),
            shaped((seqs, 8, WIDTH), f32),
        ),
        in_specs=scalar() + anywhere(H + 8) + whole(6),
        out_specs=tuple(anywhere(1) + whole(4)),
        scratch_shapes=[
            pltpu.VMEM((H, rows, model), bf16),
            pltpu.VMEM((model, DV), bf16),
        ]
        + [pltpu.VMEM(item.shape, item.dtype) for item in saved]
        + [
            pltpu.VMEM((H * seqs, HALO + size, WIDTH), f32),
            pltpu.VMEM(lead + (size, DV), f32),
            pltpu.VMEM(lead + (size, 2 * DK), bf16),
            pltpu.VMEM(lead + (DK, 2 * size), bf16),
            pltpu.VMEM(lead + (size, DV), f32),
            pltpu.VMEM(lead + (DK, DV), f32),
            pltpu.VMEM(lead + (size, DV), f32),
            pltpu.VMEM(lead + (DK, DV), f32),
            pltpu.VMEM((seqs, size + 8, WIDTH), f32),
            pltpu.VMEM(lead + (size, WIDTH + DV + 128), bf16),
            pltpu.VMEM((H * seqs, size, WIDTH), f32),
            pltpu.VMEM((H * seqs, size, WIDTH), f32),
            pltpu.VMEM((H * seqs, size, 128), f32),
            pltpu.SemaphoreType.DMA((H,)),
            pltpu.SemaphoreType.DMA,
            pltpu.SemaphoreType.DMA((7,)),
            pltpu.SemaphoreType.DMA,
        ],
        compiler_params=kernel_params(),
    )(head, *branch, weight, *saved, run, taps, gain, halo, d_end, d_after)


def out_kernel(head_ref, *refs):
    block_refs, refs = refs[:H], refs[H:]
    headed_ref, inputs_ref, gain_ref, residual_ref, normed_ref, weight_ref, sems = refs
    head = head_ref[0]

    def block_copy(source, slot):
        return pltpu.make_async_copy(source, weight_ref.at[slot], sems.at[slot])

    for slot in range(H):
        block_copy(block_refs[slot], slot).start()
    residual_ref[...] = inputs_ref[...].astype(f32)

    def add_heads(pair, _):
        slots = (2 * pair, 2 * pair + 1)
        for slot in slots:
            block_copy(block_refs[0], slot).wait()
        headed = jnp.concatenate([headed_ref[slot ^ head] for slot in slots], 1)
        weight = jnp.concatenate([weight_ref[slot] for slot in slots], 1)
        residual_ref[...] += contract_cols(headed, weight)
        return 0

    lax.fori_loop(0, H // 2, add_heads, 0)
    total = residual_ref[...]
    scale = lax.rsqrt(jnp.mean(total * total, axis=1, keepdims=True) + 1e-05)
    normed_ref[...] = (total * scale * gain_ref[...]).astype(bf16)


def out_rule(head, blocks, headed, inputs, gain):
    return pl.pallas_call(
        out_kernel,
        name="out_projection",
        out_shape=(shaped(inputs.shape, f32), shaped(inputs.shape, bf16)),
        in_specs=scalar() + anywhere(H) + whole(3),
        out_specs=tuple(whole(2)),
        scratch_shapes=[
            pltpu.VMEM((H,) + blocks[0].shape, bf16),
            pltpu.SemaphoreType.DMA((H,)),
        ],
        compiler_params=kernel_params(),
    )(head, *blocks, headed, inputs, gain)


PART = H // 2


def ffn_kernel(*refs):
    normed_refs, up_refs, refs = refs[:PART], refs[PART : 2 * PART], refs[2 * PART :]
    weight_in, d_both_ref, hidden_ref, d_even_ref, d_odd_ref, even_ref, odd_ref = refs[:7]
    normed_all_ref, up_all_ref, weight_ref, normed_sems, up_sems, weight_sem = refs[7:]
    share = weight_ref.shape[1] // 3
    step = pl.program_id(0)

    def copy_of(source, target, sems, slot):
        return pltpu.make_async_copy(source, target.at[slot], sems.at[slot])

    def start_slot(slot):
        copy_of(normed_refs[slot], normed_all_ref, normed_sems, slot).start()
        copy_of(up_refs[slot], up_all_ref, up_sems, slot).start()

    @pl.when(step == 0)
    def _():
        weight_copy = pltpu.make_async_copy(weight_in, weight_ref, weight_sem)
        weight_copy.start()
        start_slot(0)
        weight_copy.wait()

    for later in range(1, PART):

        @pl.when(step == later - 1)
        def _():
            start_slot(later)

    slot = step
    copy_of(normed_refs[0], normed_all_ref, normed_sems, slot).wait()
    copy_of(up_refs[0], up_all_ref, up_sems, slot).wait()
    both = product(normed_all_ref[slot], weight_ref[:, : 2 * share])
    d_hidden = product(up_all_ref[slot], weight_ref[:, 2 * share :])
    gate, up = both[:, :share], both[:, share:]
    logistic = jax.nn.sigmoid(gate)
    swish = gate * logistic
    hidden = (swish * up).astype(bf16)
    hidden_ref[0] = hidden
    d_gate = (d_hidden * up * logistic * (1.0 + gate * (1.0 - logistic))).astype(bf16)
    d_up = (d_hidden * swish).astype(bf16)
    d_both = jnp.concatenate([d_gate, d_up], 1)
    d_both_ref[0] = d_both
    d_in = contract_cols(d_both, weight_ref[:, : 2 * share]).astype(bf16)
    out = contract_cols(hidden, weight_ref[:, 2 * share :]).astype(bf16)
    for side, d_in_ref, out_ref in ((0, d_even_ref, even_ref), (1, d_odd_ref, odd_ref)):

        @pl.when(step % 2 == side)
        def _():
            d_in_ref[0] = d_in
            out_ref[0] = out


def ffn_rule(normed, upstream, weight):
    rows, model = normed[0].shape
    share = weight.shape[1] // 3

    def moving(width, steps):
        return pl.BlockSpec((1, rows, width), lambda step: (step // steps, 0, 0))

    return pl.pallas_call(
        ffn_kernel,
        name="feed_forward",
        grid=(PART,),
        in_specs=anywhere(2 * PART + 1),
        out_specs=[moving(2 * share, 1), moving(share, 1)] + [moving(model, 2)] * 4,
        out_shape=[shaped((PART, rows, 2 * share), bf16), shaped((PART, rows, share), bf16)]
        + [shaped((PART // 2, rows, model), bf16)] * 4,
        scratch_shapes=[pltpu.VMEM((PART, rows, model), bf16)] * 2
        + [
            pltpu.VMEM(weight.shape, bf16),
            pltpu.SemaphoreType.DMA((PART,)),
            pltpu.SemaphoreType.DMA((PART,)),
            pltpu.SemaphoreType.DMA,
        ],
        compiler_params=kernel_params(),
    )(*normed, *upstream, weight)


GRAD_TILE = 256


def ffn_grads_kernel(*refs):
    normed_refs, up_refs, refs = refs[:H], refs[H : 2 * H], refs[2 * H :]
    both_refs, hidden_refs, out_ref = refs[:2], refs[2:4], refs[4]
    wide = both_refs[0].shape[1]
    normed = jnp.concatenate([ref[...] for ref in normed_refs], 0)
    d_both = jnp.concatenate([ref[...] for ref in both_refs], 0)
    out_ref[:, :wide] = contract_rows(normed, d_both).astype(bf16)
    upstream = jnp.concatenate([ref[...] for ref in up_refs], 0)
    hidden = jnp.concatenate([ref[...] for ref in hidden_refs], 0)
    out_ref[:, wide:] = contract_rows(upstream, hidden).astype(bf16)


def ffn_grads_rule(normed, upstream, d_both, hidden):
    rows, model = normed[0].shape
    d_both = [part.reshape(PART * rows, -1) for part in d_both]
    hidden = [part.reshape(PART * rows, -1) for part in hidden]
    width = d_both[0].shape[1] + hidden[0].shape[1]
    columns = pl.BlockSpec((rows, GRAD_TILE), lambda step: (0, step))
    return pl.pallas_call(
        ffn_grads_kernel,
        name="feed_forward_grads",
        grid=(model // GRAD_TILE,),
        in_specs=[columns] * (2 * H)
        + [pl.BlockSpec(part.shape, lambda step: (0, 0)) for part in (*d_both, *hidden)],
        out_specs=pl.BlockSpec((GRAD_TILE, width), lambda step: (step, 0)),
        out_shape=shaped((model, width), bf16),
        compiler_params=kernel_params(),
    )(*normed, *upstream, *d_both, *hidden)


def mixer_grads_kernel(head_ref, *refs):
    normed_refs, branch_refs, refs = refs[:H], refs[H : 2 * H], refs[2 * H :]
    d_all_ref, headed_ref, weight_ref, beta_ref, out_ref, small_ref = refs
    head = head_ref[0]
    width = WIDTH + DV
    normed = jnp.concatenate([ref[...] for ref in normed_refs], 0)
    partial = contract_rows(normed, d_all_ref[:, :width])
    out_ref[:, :width] = partial.astype(bf16)
    beta = contract_rows(normed, d_all_ref[:, width:])
    branch = jnp.concatenate([ref[...] for ref in branch_refs], 0)
    headed = jnp.concatenate([headed_ref[slot ^ head] for slot in range(H)], 0)
    out_ref[:, width:] = contract_rows(branch, headed).astype(bf16)
    weighed = jnp.sum(partial * weight_ref[:, :width].astype(f32), axis=1, keepdims=True)
    weighed = weighed + beta[:, :1] * beta_ref[:, :1].astype(f32)
    lane = lax.broadcasted_iota(jnp.int32, beta.shape, 1)
    small_ref[...] = jnp.where(lane == 0, beta, jnp.where(lane == 1, weighed, 0.0))


def mixer_grads_rule(head, normed, branch, d_all, headed, weight, beta_w):
    rows, model = branch[0].shape
    width = WIDTH + 2 * DV
    columns = pl.BlockSpec((rows, GRAD_TILE), lambda step: (0, step))
    return pl.pallas_call(
        mixer_grads_kernel,
        name="mixer_grads",
        grid=(model // GRAD_TILE,),
        in_specs=scalar()
        + [columns] * (2 * H)
        + [
            pl.BlockSpec(d_all.shape, lambda step: (0, 0)),
            pl.BlockSpec(headed.shape, lambda step: (0, 0, 0)),
            pl.BlockSpec((GRAD_TILE, width), lambda step: (step, 0)),
            pl.BlockSpec((GRAD_TILE, 128), lambda step: (step, 0)),
        ],
        out_specs=[
            pl.BlockSpec((GRAD_TILE, width), lambda step: (step, 0)),
            pl.BlockSpec((GRAD_TILE, 128), lambda step: (step, 0)),
        ],
        out_shape=[shaped((model, width), bf16), shaped((model, 128), f32)],
        compiler_params=kernel_params(),
    )(head, *normed, *branch, d_all, headed, weight, beta_w)


def d_in_kernel(d_all_ref, weight_ref, beta_ref, even_ref, odd_ref):
    width = WIDTH + DV
    total = contract_cols(d_all_ref[0, :, :width], weight_ref[:, :width])
    total = (total + contract_cols(d_all_ref[0, :, width:], beta_ref[...])).astype(bf16)
    for side, out_ref in ((0, even_ref), (1, odd_ref)):

        @pl.when(pl.program_id(0) % 2 == side)
        def _():
            out_ref[0] = total


def d_in_rule(d_all, weight, beta_w):
    _, rows, width = d_all.shape
    model = weight.shape[0]
    out = pl.BlockSpec((1, rows, model), lambda step: (step // 2, 0, 0))
    return pl.pallas_call(
        d_in_kernel,
        name="mixer_d_in",
        grid=(H,),
        in_specs=[
            pl.BlockSpec((1, rows, width), lambda step: (step, 0, 0)),
            pl.BlockSpec(weight.shape, lambda step: (0, 0)),
            pl.BlockSpec(beta_w.shape, lambda step: (0, 0)),
        ],
        out_specs=[out, out],
        out_shape=[shaped((H // 2, rows, model), bf16)] * 2,
        compiler_params=kernel_params(),
    )(d_all, weight, beta_w)


JOIN_ROWS = 32


def join_kernel(spread_ref, *out_refs):
    start = 0
    for out_ref in out_refs:
        width = out_ref.shape[1] // H
        for peer in range(H):
            piece = spread_ref[peer, :, start : start + width]
            out_ref[:, peer * width : (peer + 1) * width] = piece.astype(f32)
        start += width


def join_rule(spread, widths):
    count, rows, width = spread.shape
    return pl.pallas_call(
        join_kernel,
        name="join_heads",
        grid=(rows // JOIN_ROWS,),
        in_specs=[pl.BlockSpec((count, JOIN_ROWS, width), lambda step: (0, step, 0))],
        out_specs=[pl.BlockSpec((JOIN_ROWS, count * width), lambda step: (step, 0)) for width in widths],
        out_shape=[shaped((rows, count * width), f32) for width in widths],
        compiler_params=kernel_params(),
    )(spread)


def join_hidden_kernel(spread_ref, *out_refs):
    count, _, width = spread_ref.shape
    share = width // len(out_refs)
    total = out_refs[0].shape[1]
    for index, out_ref in enumerate(out_refs):
        for peer in range(count):
            first = peer * share
            skip = first - min(first, total - share)
            piece = spread_ref[peer, :, index * share + skip : (index + 1) * share]
            out_ref[:, first : first + share - skip] = piece.astype(f32)


def join_hidden_rule(spread, total, pieces):
    count, rows, width = spread.shape
    return pl.pallas_call(
        join_hidden_kernel,
        name="join_hidden",
        grid=(rows // JOIN_ROWS,),
        in_specs=[pl.BlockSpec((count, JOIN_ROWS, width), lambda step: (0, step, 0))],
        out_specs=[pl.BlockSpec((JOIN_ROWS, total), lambda step: (step, 0))] * pieces,
        out_shape=[shaped((rows, total), f32)] * pieces,
        compiler_params=kernel_params(),
    )(spread)


def passed_along(array, axis, by):
    peers = lax.axis_size(axis)
    pairs = [(i, i + by) for i in range(peers) if 0 <= i + by < peers]
    return lax.ppermute(array, axis, pairs)


def swapped(array, axis, bits):
    return lax.ppermute(array, axis, [(i, i ^ bits) for i in range(lax.axis_size(axis))])


def neighbours(own):
    return [own] + [swapped(own, "seq", bits) for bits in range(2, H, 2)]


def with_siblings(blocks):
    return [each for block in blocks for each in (block, swapped(block, "seq", 1))]


def gather_blocks(own):
    return with_siblings(neighbours(own))


def pair_sums(even, handed):
    sums = [even[i].astype(f32) + handed[i].astype(f32) for i in range(even.shape[0])]
    return sums[0], [each.astype(bf16) for each in sums[1:]]


def exchanged(sums):
    return [swapped(sums[i - 1], "seq", 2 * i) for i in range(1, H // 2)]


def total_of(own, received):
    for piece in received:
        own = own + piece.astype(f32)
    return own


def rms_scale(values):
    return lax.rsqrt(jnp.mean(values * values, axis=-1, keepdims=True) + 1e-05)


def rms_back(values, gain, d_normed):
    scale = rms_scale(values)
    normed = values * scale
    pulled = d_normed * gain
    d_values = scale * (pulled - normed * jnp.mean(normed * pulled, axis=-1, keepdims=True))
    return d_values, jnp.sum(d_normed * normed, axis=0)


def shards(
    inputs,
    cotangent,
    decay,
    w_query,
    w_key,
    w_value,
    w_gate_out,
    w_out,
    w_ffn_gate,
    w_ffn_up,
    w_ffn_down,
    w_beta,
    conv_weight,
    norm_in,
    norm_mid,
    norm_head,
):
    seqs, size, model = inputs.shape
    rows = seqs * size
    peers = lax.axis_size("seq")
    stages = peers // H
    groups = None
    if stages > 1:
        groups = [[stage * H + head for head in range(H)] for stage in range(stages)]
    place = lax.axis_index("seq")
    head = lax.rem(place, H)
    head_arg = head.reshape(1)
    all_rows = H * rows
    hidden_all = w_ffn_gate.shape[1]
    share = -(-hidden_all // (H * 128)) * 128

    def gather_rows(local):
        return lax.all_gather(local, "seq", axis_index_groups=groups)

    def own_columns(weight, width):
        return lax.dynamic_slice_in_dim(weight, head * width, width, axis=1)

    def own_hidden(weight):
        start = jnp.minimum(head * share, hidden_all - share)
        piece = lax.dynamic_slice_in_dim(weight, start, share, axis=1)
        lane = lax.broadcasted_iota(jnp.int32, piece.shape, 1)
        return jnp.where(lane + start >= head * share, piece, jnp.zeros_like(piece))

    def gather_weight(local):
        return lax.all_gather(local, "wt", axis=0, tiled=True)

    mixer_w = gather_weight(
        jnp.concatenate(
            [
                own_columns(w_query, DK),
                own_columns(w_key, DK),
                own_columns(w_value, DV),
                own_columns(w_gate_out, DV),
                own_columns(w_out, DV),
            ],
            axis=1,
        )
    )
    ffn_w_own = jnp.concatenate(
        [own_hidden(w_ffn_gate), own_hidden(w_ffn_up), own_hidden(w_ffn_down)], axis=1
    )

    def reduce_weight(partial):
        return lax.psum_scatter(partial, "wt", scatter_dimension=0, tiled=True)

    def spread_grads(summed):
        spread = lax.all_gather(summed, "seq")
        if stages > 1:
            spread = spread.reshape((stages, H) + summed.shape).astype(f32)
            spread = jnp.sum(spread, axis=0)
        return spread

    own_in = inputs.reshape(rows, model)
    flat_in = own_in.astype(f32)
    normed_own = (flat_in * rms_scale(flat_in) * norm_in).astype(bf16)
    upstream_own = cotangent.reshape(rows, model)
    decay_rows = decay.reshape(rows, H).T
    near_in = neighbours(normed_own)
    near_in, late_upstream, ffn_w_own = lax.optimization_barrier(
        (near_in, upstream_own, ffn_w_own)
    )
    up_near = neighbours(late_upstream)
    decay_rows, up_sides = lax.optimization_barrier((decay_rows, up_near[:3]))
    up_near = up_sides + up_near[3:]
    taps = jnp.concatenate(
        [
            own_columns(conv_weight[:, : H * DK], DK),
            own_columns(conv_weight[:, H * DK : 2 * H * DK], DK),
            own_columns(conv_weight[:, 2 * H * DK :], DV),
        ],
        axis=1,
    )
    taps = jnp.pad(taps, ((0, 8 - CONV), (0, 0)))
    beta_w = jnp.pad(own_columns(w_beta, 1), ((0, 0), (0, 127)))
    decay_rows, taps, beta_w = lax.optimization_barrier((decay_rows, taps, beta_w))
    normed_in, decay_blocks, mixer_w = lax.optimization_barrier(
        (with_siblings(near_in), gather_blocks(decay_rows), mixer_w)
    )
    ffn_w = gather_weight(ffn_w_own)
    in_width = WIDTH + DV
    out_near = neighbours(mixer_w[:, in_width:])

    gain = norm_head[None, :]

    state = jnp.zeros((seqs, DK, DV), f32)
    halo = jnp.zeros((seqs, HALO, WIDTH), bf16)
    if stages > 1:
        edges = lax.all_gather(normed_own.reshape(seqs, size, model)[:, size - HALO :], "seq")
        before = lax.dynamic_index_in_dim(edges, jnp.maximum(place - head - 1, 0), keepdims=False)
        rolled = product(before.reshape(seqs * HALO, model), mixer_w[:, :WIDTH]).astype(bf16)
        halo = jnp.where(place >= H, rolled.reshape(halo.shape), halo)
    for stage in range(stages):
        headed, *saved, ending = forward_rule(
            head_arg, normed_in, decay_blocks, mixer_w, beta_w, taps, gain, state, halo
        )
        run = saved.pop()
        if stage < stages - 1:
            state = passed_along(ending, "seq", H)

    headed = headed.reshape(H, rows, DV)
    headed, up_near, out_near = lax.optimization_barrier((headed, up_near, out_near))
    upstream = with_siblings(up_near)
    own_headed = lax.all_to_all(headed, "seq", 0, 0, axis_index_groups=groups, tiled=True)
    residual, normed_own = out_rule(
        head_arg, with_siblings(out_near), own_headed, own_in, norm_mid[None, :]
    )
    across = swapped(normed_own, "seq", 6)
    near, far = swapped(normed_own, "seq", 2), swapped(normed_own, "seq", 4)
    mid_first = with_siblings([normed_own, across])
    up_first, up_last = upstream[:2] + upstream[6:], upstream[2:6]
    both_first, hidden_first, d_even, d_odd, even_first, odd_first = ffn_rule(
        mid_first, up_first, ffn_w
    )
    d_odd, near, far = lax.optimization_barrier((d_odd, near, far))
    own_sum, across_sum = pair_sums(d_even, swapped(d_odd, "seq", 1))
    mid_last, across_sum = lax.optimization_barrier((with_siblings([near, far]), across_sum))
    across_sum = swapped(across_sum[0], "seq", 6)
    both_last, hidden_last, d_even, d_odd, even_last, odd_last = ffn_rule(
        mid_last, up_last, ffn_w
    )
    both_last, d_odd, across_sum = lax.optimization_barrier((both_last, d_odd, across_sum))
    ffn_partial = ffn_grads_rule(
        mid_first + mid_last,
        up_first + up_last,
        (both_first, both_last),
        (hidden_first, hidden_last),
    )
    handed, ffn_partial = lax.optimization_barrier((swapped(d_odd, "seq", 1), ffn_partial))
    ffn_summed = reduce_weight(ffn_partial)
    near_sum, far_sum = ((d_even[i].astype(f32) + handed[i].astype(f32)).astype(bf16) for i in (0, 1))
    received = [swapped(near_sum, "seq", 2), swapped(far_sum, "seq", 4), across_sum]
    ffn_own, ffn_across = pair_sums(even_first, swapped(odd_first, "seq", 1))
    ffn_handed = swapped(odd_last, "seq", 1)
    ffn_sums = [
        (even_last[i].astype(f32) + ffn_handed[i].astype(f32)).astype(bf16) for i in (0, 1)
    ] + ffn_across
    received, ffn_own, ffn_sums = lax.optimization_barrier((received, ffn_own, ffn_sums))
    d_normed_mid = total_of(own_sum, received)
    d_from_mid, grad_mid = rms_back(residual, norm_mid, d_normed_mid)
    d_residual = upstream_own.astype(f32) + d_from_mid
    branch, ffn_sums, ffn_summed = lax.optimization_barrier(
        (gather_blocks(d_residual.astype(bf16)), ffn_sums, ffn_summed)
    )
    ffn_received = exchanged(ffn_sums)
    ffn_spread = spread_grads(ffn_summed)

    d_end = jnp.zeros((seqs, DK, DV), f32)
    d_after = jnp.zeros((seqs, 8, WIDTH), f32)
    for stage in range(stages):
        d_all, grad_taps, grad_gain, d_start, d_before = backward_rule(
            head_arg, branch, mixer_w, saved, run, taps, gain, halo, d_end, d_after
        )
        if stage < stages - 1:
            d_end = passed_along(d_start, "seq", -H)
            d_after = passed_along(d_before, "seq", -H)
    d_all = d_all.reshape(H, rows, -1)

    mixer_partial, narrow = mixer_grads_rule(
        head_arg, normed_in, branch, d_all.reshape(all_rows, -1), headed, mixer_w, beta_w
    )
    mixer_partial, ffn_spread, ffn_received = lax.optimization_barrier(
        (mixer_partial, ffn_spread, ffn_received)
    )
    mixer_summed = reduce_weight(mixer_partial)
    ffn_grads = join_hidden_rule(ffn_spread, hidden_all, 3)

    d_even, d_odd = d_in_rule(d_all, mixer_w, beta_w)
    own_sum, sums = pair_sums(d_even, swapped(d_odd, "seq", 1))
    received, mixer_summed, narrow, ffn_grads = lax.optimization_barrier(
        (exchanged(sums), mixer_summed, narrow, ffn_grads)
    )
    layer_out = (residual + total_of(ffn_own, ffn_received)).astype(bf16).reshape(inputs.shape)
    mixer_grads = join_rule(spread_grads(mixer_summed), [DK, DK, DV, DV, DV])
    d_normed_in = total_of(own_sum, received)
    d_from_in, _ = rms_back(flat_in, norm_in, d_normed_in)
    grad_input = (d_residual + d_from_in).reshape(inputs.shape)

    small = jnp.concatenate(
        [
            grad_taps[:CONV].reshape(-1),
            narrow[:, 0],
            grad_gain[0],
            grad_mid,
            narrow[:, 1] / norm_in,
        ]
    ).reshape(-1, 128)
    step = 1
    while step < lax.axis_size("wt"):
        small = small + swapped(small, "wt", step)
        step *= 2
    step = H
    while step < peers:
        small = small + swapped(small, "seq", step)
        step *= 2
    small = small[None]
    for bits in (1, 2, 4):
        small = jnp.concatenate([small, swapped(small, "seq", bits)], axis=0)
    small = small[jnp.arange(H) ^ head].reshape(H, -1)
    ends = []
    for bound in (CONV * WIDTH, model, DV, model, model):
        ends.append(bound + (ends[-1] if ends else 0))
    taps_part = small[:, : ends[0]].reshape(H, CONV, WIDTH)

    def joined(pieces):
        return jnp.swapaxes(pieces, 0, 1).reshape(CONV, -1)

    grad_conv = jnp.concatenate(
        [
            joined(taps_part[:, :, :DK]),
            joined(taps_part[:, :, DK : 2 * DK]),
            joined(taps_part[:, :, 2 * DK :]),
        ],
        axis=1,
    )
    grad_beta = small[:, ends[0] : ends[1]].T
    shared = jnp.sum(small[:, ends[1] :], axis=0)
    return (
        layer_out,
        grad_input,
        *mixer_grads,
        *ffn_grads,
        grad_beta,
        grad_conv,
        shared[DV + model :],
        shared[DV : DV + model],
        shared[:DV],
    )


def solution(mesh):
    rows = P("wt", "seq", None)
    cut = P("wt", None)
    in_specs = (rows,) * 3 + (cut,) * 8 + (P(),) * 5
    out_specs = (rows,) * 2 + (cut,) * 8 + (P(),) * 5
    return jax.shard_map(shards, mesh=mesh, in_specs=in_specs, out_specs=out_specs, check_vma=False)
```

```python
import jax
import jax.numpy as jnp
from jax import lax
from jax.experimental import pallas as pl
from jax.experimental.pallas import tpu as pltpu
from jax.sharding import PartitionSpec as P

H = 8
DK = 128
DV = 256
CONV = 4
HALO = 16
WIDTH = 2 * DK + DV
VMEM_LIMIT = 60 * 1024 * 1024
bf16 = jnp.bfloat16
f32 = jnp.float32


def dot(left, right, dims):
    return lax.dot_general(left, right, (dims, ((), ())), preferred_element_type=f32)


def product(left, right):
    return dot(left, right, ((1,), (0,)))


def contract_rows(left, right):
    return dot(left, right, ((0,), (0,)))


def contract_cols(left, right):
    return dot(left, right, ((1,), (1,)))


def parts(values):
    high = values.astype(bf16)
    return high, (values - high.astype(f32)).astype(bf16)


def mul(left, right):
    (lh, ll), (rh, rl) = left, right
    wide = product(jnp.concatenate([lh, ll], 1), jnp.concatenate([rh, rh], 0))
    return wide + product(lh, rl)


def mul_t(left, right):
    (lh, ll), (rh, rl) = left, right
    wide = contract_cols(jnp.concatenate([lh, ll], 1), jnp.concatenate([rh, rh], 1))
    return wide + contract_cols(lh, rl)


def cat_parts(values):
    return jnp.concatenate(parts(values), 1)


def from_cat(both):
    half = both.shape[1] // 2
    return both[:, :half], both[:, half:]


def iotas(size):
    return (
        lax.broadcasted_iota(jnp.int32, (size, size), 0),
        lax.broadcasted_iota(jnp.int32, (size, size), 1),
    )


def unit_inverses(lowers, rows, cols):
    size = rows.shape[0]
    level = 0
    eye = jnp.where(rows == cols, 1.0, 0.0)
    inverses = [eye] * len(lowers)
    while (1 << level) < size:
        together = (rows >> (level + 1)) == (cols >> (level + 1))
        corner = together & (((rows >> level) & 1) == 1) & (((cols >> level) & 1) == 0)
        blocks = [jnp.where(corner, lower, 0.0) for lower in lowers]
        if level == 0:
            inverses = [inverse - block for inverse, block in zip(inverses, blocks)]
        elif (1 << level) >= 16:
            half = 1 << level
            starts = range(half, size, 2 * half)
            below = [jnp.concatenate([i[at : at + half] for at in starts], 0) for i in inverses]
            blocks = [jnp.concatenate([b[at : at + half] for at in starts], 0) for b in blocks]
            steps = [mul(parts(b), parts(i)) for b, i in zip(blocks, inverses)]
            gap = jnp.zeros((half, size), f32)
            spread = [
                jnp.concatenate(
                    [
                        piece
                        for index in range(len(starts))
                        for piece in (gap, step[index * half : (index + 1) * half])
                    ],
                    0,
                )
                for step in steps
            ]
            steps = [low - mul(parts(low), parts(wide)) for low, wide in zip(below, spread)]
            inverses = [
                jnp.concatenate(
                    [
                        piece
                        for index, at in enumerate(starts)
                        for piece in (
                            inverse[at - half : at], step[index * half : (index + 1) * half]
                        )
                    ],
                    0,
                )
                for inverse, step in zip(inverses, steps)
            ]
        else:
            wholes = [parts(inverse) for inverse in inverses]
            steps = [mul(parts(block), whole) for block, whole in zip(blocks, wholes)]
            steps = [mul(whole, parts(step)) for step, whole in zip(steps, wholes)]
            inverses = [inverse - step for inverse, step in zip(inverses, steps)]
        level += 1
    return inverses


def conv_rows(conv_ref, halo_ref, rows_ref, taps_ref, chunk, seq, slot):
    size = conv_ref.shape[2]
    before = conv_ref[jnp.maximum(chunk - 1, 0), seq, size - HALO :, :]
    before = jnp.where(chunk == 0, halo_ref[seq], before)
    rows_ref[slot, :HALO, :] = before.astype(f32)
    rows_ref[slot, HALO:, :] = conv_ref[chunk, seq].astype(f32)
    total = None
    for tap in range(CONV):
        start = HALO - (CONV - 1) + tap
        term = rows_ref[slot, start : start + size, :] * taps_ref[tap : tap + 1, :]
        total = term if total is None else total + term
    return total


def run_row_of(run_ref, chunk, seq, seqs):
    return run_ref[pl.ds(chunk * seqs + seq, 1), :]


def decays(run_row, rows, cols):
    size = rows.shape[0]
    run_col = jnp.sum(jnp.where(rows == cols, run_row, 0.0), axis=1, keepdims=True)
    spread = jnp.where(rows >= cols, run_col - run_row, 0.0)
    decay_mat = jnp.where(rows >= cols, jnp.exp(spread), 0.0)
    last = run_row[:, size - 1 : size]
    return decay_mat, jnp.exp(run_col), jnp.exp(last - run_col)


def running_sums(values, rows, cols):
    upper = jnp.where(rows <= cols, 1.0, 0.0).astype(bf16)
    total = None
    for _ in range(3):
        part = values.astype(bf16)
        values = values - part.astype(f32)
        term = product(part, upper)
        total = term if total is None else total + term
    return total


def units_of(first, count, seqs):
    return [(first + chunk, seq) for chunk in range(count) for seq in range(seqs)]


FORWARD_CHUNKS = 4


def forward_kernel(head_ref, *refs):
    block_refs, decay_ref, refs = refs[:H], refs[H], refs[H + 1 :]
    weight_in, beta_ref, taps_ref, gain_ref, state_ref, halo_ref = refs[:6]
    outs, (run_ref, end_ref), held, refs = refs[6:14], refs[14:16], refs[16:24], refs[24:]
    headed_ref, conv_ref, gate_ref, mixed_ref, inverse_ref, scores_ref, delta_ref, starts_ref = held
    (
        block_ref, weight_ref, log_ref, rows_ref, recall_ref, target_ref, query_ref, write_ref,
        plain_ref, block_sems, weight_sem, out_sems,
    ) = refs
    chunks, seqs, size, _ = conv_ref.shape
    rows, cols = iotas(size)
    head = head_ref[0]

    weight_copy = pltpu.make_async_copy(
        weight_in.at[:, pl.ds(0, WIDTH + DV)], weight_ref, weight_sem
    )
    weight_copy.start()
    def block_copy(source, slot):
        return pltpu.make_async_copy(source, block_ref.at[slot], block_sems.at[slot])

    for slot in range(H):
        block_copy(block_refs[slot], slot).start()
    logs = jnp.log(decay_ref[...])
    for chunk in range(chunks):
        for seq in range(seqs):
            row = chunk * seqs + seq
            log_ref[row : row + 1, :] = logs[chunk : chunk + 1, seq * size : (seq + 1) * size]
    run_ref[...] = running_sums(log_ref[...], rows, cols)

    weight_copy.wait()

    def project(slot, _):
        chunk = slot ^ head
        block_copy(block_refs[0], slot).wait()
        block = block_ref[slot]
        conv = product(block, weight_ref[:, :WIDTH]).astype(bf16)
        gate = product(block, weight_ref[:, WIDTH:])
        beta = product(block, beta_ref[...])
        for seq in range(seqs):
            span = slice(seq * size, (seq + 1) * size)
            conv_ref[chunk, seq] = conv[span]
            gate_ref[chunk, seq, :, :DV] = gate[span]
            gate_ref[chunk, seq, :, DV:] = beta[span]
        return 0

    lax.fori_loop(0, H, project, 0)

    def send(index, first, count):
        span = pl.ds(first, count)
        pltpu.make_async_copy(
            held[index].at[span], outs[index].at[span], out_sems.at[index]
        ).start()

    def prepare(turn, _):
        units = units_of(turn * FORWARD_CHUNKS, FORWARD_CHUNKS, seqs)
        lowers = []

        @pl.when(turn > 0)
        def _():
            for index in (1, 2, 4, 5):
                send(index, (turn - 1) * FORWARD_CHUNKS, FORWARD_CHUNKS)

        for slot, (chunk, seq) in enumerate(units):
            summed = conv_rows(conv_ref, halo_ref, rows_ref, taps_ref, chunk, seq, slot)
            active = summed * jax.nn.sigmoid(summed)
            query = active[:, :DK]
            key = active[:, DK : 2 * DK]
            key = key * lax.rsqrt(jnp.sum(key * key, axis=1, keepdims=True) + 1e-06)
            beta = jax.nn.sigmoid(gate_ref[chunk, seq, :, DV : DV + 1])
            decay_mat, growth, fade = decays(run_row_of(run_ref, chunk, seq, seqs), rows, cols)
            target_ref[chunk, seq] = beta * active[:, 2 * DK :]
            query_ref[chunk, seq] = cat_parts(growth * query)
            write_ref[chunk, seq] = cat_parts((fade * key).T)
            recall_ref[chunk, seq] = cat_parts(beta * growth * key)
            key_parts = parts(key)
            gram = mul_t(key_parts, key_parts)
            lowers.append(jnp.where(rows > cols, beta * gram * decay_mat, 0.0))
            scores = mul_t(parts(query), key_parts) * decay_mat
            plain_ref[chunk, seq] = cat_parts(scores)
            scores_ref[chunk, seq] = cat_parts(scores.T)
        inverses = unit_inverses(lowers, rows, cols)
        for (chunk, seq), inverse in zip(units, inverses):
            inverse_parts = parts(inverse)
            recall = mul(inverse_parts, from_cat(recall_ref[chunk, seq]))
            recall_ref[chunk, seq] = cat_parts(recall)
            target_ref[chunk, seq] = mul(inverse_parts, parts(target_ref[chunk, seq]))
            inverse_ref[chunk, seq] = cat_parts(inverse.T)
        return 0

    lax.fori_loop(0, chunks // FORWARD_CHUNKS, prepare, 0)

    def advance(chunk, states):
        following = []

        @pl.when(chunk == 0)
        def _():
            for index in (1, 2, 4, 5):
                send(index, chunks - FORWARD_CHUNKS, FORWARD_CHUNKS)

        @pl.when(chunk > 0)
        def _():
            for index in (0, 3, 6, 7):
                send(index, chunk - 1, 1)

        for seq in range(seqs):
            state = states[seq]
            starts_ref[chunk, seq] = state
            state_parts = parts(state)
            delta = target_ref[chunk, seq] - mul(from_cat(recall_ref[chunk, seq]), state_parts)
            delta_parts = parts(delta)
            total = jnp.exp(run_row_of(run_ref, chunk, seq, seqs)[:, size - 1 : size])
            following.append(
                total * state + mul(from_cat(write_ref[chunk, seq]), delta_parts)
            )
            delta_ref[chunk, seq] = delta
            read = mul(from_cat(query_ref[chunk, seq]), state_parts)
            read = read + mul(from_cat(plain_ref[chunk, seq]), delta_parts)
            mixed_ref[chunk, seq] = read
            scale = lax.rsqrt(jnp.mean(read * read, axis=1, keepdims=True) + 1e-05)
            gate = gate_ref[chunk, seq, :, :DV]
            headed = read * scale * gain_ref[...] * (gate * jax.nn.sigmoid(gate))
            headed_ref[chunk, seq] = headed.astype(bf16)
        return tuple(following)

    final = lax.fori_loop(0, chunks, advance, tuple(state_ref[seq] for seq in range(seqs)))
    for seq in range(seqs):
        end_ref[seq] = final[seq]
    for index in (0, 3, 6, 7):
        send(index, chunks - 1, 1)
    for index in range(len(held)):
        pltpu.make_async_copy(held[index], outs[index], out_sems.at[index]).wait()


BACKWARD_CHUNKS = 2


def backward_kernel(head_ref, *refs):
    branch_refs, weight_in, refs = refs[:H], refs[H], refs[H + 1 :]
    saved, refs = refs[:7], refs[7:]
    run_ref, taps_ref, gain_ref, halo_ref, d_end_ref, d_after_ref = refs[:6]
    d_all_out, grad_taps_ref, grad_gain_ref, d_start_ref, d_before_ref = refs[6:11]
    branch_ref, weight_ref, held, refs = refs[11], refs[12], refs[13:20], refs[20:]
    conv_ref, gate_ref, mixed_ref, inverse_ref, scores_ref, delta_ref, starts_ref = held
    (
        rows_ref, d_headed_ref, hold_ref, carry_ref, base_ref, back_ref, d_target_ref, d_state_ref,
        d_conv_ref, d_all_ref, slope_ref, active_ref, column_ref,
        block_sems, weight_sem, saved_sems, out_sem,
    ) = refs
    chunks, seqs, size, _ = conv_ref.shape
    rows, cols = iotas(size)
    head = head_ref[0]

    weight_copy = pltpu.make_async_copy(
        weight_in.at[:, pl.ds(WIDTH + DV, DV)], weight_ref, weight_sem
    )
    weight_copy.start()

    def block_copy(source, slot):
        return pltpu.make_async_copy(source, branch_ref.at[slot], block_sems.at[slot])

    for slot in range(H):
        block_copy(branch_refs[slot], slot).start()
    saved_copies = [
        pltpu.make_async_copy(saved[index], held[index], saved_sems.at[index])
        for index in range(len(saved))
    ]

    lane = lax.broadcasted_iota(jnp.int32, (size, 128), 1)
    grad_gain_ref[...] = jnp.zeros_like(grad_gain_ref)
    grad_taps_ref[...] = jnp.zeros_like(grad_taps_ref)

    weight_copy.wait()

    def project(slot, _):
        @pl.when(slot == 1)
        def _():
            for copy in saved_copies[:5]:
                copy.start()

        block_copy(branch_refs[0], slot).wait()
        d_headed = product(branch_ref[slot], weight_ref[...])
        for seq in range(seqs):
            d_headed_ref[slot ^ head, seq] = d_headed[seq * size : (seq + 1) * size]
        return 0

    lax.fori_loop(0, H, project, 0)
    for copy in saved_copies[:5]:
        copy.wait()
    for copy in saved_copies[5:]:
        copy.start()

    def prepare(turn, _):
        units = units_of(turn * BACKWARD_CHUNKS, BACKWARD_CHUNKS, seqs)
        for chunk, seq in units:
            unit = chunk * seqs + seq
            summed = conv_rows(conv_ref, halo_ref, rows_ref, taps_ref, chunk, seq, unit)
            logistic = jax.nn.sigmoid(summed)
            active = summed * logistic
            slope_ref[unit] = logistic * (1.0 + summed * (1.0 - logistic))
            query = active[:, :DK]
            raw = active[:, DK : 2 * DK]
            shrink = lax.rsqrt(jnp.sum(raw * raw, axis=1, keepdims=True) + 1e-06)
            key = raw * shrink
            active_ref[unit, :, :DK] = query
            active_ref[unit, :, DK : 2 * DK] = key
            active_ref[unit, :, 2 * DK :] = active[:, 2 * DK :]
            beta = jax.nn.sigmoid(gate_ref[chunk, seq, :, DV : DV + 1])
            column_ref[unit] = jnp.where(lane == 0, shrink, beta)
            _, growth, fade = decays(run_row_of(run_ref, chunk, seq, seqs), rows, cols)
            mixed = mixed_ref[chunk, seq]
            d_headed = d_headed_ref[chunk, seq]
            gate = gate_ref[chunk, seq, :, :DV]
            logistic = jax.nn.sigmoid(gate)
            scale = lax.rsqrt(jnp.mean(mixed * mixed, axis=1, keepdims=True) + 1e-05)
            normed = mixed * scale
            swish = gate * logistic
            inner = d_headed * gain_ref[...] * swish
            d_mixed = scale * (inner - normed * jnp.mean(normed * inner, axis=1, keepdims=True))
            grad_gain_ref[...] += jnp.sum(d_headed * normed * swish, axis=0, keepdims=True)
            d_gate = d_headed * gain_ref[...] * normed * logistic * (1.0 + gate * (1.0 - logistic))
            d_all_ref[chunk ^ head, seq, :, WIDTH : WIDTH + DV] = d_gate.astype(bf16)
            d_headed_ref[chunk, seq] = d_mixed
            d_mixed_parts = parts(d_mixed)
            inverse_parts = from_cat(inverse_ref[chunk, seq])
            scored = mul(from_cat(scores_ref[chunk, seq]), d_mixed_parts)
            base_ref[chunk, seq] = mul(inverse_parts, parts(scored))
            hold_ref[chunk, seq] = cat_parts(mul(inverse_parts, parts(fade * key)))
            back_ref[chunk, seq] = mul(parts((growth * query).T), d_mixed_parts)
            carry_ref[chunk, seq] = cat_parts((beta * growth * key).T)
        return 0

    lax.fori_loop(0, chunks // BACKWARD_CHUNKS, prepare, 0)

    def advance(step, d_states):
        chunk = chunks - 1 - step
        following = []
        for seq in range(seqs):
            d_state = d_states[seq]
            d_state_ref[chunk, seq] = d_state
            d_target = base_ref[chunk, seq] + mul(from_cat(hold_ref[chunk, seq]), parts(d_state))
            d_target_ref[chunk, seq] = d_target
            total = jnp.exp(run_row_of(run_ref, chunk, seq, seqs)[:, size - 1 : size])
            back = mul(from_cat(carry_ref[chunk, seq]), parts(d_target))
            following.append(total * d_state + back_ref[chunk, seq] - back)
        return tuple(following)

    first = lax.fori_loop(0, chunks, advance, tuple(d_end_ref[seq] for seq in range(seqs)))
    for seq in range(seqs):
        d_start_ref[seq] = first[seq]
        d_conv_ref[seq, size:, :] = d_after_ref[seq]
    for copy in saved_copies[5:]:
        copy.wait()

    def send(chunk):
        slot = chunk ^ head
        pltpu.make_async_copy(d_all_ref.at[slot], d_all_out.at[slot], out_sem).start()

    def finish(turn, _):
        units = [
            (chunks - 1 - turn * BACKWARD_CHUNKS - back, seq)
            for back in range(BACKWARD_CHUNKS)
            for seq in range(seqs)
        ]

        @pl.when(turn > 0)
        def _():
            for back in range(BACKWARD_CHUNKS):
                send(chunks - 1 - (turn - 1) * BACKWARD_CHUNKS - back)

        for chunk, seq in units:
            unit = chunk * seqs + seq
            slope = slope_ref[unit]
            query = active_ref[unit, :, :DK]
            key = active_ref[unit, :, DK : 2 * DK]
            value = active_ref[unit, :, 2 * DK :]
            shrink = column_ref[unit, :, 0:1]
            beta = column_ref[unit, :, 1:2]
            decay_mat, growth, fade = decays(run_row_of(run_ref, chunk, seq, seqs), rows, cols)
            key_parts = parts(key)
            gram = mul_t(key_parts, key_parts) * decay_mat
            d_target = d_target_ref[chunk, seq]
            delta_parts = parts(delta_ref[chunk, seq])
            start_parts = parts(starts_ref[chunk, seq])
            both = parts(jnp.concatenate([d_target, d_headed_ref[chunk, seq]], 0))
            on_delta = mul_t(both, delta_parts)
            on_state = mul_t(both, start_parts)
            d_lower = jnp.where(rows > cols, -on_delta[:size], 0.0)
            d_scores = on_delta[size:] * decay_mat
            through = on_state[:size]
            d_gram = d_lower * decay_mat * beta
            d_query = growth * on_state[size:] + mul(parts(d_scores), key_parts)
            d_key = mul(parts(d_scores.T), parts(query))
            d_key = d_key + mul(parts(d_gram + d_gram.T), key_parts)
            d_key = d_key + fade * mul_t(delta_parts, parts(d_state_ref[chunk, seq]))
            d_key = d_key - (beta * growth) * through
            d_beta = (
                jnp.sum(d_target * value, axis=1, keepdims=True)
                - growth * jnp.sum(key * through, axis=1, keepdims=True)
                + jnp.sum(d_lower * gram, axis=1, keepdims=True)
            )
            d_raw = shrink * (d_key - key * jnp.sum(key * d_key, axis=1, keepdims=True))
            d_conv = jnp.concatenate([d_query, d_raw, beta * d_target], 1) * slope
            d_conv_ref[seq, :size, :] = d_conv
            d_in = None
            for tap in range(CONV):
                start = HALO - (CONV - 1) + tap
                grad_taps_ref[tap : tap + 1, :] += jnp.sum(
                    d_conv * rows_ref[unit, start : start + size, :], axis=0, keepdims=True
                )
                shift = CONV - 1 - tap
                term = d_conv_ref[seq, shift : shift + size, :] * taps_ref[tap : tap + 1, :]
                d_in = term if d_in is None else d_in + term
            d_conv_ref[seq, size:, :] = d_conv[:8, :]
            d_all_ref[chunk ^ head, seq, :, :WIDTH] = d_in.astype(bf16)
            d_logit = d_beta * beta * (1.0 - beta)
            d_all_ref[chunk ^ head, seq, :, WIDTH + DV :] = jnp.where(
                lane == 0, d_logit, 0.0
            ).astype(bf16)
        return 0

    lax.fori_loop(0, chunks // BACKWARD_CHUNKS, finish, 0)
    for seq in range(seqs):
        d_before_ref[seq] = d_conv_ref[seq, size:, :]
    for chunk in range(BACKWARD_CHUNKS):
        send(chunk)
    pltpu.make_async_copy(d_all_ref, d_all_out, out_sem).wait()


def whole(count):
    return [pl.BlockSpec(memory_space=pltpu.VMEM)] * count


def scalar():
    return [pl.BlockSpec(memory_space=pltpu.SMEM)]


shaped = jax.ShapeDtypeStruct


def cost(flops):
    return pl.CostEstimate(flops=flops, bytes_accessed=0, transcendentals=0)


def kernel_params():
    return pltpu.CompilerParams(vmem_limit_bytes=VMEM_LIMIT)


def anywhere(count):
    return [pl.BlockSpec(memory_space=pltpu.HBM)] * count


def forward_rule(head, blocks, own_decay, weight, beta_w, taps, gain, state, halo):
    rows, model = blocks[0].shape
    seqs = state.shape[0]
    size = rows // seqs
    lead = (H, seqs)
    held = [
        (lead + (size, DV), bf16),
        (lead + (size, WIDTH), bf16),
        (lead + (size, DV + 128), f32),
        (lead + (size, DV), f32),
        (lead + (size, 2 * size), bf16),
        (lead + (size, 2 * size), bf16),
        (lead + (size, DV), f32),
        (lead + (DK, DV), f32),
    ]
    return pl.pallas_call(
        forward_kernel,
        name="mixer_forward",
        out_shape=[shaped(*item) for item in held]
        + [shaped((H * seqs, size), f32), shaped((seqs, DK, DV), f32)],
        in_specs=scalar() + anywhere(H) + whole(1) + anywhere(1) + whole(5),
        out_specs=anywhere(8) + whole(2),
        scratch_shapes=[pltpu.VMEM(*item) for item in held]
        + [
            pltpu.VMEM((H, rows, model), bf16),
            pltpu.VMEM((model, WIDTH + DV), bf16),
            pltpu.VMEM((H * seqs, size), f32),
            pltpu.VMEM((FORWARD_CHUNKS * seqs, HALO + size, WIDTH), f32),
            pltpu.VMEM(lead + (size, 2 * DK), bf16),
            pltpu.VMEM(lead + (size, DV), f32),
            pltpu.VMEM(lead + (size, 2 * DK), bf16),
            pltpu.VMEM(lead + (DK, 2 * size), bf16),
            pltpu.VMEM(lead + (size, 2 * size), bf16),
            pltpu.SemaphoreType.DMA((H,)),
            pltpu.SemaphoreType.DMA,
            pltpu.SemaphoreType.DMA((8,)),
        ],
        compiler_params=kernel_params(),
    )(head, *blocks, own_decay, weight, beta_w, taps, gain, state, halo)


def backward_rule(head, branch, weight, saved, run, taps, gain, halo, d_end, d_after):
    rows, model = branch[0].shape
    seqs = d_end.shape[0]
    size = rows // seqs
    lead = (H, seqs)
    return pl.pallas_call(
        backward_kernel,
        name="mixer_backward",
        out_shape=(
            shaped(lead + (size, WIDTH + DV + 128), bf16),
            shaped((8, WIDTH), f32),
            shaped((1, DV), f32),
            shaped((seqs, DK, DV), f32),
            shaped((seqs, 8, WIDTH), f32),
        ),
        in_specs=scalar() + anywhere(H + 8) + whole(6),
        out_specs=tuple(anywhere(1) + whole(4)),
        scratch_shapes=[
            pltpu.VMEM((H, rows, model), bf16),
            pltpu.VMEM((model, DV), bf16),
        ]
        + [pltpu.VMEM(item.shape, item.dtype) for item in saved]
        + [
            pltpu.VMEM((H * seqs, HALO + size, WIDTH), f32),
            pltpu.VMEM(lead + (size, DV), f32),
            pltpu.VMEM(lead + (size, 2 * DK), bf16),
            pltpu.VMEM(lead + (DK, 2 * size), bf16),
            pltpu.VMEM(lead + (size, DV), f32),
            pltpu.VMEM(lead + (DK, DV), f32),
            pltpu.VMEM(lead + (size, DV), f32),
            pltpu.VMEM(lead + (DK, DV), f32),
            pltpu.VMEM((seqs, size + 8, WIDTH), f32),
            pltpu.VMEM(lead + (size, WIDTH + DV + 128), bf16),
            pltpu.VMEM((H * seqs, size, WIDTH), f32),
            pltpu.VMEM((H * seqs, size, WIDTH), f32),
            pltpu.VMEM((H * seqs, size, 128), f32),
            pltpu.SemaphoreType.DMA((H,)),
            pltpu.SemaphoreType.DMA,
            pltpu.SemaphoreType.DMA((7,)),
            pltpu.SemaphoreType.DMA,
        ],
        compiler_params=kernel_params(),
    )(head, *branch, weight, *saved, run, taps, gain, halo, d_end, d_after)


def out_kernel(head_ref, *refs):
    block_refs, refs = refs[:H], refs[H:]
    headed_ref, inputs_ref, gain_ref, residual_ref, normed_ref, weight_ref, sems = refs
    head = head_ref[0]

    def block_copy(source, slot):
        return pltpu.make_async_copy(source, weight_ref.at[slot], sems.at[slot])

    for slot in range(H):
        block_copy(block_refs[slot], slot).start()
    residual_ref[...] = inputs_ref[...].astype(f32)

    def add_heads(pair, _):
        slots = (2 * pair, 2 * pair + 1)
        for slot in slots:
            block_copy(block_refs[0], slot).wait()
        headed = jnp.concatenate([headed_ref[slot ^ head] for slot in slots], 1)
        weight = jnp.concatenate([weight_ref[slot] for slot in slots], 1)
        residual_ref[...] += contract_cols(headed, weight)
        return 0

    lax.fori_loop(0, H // 2, add_heads, 0)
    total = residual_ref[...]
    scale = lax.rsqrt(jnp.mean(total * total, axis=1, keepdims=True) + 1e-05)
    normed_ref[...] = (total * scale * gain_ref[...]).astype(bf16)


def out_rule(head, blocks, headed, inputs, gain):
    return pl.pallas_call(
        out_kernel,
        name="out_projection",
        out_shape=(shaped(inputs.shape, f32), shaped(inputs.shape, bf16)),
        in_specs=scalar() + anywhere(H) + whole(3),
        out_specs=tuple(whole(2)),
        scratch_shapes=[
            pltpu.VMEM((H,) + blocks[0].shape, bf16),
            pltpu.SemaphoreType.DMA((H,)),
        ],
        compiler_params=kernel_params(),
    )(head, *blocks, headed, inputs, gain)


PART = H // 2


def ffn_kernel(*refs):
    normed_refs, up_refs, refs = refs[:PART], refs[PART : 2 * PART], refs[2 * PART :]
    weight_in, d_both_ref, hidden_ref, d_even_ref, d_odd_ref, even_ref, odd_ref = refs[:7]
    normed_all_ref, up_all_ref, weight_ref, normed_sems, up_sems, weight_sem = refs[7:]
    share = weight_ref.shape[1] // 3
    step = pl.program_id(0)

    def copy_of(source, target, sems, slot):
        return pltpu.make_async_copy(source, target.at[slot], sems.at[slot])

    def start_slot(slot):
        copy_of(normed_refs[slot], normed_all_ref, normed_sems, slot).start()
        copy_of(up_refs[slot], up_all_ref, up_sems, slot).start()

    @pl.when(step == 0)
    def _():
        weight_copy = pltpu.make_async_copy(weight_in, weight_ref, weight_sem)
        weight_copy.start()
        start_slot(0)
        weight_copy.wait()

    for later in range(1, PART):

        @pl.when(step == later - 1)
        def _():
            start_slot(later)

    slot = step
    copy_of(normed_refs[0], normed_all_ref, normed_sems, slot).wait()
    copy_of(up_refs[0], up_all_ref, up_sems, slot).wait()
    both = product(normed_all_ref[slot], weight_ref[:, : 2 * share])
    d_hidden = product(up_all_ref[slot], weight_ref[:, 2 * share :])
    gate, up = both[:, :share], both[:, share:]
    logistic = jax.nn.sigmoid(gate)
    swish = gate * logistic
    hidden = (swish * up).astype(bf16)
    hidden_ref[0] = hidden
    d_gate = (d_hidden * up * logistic * (1.0 + gate * (1.0 - logistic))).astype(bf16)
    d_up = (d_hidden * swish).astype(bf16)
    d_both = jnp.concatenate([d_gate, d_up], 1)
    d_both_ref[0] = d_both
    d_in = contract_cols(d_both, weight_ref[:, : 2 * share]).astype(bf16)
    out = contract_cols(hidden, weight_ref[:, 2 * share :]).astype(bf16)
    for side, d_in_ref, out_ref in ((0, d_even_ref, even_ref), (1, d_odd_ref, odd_ref)):

        @pl.when(step % 2 == side)
        def _():
            d_in_ref[0] = d_in
            out_ref[0] = out


def ffn_rule(normed, upstream, weight):
    rows, model = normed[0].shape
    share = weight.shape[1] // 3

    def moving(width, steps):
        return pl.BlockSpec((1, rows, width), lambda step: (step // steps, 0, 0))

    return pl.pallas_call(
        ffn_kernel,
        name="feed_forward",
        grid=(PART,),
        in_specs=anywhere(2 * PART + 1),
        out_specs=[moving(2 * share, 1), moving(share, 1)] + [moving(model, 2)] * 4,
        out_shape=[shaped((PART, rows, 2 * share), bf16), shaped((PART, rows, share), bf16)]
        + [shaped((PART // 2, rows, model), bf16)] * 4,
        scratch_shapes=[pltpu.VMEM((PART, rows, model), bf16)] * 2
        + [
            pltpu.VMEM(weight.shape, bf16),
            pltpu.SemaphoreType.DMA((PART,)),
            pltpu.SemaphoreType.DMA((PART,)),
            pltpu.SemaphoreType.DMA,
        ],
        compiler_params=kernel_params(),
    )(*normed, *upstream, weight)


GRAD_TILE = 256


def ffn_grads_kernel(*refs):
    normed_refs, up_refs, refs = refs[:H], refs[H : 2 * H], refs[2 * H :]
    both_refs, hidden_refs, out_ref = refs[:2], refs[2:4], refs[4]
    wide = both_refs[0].shape[1]
    normed = jnp.concatenate([ref[...] for ref in normed_refs], 0)
    d_both = jnp.concatenate([ref[...] for ref in both_refs], 0)
    out_ref[:, :wide] = contract_rows(normed, d_both).astype(bf16)
    upstream = jnp.concatenate([ref[...] for ref in up_refs], 0)
    hidden = jnp.concatenate([ref[...] for ref in hidden_refs], 0)
    out_ref[:, wide:] = contract_rows(upstream, hidden).astype(bf16)


def ffn_grads_rule(normed, upstream, d_both, hidden):
    rows, model = normed[0].shape
    d_both = [part.reshape(PART * rows, -1) for part in d_both]
    hidden = [part.reshape(PART * rows, -1) for part in hidden]
    width = d_both[0].shape[1] + hidden[0].shape[1]
    columns = pl.BlockSpec((rows, GRAD_TILE), lambda step: (0, step))
    return pl.pallas_call(
        ffn_grads_kernel,
        name="feed_forward_grads",
        grid=(model // GRAD_TILE,),
        in_specs=[columns] * (2 * H)
        + [pl.BlockSpec(part.shape, lambda step: (0, 0)) for part in (*d_both, *hidden)],
        out_specs=pl.BlockSpec((GRAD_TILE, width), lambda step: (step, 0)),
        out_shape=shaped((model, width), bf16),
        compiler_params=kernel_params(),
    )(*normed, *upstream, *d_both, *hidden)


def mixer_grads_kernel(head_ref, *refs):
    normed_refs, branch_refs, refs = refs[:H], refs[H : 2 * H], refs[2 * H :]
    d_all_ref, headed_ref, weight_ref, beta_ref, out_ref, small_ref = refs
    head = head_ref[0]
    width = WIDTH + DV
    normed = jnp.concatenate([ref[...] for ref in normed_refs], 0)
    partial = contract_rows(normed, d_all_ref[:, :width])
    out_ref[:, :width] = partial.astype(bf16)
    beta = contract_rows(normed, d_all_ref[:, width:])
    branch = jnp.concatenate([ref[...] for ref in branch_refs], 0)
    headed = jnp.concatenate([headed_ref[slot ^ head] for slot in range(H)], 0)
    out_ref[:, width:] = contract_rows(branch, headed).astype(bf16)
    weighed = jnp.sum(partial * weight_ref[:, :width].astype(f32), axis=1, keepdims=True)
    weighed = weighed + beta[:, :1] * beta_ref[:, :1].astype(f32)
    lane = lax.broadcasted_iota(jnp.int32, beta.shape, 1)
    small_ref[...] = jnp.where(lane == 0, beta, jnp.where(lane == 1, weighed, 0.0))


def mixer_grads_rule(head, normed, branch, d_all, headed, weight, beta_w):
    rows, model = branch[0].shape
    width = WIDTH + 2 * DV
    columns = pl.BlockSpec((rows, GRAD_TILE), lambda step: (0, step))
    return pl.pallas_call(
        mixer_grads_kernel,
        name="mixer_grads",
        grid=(model // GRAD_TILE,),
        in_specs=scalar()
        + [columns] * (2 * H)
        + [
            pl.BlockSpec(d_all.shape, lambda step: (0, 0)),
            pl.BlockSpec(headed.shape, lambda step: (0, 0, 0)),
            pl.BlockSpec((GRAD_TILE, width), lambda step: (step, 0)),
            pl.BlockSpec((GRAD_TILE, 128), lambda step: (step, 0)),
        ],
        out_specs=[
            pl.BlockSpec((GRAD_TILE, width), lambda step: (step, 0)),
            pl.BlockSpec((GRAD_TILE, 128), lambda step: (step, 0)),
        ],
        out_shape=[shaped((model, width), bf16), shaped((model, 128), f32)],
        compiler_params=kernel_params(),
    )(head, *normed, *branch, d_all, headed, weight, beta_w)


def d_in_kernel(d_all_ref, weight_ref, beta_ref, even_ref, odd_ref):
    width = WIDTH + DV
    total = contract_cols(d_all_ref[0, :, :width], weight_ref[:, :width])
    total = (total + contract_cols(d_all_ref[0, :, width:], beta_ref[...])).astype(bf16)
    for side, out_ref in ((0, even_ref), (1, odd_ref)):

        @pl.when(pl.program_id(0) % 2 == side)
        def _():
            out_ref[0] = total


def d_in_rule(d_all, weight, beta_w):
    _, rows, width = d_all.shape
    model = weight.shape[0]
    out = pl.BlockSpec((1, rows, model), lambda step: (step // 2, 0, 0))
    return pl.pallas_call(
        d_in_kernel,
        name="mixer_d_in",
        grid=(H,),
        in_specs=[
            pl.BlockSpec((1, rows, width), lambda step: (step, 0, 0)),
            pl.BlockSpec(weight.shape, lambda step: (0, 0)),
            pl.BlockSpec(beta_w.shape, lambda step: (0, 0)),
        ],
        out_specs=[out, out],
        out_shape=[shaped((H // 2, rows, model), bf16)] * 2,
        compiler_params=kernel_params(),
    )(d_all, weight, beta_w)


JOIN_ROWS = 32


def join_kernel(spread_ref, *out_refs):
    start = 0
    for out_ref in out_refs:
        width = out_ref.shape[1] // H
        for peer in range(H):
            piece = spread_ref[peer, :, start : start + width]
            out_ref[:, peer * width : (peer + 1) * width] = piece.astype(f32)
        start += width


def join_rule(spread, widths):
    count, rows, width = spread.shape
    return pl.pallas_call(
        join_kernel,
        name="join_heads",
        grid=(rows // JOIN_ROWS,),
        in_specs=[pl.BlockSpec((count, JOIN_ROWS, width), lambda step: (0, step, 0))],
        out_specs=[pl.BlockSpec((JOIN_ROWS, count * width), lambda step: (step, 0)) for width in widths],
        out_shape=[shaped((rows, count * width), f32) for width in widths],
        compiler_params=kernel_params(),
    )(spread)


def join_hidden_kernel(spread_ref, *out_refs):
    count, _, width = spread_ref.shape
    share = width // len(out_refs)
    total = out_refs[0].shape[1]
    for index, out_ref in enumerate(out_refs):
        for peer in range(count):
            first = peer * share
            skip = first - min(first, total - share)
            piece = spread_ref[peer, :, index * share + skip : (index + 1) * share]
            out_ref[:, first : first + share - skip] = piece.astype(f32)


def join_hidden_rule(spread, total, pieces):
    count, rows, width = spread.shape
    return pl.pallas_call(
        join_hidden_kernel,
        name="join_hidden",
        grid=(rows // JOIN_ROWS,),
        in_specs=[pl.BlockSpec((count, JOIN_ROWS, width), lambda step: (0, step, 0))],
        out_specs=[pl.BlockSpec((JOIN_ROWS, total), lambda step: (step, 0))] * pieces,
        out_shape=[shaped((rows, total), f32)] * pieces,
        compiler_params=kernel_params(),
    )(spread)


def passed_along(array, axis, by):
    peers = lax.axis_size(axis)
    pairs = [(i, i + by) for i in range(peers) if 0 <= i + by < peers]
    return lax.ppermute(array, axis, pairs)


def swapped(array, axis, bits):
    return lax.ppermute(array, axis, [(i, i ^ bits) for i in range(lax.axis_size(axis))])


def neighbours(own):
    return [own] + [swapped(own, "seq", bits) for bits in range(2, H, 2)]


def with_siblings(blocks):
    return [each for block in blocks for each in (block, swapped(block, "seq", 1))]


def gather_blocks(own):
    return with_siblings(neighbours(own))


def pair_sums(even, handed):
    sums = [even[i].astype(f32) + handed[i].astype(f32) for i in range(even.shape[0])]
    return sums[0], [each.astype(bf16) for each in sums[1:]]


def exchanged(sums):
    return [swapped(sums[i - 1], "seq", 2 * i) for i in range(1, H // 2)]


def total_of(own, received):
    for piece in received:
        own = own + piece.astype(f32)
    return own


def rms_scale(values):
    return lax.rsqrt(jnp.mean(values * values, axis=-1, keepdims=True) + 1e-05)


def rms_back(values, gain, d_normed):
    scale = rms_scale(values)
    normed = values * scale
    pulled = d_normed * gain
    d_values = scale * (pulled - normed * jnp.mean(normed * pulled, axis=-1, keepdims=True))
    return d_values, jnp.sum(d_normed * normed, axis=0)


def shards(
    inputs,
    cotangent,
    decay,
    w_query,
    w_key,
    w_value,
    w_gate_out,
    w_out,
    w_ffn_gate,
    w_ffn_up,
    w_ffn_down,
    w_beta,
    conv_weight,
    norm_in,
    norm_mid,
    norm_head,
):
    seqs, size, model = inputs.shape
    rows = seqs * size
    peers = lax.axis_size("seq")
    stages = peers // H
    groups = None
    if stages > 1:
        groups = [[stage * H + head for head in range(H)] for stage in range(stages)]
    place = lax.axis_index("seq")
    head = lax.rem(place, H)
    head_arg = head.reshape(1)
    all_rows = H * rows
    hidden_all = w_ffn_gate.shape[1]
    share = -(-hidden_all // (H * 128)) * 128

    def gather_rows(local):
        return lax.all_gather(local, "seq", axis_index_groups=groups)

    def own_columns(weight, width):
        return lax.dynamic_slice_in_dim(weight, head * width, width, axis=1)

    def own_hidden(weight):
        start = jnp.minimum(head * share, hidden_all - share)
        piece = lax.dynamic_slice_in_dim(weight, start, share, axis=1)
        lane = lax.broadcasted_iota(jnp.int32, piece.shape, 1)
        return jnp.where(lane + start >= head * share, piece, jnp.zeros_like(piece))

    def gather_weight(local):
        return lax.all_gather(local, "wt", axis=0, tiled=True)

    mixer_w = gather_weight(
        jnp.concatenate(
            [
                own_columns(w_query, DK),
                own_columns(w_key, DK),
                own_columns(w_value, DV),
                own_columns(w_gate_out, DV),
                own_columns(w_out, DV),
            ],
            axis=1,
        )
    )
    ffn_w_own = jnp.concatenate(
        [own_hidden(w_ffn_gate), own_hidden(w_ffn_up), own_hidden(w_ffn_down)], axis=1
    )

    def reduce_weight(partial):
        return lax.psum_scatter(partial, "wt", scatter_dimension=0, tiled=True)

    def spread_grads(summed):
        spread = lax.all_gather(summed, "seq")
        if stages > 1:
            spread = spread.reshape((stages, H) + summed.shape).astype(f32)
            spread = jnp.sum(spread, axis=0)
        return spread

    own_in = inputs.reshape(rows, model)
    flat_in = own_in.astype(f32)
    normed_own = (flat_in * rms_scale(flat_in) * norm_in).astype(bf16)
    upstream_own = cotangent.reshape(rows, model)
    decay_rows = decay.reshape(rows, H).T
    near_in = neighbours(normed_own)
    near_in, late_upstream, ffn_w_own = lax.optimization_barrier(
        (near_in, upstream_own, ffn_w_own)
    )
    up_near = neighbours(late_upstream)
    taps = jnp.concatenate(
        [
            own_columns(conv_weight[:, : H * DK], DK),
            own_columns(conv_weight[:, H * DK : 2 * H * DK], DK),
            own_columns(conv_weight[:, 2 * H * DK :], DV),
        ],
        axis=1,
    )
    taps = jnp.pad(taps, ((0, 8 - CONV), (0, 0)))
    beta_w = jnp.pad(own_columns(w_beta, 1), ((0, 0), (0, 127)))
    own_decay = lax.all_to_all(
        decay_rows, "seq", 0, 0, axis_index_groups=groups, tiled=True
    )
    own_decay, taps, beta_w, near_in = lax.optimization_barrier((own_decay, taps, beta_w, near_in))
    normed_in, mixer_w, up_sides = lax.optimization_barrier(
        (with_siblings(near_in), mixer_w, up_near[:3])
    )
    up_near = up_sides + up_near[3:]
    ffn_w = gather_weight(ffn_w_own)
    in_width = WIDTH + DV
    out_near = neighbours(mixer_w[:, in_width:])

    gain = norm_head[None, :]

    state = jnp.zeros((seqs, DK, DV), f32)
    halo = jnp.zeros((seqs, HALO, WIDTH), bf16)
    if stages > 1:
        edges = lax.all_gather(normed_own.reshape(seqs, size, model)[:, size - HALO :], "seq")
        before = lax.dynamic_index_in_dim(edges, jnp.maximum(place - head - 1, 0), keepdims=False)
        rolled = product(before.reshape(seqs * HALO, model), mixer_w[:, :WIDTH]).astype(bf16)
        halo = jnp.where(place >= H, rolled.reshape(halo.shape), halo)
    for stage in range(stages):
        headed, *saved, ending = forward_rule(
            head_arg, normed_in, own_decay, mixer_w, beta_w, taps, gain, state, halo
        )
        run = saved.pop()
        if stage < stages - 1:
            state = passed_along(ending, "seq", H)

    headed = headed.reshape(H, rows, DV)
    headed, up_near, out_near = lax.optimization_barrier((headed, up_near, out_near))
    upstream = with_siblings(up_near)
    own_headed = lax.all_to_all(headed, "seq", 0, 0, axis_index_groups=groups, tiled=True)
    residual, normed_own = out_rule(
        head_arg, with_siblings(out_near), own_headed, own_in, norm_mid[None, :]
    )
    across = swapped(normed_own, "seq", 6)
    near, far = swapped(normed_own, "seq", 2), swapped(normed_own, "seq", 4)
    mid_first = with_siblings([normed_own, across])
    up_first, up_last = upstream[:2] + upstream[6:], upstream[2:6]
    both_first, hidden_first, d_even, d_odd, even_first, odd_first = ffn_rule(
        mid_first, up_first, ffn_w
    )
    d_odd, near, far = lax.optimization_barrier((d_odd, near, far))
    own_sum, across_sum = pair_sums(d_even, swapped(d_odd, "seq", 1))
    mid_last, across_sum = lax.optimization_barrier((with_siblings([near, far]), across_sum))
    across_sum = swapped(across_sum[0], "seq", 6)
    both_last, hidden_last, d_even, d_odd, even_last, odd_last = ffn_rule(
        mid_last, up_last, ffn_w
    )
    both_last, d_odd, across_sum = lax.optimization_barrier((both_last, d_odd, across_sum))
    ffn_partial = ffn_grads_rule(
        mid_first + mid_last,
        up_first + up_last,
        (both_first, both_last),
        (hidden_first, hidden_last),
    )
    handed, ffn_partial = lax.optimization_barrier((swapped(d_odd, "seq", 1), ffn_partial))
    ffn_summed = reduce_weight(ffn_partial)
    near_sum, far_sum = ((d_even[i].astype(f32) + handed[i].astype(f32)).astype(bf16) for i in (0, 1))
    received = [swapped(near_sum, "seq", 2), swapped(far_sum, "seq", 4), across_sum]
    ffn_own, ffn_across = pair_sums(even_first, swapped(odd_first, "seq", 1))
    ffn_handed = swapped(odd_last, "seq", 1)
    ffn_sums = [
        (even_last[i].astype(f32) + ffn_handed[i].astype(f32)).astype(bf16) for i in (0, 1)
    ] + ffn_across
    received, ffn_own, ffn_sums = lax.optimization_barrier((received, ffn_own, ffn_sums))
    d_normed_mid = total_of(own_sum, received)
    d_from_mid, grad_mid = rms_back(residual, norm_mid, d_normed_mid)
    d_residual = upstream_own.astype(f32) + d_from_mid
    branch, ffn_sums, ffn_summed = lax.optimization_barrier(
        (gather_blocks(d_residual.astype(bf16)), ffn_sums, ffn_summed)
    )
    ffn_received = exchanged(ffn_sums)
    ffn_spread = spread_grads(ffn_summed)

    d_end = jnp.zeros((seqs, DK, DV), f32)
    d_after = jnp.zeros((seqs, 8, WIDTH), f32)
    for stage in range(stages):
        d_all, grad_taps, grad_gain, d_start, d_before = backward_rule(
            head_arg, branch, mixer_w, saved, run, taps, gain, halo, d_end, d_after
        )
        if stage < stages - 1:
            d_end = passed_along(d_start, "seq", -H)
            d_after = passed_along(d_before, "seq", -H)
    d_all = d_all.reshape(H, rows, -1)

    mixer_partial, narrow = mixer_grads_rule(
        head_arg, normed_in, branch, d_all.reshape(all_rows, -1), headed, mixer_w, beta_w
    )
    mixer_partial, ffn_spread, ffn_received = lax.optimization_barrier(
        (mixer_partial, ffn_spread, ffn_received)
    )
    mixer_summed = reduce_weight(mixer_partial)
    ffn_grads = join_hidden_rule(ffn_spread, hidden_all, 3)

    d_even, d_odd = d_in_rule(d_all, mixer_w, beta_w)
    own_sum, sums = pair_sums(d_even, swapped(d_odd, "seq", 1))
    received, mixer_summed, narrow, ffn_grads = lax.optimization_barrier(
        (exchanged(sums), mixer_summed, narrow, ffn_grads)
    )
    layer_out = (residual + total_of(ffn_own, ffn_received)).astype(bf16).reshape(inputs.shape)
    mixer_grads = join_rule(spread_grads(mixer_summed), [DK, DK, DV, DV, DV])
    d_normed_in = total_of(own_sum, received)
    d_from_in, _ = rms_back(flat_in, norm_in, d_normed_in)
    grad_input = (d_residual + d_from_in).reshape(inputs.shape)

    small = jnp.concatenate(
        [
            grad_taps[:CONV].reshape(-1),
            narrow[:, 0],
            grad_gain[0],
            grad_mid,
            narrow[:, 1] / norm_in,
        ]
    ).reshape(-1, 128)
    step = 1
    while step < lax.axis_size("wt"):
        small = small + swapped(small, "wt", step)
        step *= 2
    step = H
    while step < peers:
        small = small + swapped(small, "seq", step)
        step *= 2
    small = small[None]
    for bits in (1, 2, 4):
        small = jnp.concatenate([small, swapped(small, "seq", bits)], axis=0)
    small = small[jnp.arange(H) ^ head].reshape(H, -1)
    ends = []
    for bound in (CONV * WIDTH, model, DV, model, model):
        ends.append(bound + (ends[-1] if ends else 0))
    taps_part = small[:, : ends[0]].reshape(H, CONV, WIDTH)

    def joined(pieces):
        return jnp.swapaxes(pieces, 0, 1).reshape(CONV, -1)

    grad_conv = jnp.concatenate(
        [
            joined(taps_part[:, :, :DK]),
            joined(taps_part[:, :, DK : 2 * DK]),
            joined(taps_part[:, :, 2 * DK :]),
        ],
        axis=1,
    )
    grad_beta = small[:, ends[0] : ends[1]].T
    shared = jnp.sum(small[:, ends[1] :], axis=0)
    return (
        layer_out,
        grad_input,
        *mixer_grads,
        *ffn_grads,
        grad_beta,
        grad_conv,
        shared[DV + model :],
        shared[DV : DV + model],
        shared[:DV],
    )


def solution(mesh):
    rows = P("wt", "seq", None)
    cut = P("wt", None)
    in_specs = (rows,) * 3 + (cut,) * 8 + (P(),) * 5
    out_specs = (rows,) * 2 + (cut,) * 8 + (P(),) * 5
    return jax.shard_map(shards, mesh=mesh, in_specs=in_specs, out_specs=out_specs, check_vma=False)
```

```python
import jax
import jax.numpy as jnp
from jax import lax
from jax.experimental import pallas as pl
from jax.experimental.pallas import tpu as pltpu
from jax.sharding import PartitionSpec as P

H = 8
DK = 128
DV = 256
CONV = 4
HALO = 16
WIDTH = 2 * DK + DV
VMEM_LIMIT = 60 * 1024 * 1024
bf16 = jnp.bfloat16
f32 = jnp.float32


def dot(left, right, dims):
    return lax.dot_general(left, right, (dims, ((), ())), preferred_element_type=f32)


def product(left, right):
    return dot(left, right, ((1,), (0,)))


def contract_rows(left, right):
    return dot(left, right, ((0,), (0,)))


def contract_cols(left, right):
    return dot(left, right, ((1,), (1,)))


def parts(values):
    high = values.astype(bf16)
    return high, (values - high.astype(f32)).astype(bf16)


def mul(left, right):
    (lh, ll), (rh, rl) = left, right
    wide = product(jnp.concatenate([lh, ll], 1), jnp.concatenate([rh, rh], 0))
    return wide + product(lh, rl)


def mul_t(left, right):
    (lh, ll), (rh, rl) = left, right
    wide = contract_cols(jnp.concatenate([lh, ll], 1), jnp.concatenate([rh, rh], 1))
    return wide + contract_cols(lh, rl)


def cat_parts(values):
    return jnp.concatenate(parts(values), 1)


def from_cat(both):
    half = both.shape[1] // 2
    return both[:, :half], both[:, half:]


def iotas(size):
    return (
        lax.broadcasted_iota(jnp.int32, (size, size), 0),
        lax.broadcasted_iota(jnp.int32, (size, size), 1),
    )


def unit_inverses(lowers, rows, cols):
    size = rows.shape[0]
    level = 0
    eye = jnp.where(rows == cols, 1.0, 0.0)
    inverses = [eye] * len(lowers)
    while (1 << level) < size:
        together = (rows >> (level + 1)) == (cols >> (level + 1))
        corner = together & (((rows >> level) & 1) == 1) & (((cols >> level) & 1) == 0)
        blocks = [jnp.where(corner, lower, 0.0) for lower in lowers]
        if level == 0:
            inverses = [inverse - block for inverse, block in zip(inverses, blocks)]
        elif (1 << level) >= 16:
            half = 1 << level
            starts = range(half, size, 2 * half)
            below = [jnp.concatenate([i[at : at + half] for at in starts], 0) for i in inverses]
            blocks = [jnp.concatenate([b[at : at + half] for at in starts], 0) for b in blocks]
            steps = [mul(parts(b), parts(i)) for b, i in zip(blocks, inverses)]
            gap = jnp.zeros((half, size), f32)
            spread = [
                jnp.concatenate(
                    [
                        piece
                        for index in range(len(starts))
                        for piece in (gap, step[index * half : (index + 1) * half])
                    ],
                    0,
                )
                for step in steps
            ]
            steps = [low - mul(parts(low), parts(wide)) for low, wide in zip(below, spread)]
            inverses = [
                jnp.concatenate(
                    [
                        piece
                        for index, at in enumerate(starts)
                        for piece in (
                            inverse[at - half : at], step[index * half : (index + 1) * half]
                        )
                    ],
                    0,
                )
                for inverse, step in zip(inverses, steps)
            ]
        else:
            wholes = [parts(inverse) for inverse in inverses]
            steps = [mul(parts(block), whole) for block, whole in zip(blocks, wholes)]
            steps = [mul(whole, parts(step)) for step, whole in zip(steps, wholes)]
            inverses = [inverse - step for inverse, step in zip(inverses, steps)]
        level += 1
    return inverses


def conv_rows(conv_ref, halo_ref, rows_ref, taps_ref, chunk, seq, slot):
    size = conv_ref.shape[2]
    before = conv_ref[jnp.maximum(chunk - 1, 0), seq, size - HALO :, :]
    before = jnp.where(chunk == 0, halo_ref[seq], before)
    rows_ref[slot, :HALO, :] = before.astype(f32)
    rows_ref[slot, HALO:, :] = conv_ref[chunk, seq].astype(f32)
    total = None
    for tap in range(CONV):
        start = HALO - (CONV - 1) + tap
        term = rows_ref[slot, start : start + size, :] * taps_ref[tap : tap + 1, :]
        total = term if total is None else total + term
    return total


def run_row_of(run_ref, chunk, seq, seqs):
    return run_ref[pl.ds(chunk * seqs + seq, 1), :]


def decays(run_row, rows, cols):
    size = rows.shape[0]
    run_col = jnp.sum(jnp.where(rows == cols, run_row, 0.0), axis=1, keepdims=True)
    spread = jnp.where(rows >= cols, run_col - run_row, 0.0)
    decay_mat = jnp.where(rows >= cols, jnp.exp(spread), 0.0)
    last = run_row[:, size - 1 : size]
    return decay_mat, jnp.exp(run_col), jnp.exp(last - run_col)


def running_sums(values, rows, cols):
    upper = jnp.where(rows <= cols, 1.0, 0.0).astype(bf16)
    total = None
    for _ in range(3):
        part = values.astype(bf16)
        values = values - part.astype(f32)
        term = product(part, upper)
        total = term if total is None else total + term
    return total


def units_of(first, count, seqs):
    return [(first + chunk, seq) for chunk in range(count) for seq in range(seqs)]


FORWARD_CHUNKS = 4


def forward_kernel(head_ref, *refs):
    block_refs, decay_ref, refs = refs[:H], refs[H], refs[H + 1 :]
    weight_in, beta_ref, taps_ref, gain_ref, state_ref, halo_ref = refs[:6]
    outs, (run_ref, end_ref), held, refs = refs[6:14], refs[14:16], refs[16:24], refs[24:]
    headed_ref, conv_ref, gate_ref, mixed_ref, inverse_ref, scores_ref, delta_ref, starts_ref = held
    (
        block_ref, weight_ref, log_ref, rows_ref, recall_ref, target_ref, query_ref, write_ref,
        plain_ref, block_sems, weight_sem, out_sems,
    ) = refs
    chunks, seqs, size, _ = conv_ref.shape
    rows, cols = iotas(size)
    head = head_ref[0]

    weight_copy = pltpu.make_async_copy(
        weight_in.at[:, pl.ds(0, WIDTH + DV)], weight_ref, weight_sem
    )
    weight_copy.start()
    def block_copy(source, slot):
        return pltpu.make_async_copy(source, block_ref.at[slot], block_sems.at[slot])

    for slot in range(H):
        block_copy(block_refs[slot], slot).start()
    logs = jnp.log(decay_ref[...])
    for chunk in range(chunks):
        for seq in range(seqs):
            row = chunk * seqs + seq
            log_ref[row : row + 1, :] = logs[chunk : chunk + 1, seq * size : (seq + 1) * size]
    run_ref[...] = running_sums(log_ref[...], rows, cols)

    weight_copy.wait()

    def project(slot, _):
        chunk = slot ^ head
        block_copy(block_refs[0], slot).wait()
        block = block_ref[slot]
        conv = product(block, weight_ref[:, :WIDTH]).astype(bf16)
        gate = product(block, weight_ref[:, WIDTH:])
        beta = product(block, beta_ref[...])
        for seq in range(seqs):
            span = slice(seq * size, (seq + 1) * size)
            conv_ref[chunk, seq] = conv[span]
            gate_ref[chunk, seq, :, :DV] = gate[span]
            gate_ref[chunk, seq, :, DV:] = beta[span]
        return 0

    lax.fori_loop(0, H, project, 0)

    def send(index, first, count):
        span = pl.ds(first, count)
        pltpu.make_async_copy(
            held[index].at[span], outs[index].at[span], out_sems.at[index]
        ).start()

    def prepare(turn, _):
        units = units_of(turn * FORWARD_CHUNKS, FORWARD_CHUNKS, seqs)
        lowers = []

        @pl.when(turn > 0)
        def _():
            for index in (1, 2, 4, 5):
                send(index, (turn - 1) * FORWARD_CHUNKS, FORWARD_CHUNKS)

        for slot, (chunk, seq) in enumerate(units):
            summed = conv_rows(conv_ref, halo_ref, rows_ref, taps_ref, chunk, seq, slot)
            active = summed * jax.nn.sigmoid(summed)
            query = active[:, :DK]
            key = active[:, DK : 2 * DK]
            key = key * lax.rsqrt(jnp.sum(key * key, axis=1, keepdims=True) + 1e-06)
            beta = jax.nn.sigmoid(gate_ref[chunk, seq, :, DV : DV + 1])
            decay_mat, growth, fade = decays(run_row_of(run_ref, chunk, seq, seqs), rows, cols)
            target_ref[chunk, seq] = beta * active[:, 2 * DK :]
            query_ref[chunk, seq] = cat_parts(growth * query)
            write_ref[chunk, seq] = cat_parts((fade * key).T)
            recall_ref[chunk, seq] = cat_parts(beta * growth * key)
            key_parts = parts(key)
            gram = mul_t(key_parts, key_parts)
            lowers.append(jnp.where(rows > cols, beta * gram * decay_mat, 0.0))
            scores = mul_t(parts(query), key_parts) * decay_mat
            plain_ref[chunk, seq] = cat_parts(scores)
            scores_ref[chunk, seq] = cat_parts(scores.T)
        inverses = unit_inverses(lowers, rows, cols)
        for (chunk, seq), inverse in zip(units, inverses):
            inverse_parts = parts(inverse)
            recall = mul(inverse_parts, from_cat(recall_ref[chunk, seq]))
            recall_ref[chunk, seq] = cat_parts(recall)
            target_ref[chunk, seq] = mul(inverse_parts, parts(target_ref[chunk, seq]))
            inverse_ref[chunk, seq] = cat_parts(inverse.T)
        return 0

    lax.fori_loop(0, chunks // FORWARD_CHUNKS, prepare, 0)

    def advance(chunk, states):
        following = []

        @pl.when(chunk == 0)
        def _():
            for index in (1, 2, 4, 5):
                send(index, chunks - FORWARD_CHUNKS, FORWARD_CHUNKS)

        @pl.when(chunk > 0)
        def _():
            for index in (0, 3, 6, 7):
                send(index, chunk - 1, 1)

        for seq in range(seqs):
            state = states[seq]
            starts_ref[chunk, seq] = state
            state_parts = parts(state)
            delta = target_ref[chunk, seq] - mul(from_cat(recall_ref[chunk, seq]), state_parts)
            delta_parts = parts(delta)
            total = jnp.exp(run_row_of(run_ref, chunk, seq, seqs)[:, size - 1 : size])
            following.append(
                total * state + mul(from_cat(write_ref[chunk, seq]), delta_parts)
            )
            delta_ref[chunk, seq] = delta
            read = mul(from_cat(query_ref[chunk, seq]), state_parts)
            read = read + mul(from_cat(plain_ref[chunk, seq]), delta_parts)
            mixed_ref[chunk, seq] = read
            scale = lax.rsqrt(jnp.mean(read * read, axis=1, keepdims=True) + 1e-05)
            gate = gate_ref[chunk, seq, :, :DV]
            headed = read * scale * gain_ref[...] * (gate * jax.nn.sigmoid(gate))
            headed_ref[chunk, seq] = headed.astype(bf16)
        return tuple(following)

    final = lax.fori_loop(0, chunks, advance, tuple(state_ref[seq] for seq in range(seqs)))
    for seq in range(seqs):
        end_ref[seq] = final[seq]
    for index in (0, 3, 6, 7):
        send(index, chunks - 1, 1)
    for index in range(len(held)):
        pltpu.make_async_copy(held[index], outs[index], out_sems.at[index]).wait()


BACKWARD_CHUNKS = 2


def backward_kernel(head_ref, *refs):
    branch_refs, weight_in, refs = refs[:H], refs[H], refs[H + 1 :]
    saved, refs = refs[:7], refs[7:]
    run_ref, taps_ref, gain_ref, halo_ref, d_end_ref, d_after_ref = refs[:6]
    d_all_out, grad_taps_ref, grad_gain_ref, d_start_ref, d_before_ref = refs[6:11]
    branch_ref, weight_ref, held, refs = refs[11], refs[12], refs[13:20], refs[20:]
    conv_ref, gate_ref, mixed_ref, inverse_ref, scores_ref, delta_ref, starts_ref = held
    (
        rows_ref, d_headed_ref, hold_ref, carry_ref, base_ref, back_ref, d_target_ref, d_state_ref,
        d_conv_ref, d_all_ref, slope_ref, active_ref, column_ref,
        block_sems, weight_sem, saved_sems, out_sem,
    ) = refs
    chunks, seqs, size, _ = conv_ref.shape
    rows, cols = iotas(size)
    head = head_ref[0]

    weight_copy = pltpu.make_async_copy(
        weight_in.at[:, pl.ds(WIDTH + DV, DV)], weight_ref, weight_sem
    )
    weight_copy.start()

    def block_copy(source, slot):
        return pltpu.make_async_copy(source, branch_ref.at[slot], block_sems.at[slot])

    for slot in range(H):
        block_copy(branch_refs[slot], slot).start()
    saved_copies = [
        pltpu.make_async_copy(saved[index], held[index], saved_sems.at[index])
        for index in range(len(saved))
    ]

    lane = lax.broadcasted_iota(jnp.int32, (size, 128), 1)
    grad_gain_ref[...] = jnp.zeros_like(grad_gain_ref)
    grad_taps_ref[...] = jnp.zeros_like(grad_taps_ref)

    weight_copy.wait()

    def project(slot, _):
        @pl.when(slot == 1)
        def _():
            for copy in saved_copies[:5]:
                copy.start()

        block_copy(branch_refs[0], slot).wait()
        d_headed = product(branch_ref[slot], weight_ref[...])
        for seq in range(seqs):
            d_headed_ref[slot ^ head, seq] = d_headed[seq * size : (seq + 1) * size]
        return 0

    lax.fori_loop(0, H, project, 0)
    for copy in saved_copies[:5]:
        copy.wait()
    for copy in saved_copies[5:]:
        copy.start()

    def prepare(turn, _):
        units = units_of(turn * BACKWARD_CHUNKS, BACKWARD_CHUNKS, seqs)
        for chunk, seq in units:
            unit = chunk * seqs + seq
            summed = conv_rows(conv_ref, halo_ref, rows_ref, taps_ref, chunk, seq, unit)
            logistic = jax.nn.sigmoid(summed)
            active = summed * logistic
            slope_ref[unit] = logistic * (1.0 + summed * (1.0 - logistic))
            query = active[:, :DK]
            raw = active[:, DK : 2 * DK]
            shrink = lax.rsqrt(jnp.sum(raw * raw, axis=1, keepdims=True) + 1e-06)
            key = raw * shrink
            active_ref[unit, :, :DK] = query
            active_ref[unit, :, DK : 2 * DK] = key
            active_ref[unit, :, 2 * DK :] = active[:, 2 * DK :]
            beta = jax.nn.sigmoid(gate_ref[chunk, seq, :, DV : DV + 1])
            column_ref[unit] = jnp.where(lane == 0, shrink, beta)
            _, growth, fade = decays(run_row_of(run_ref, chunk, seq, seqs), rows, cols)
            mixed = mixed_ref[chunk, seq]
            d_headed = d_headed_ref[chunk, seq]
            gate = gate_ref[chunk, seq, :, :DV]
            logistic = jax.nn.sigmoid(gate)
            scale = lax.rsqrt(jnp.mean(mixed * mixed, axis=1, keepdims=True) + 1e-05)
            normed = mixed * scale
            swish = gate * logistic
            inner = d_headed * gain_ref[...] * swish
            d_mixed = scale * (inner - normed * jnp.mean(normed * inner, axis=1, keepdims=True))
            grad_gain_ref[...] += jnp.sum(d_headed * normed * swish, axis=0, keepdims=True)
            d_gate = d_headed * gain_ref[...] * normed * logistic * (1.0 + gate * (1.0 - logistic))
            d_all_ref[chunk ^ head, seq, :, WIDTH : WIDTH + DV] = d_gate.astype(bf16)
            d_headed_ref[chunk, seq] = d_mixed
            d_mixed_parts = parts(d_mixed)
            inverse_parts = from_cat(inverse_ref[chunk, seq])
            scored = mul(from_cat(scores_ref[chunk, seq]), d_mixed_parts)
            base_ref[chunk, seq] = mul(inverse_parts, parts(scored))
            hold_ref[chunk, seq] = cat_parts(mul(inverse_parts, parts(fade * key)))
            back_ref[chunk, seq] = mul(parts((growth * query).T), d_mixed_parts)
            carry_ref[chunk, seq] = cat_parts((beta * growth * key).T)
        return 0

    lax.fori_loop(0, chunks // BACKWARD_CHUNKS, prepare, 0)

    def advance(step, d_states):
        chunk = chunks - 1 - step
        following = []
        for seq in range(seqs):
            d_state = d_states[seq]
            d_state_ref[chunk, seq] = d_state
            d_target = base_ref[chunk, seq] + mul(from_cat(hold_ref[chunk, seq]), parts(d_state))
            d_target_ref[chunk, seq] = d_target
            total = jnp.exp(run_row_of(run_ref, chunk, seq, seqs)[:, size - 1 : size])
            back = mul(from_cat(carry_ref[chunk, seq]), parts(d_target))
            following.append(total * d_state + back_ref[chunk, seq] - back)
        return tuple(following)

    first = lax.fori_loop(0, chunks, advance, tuple(d_end_ref[seq] for seq in range(seqs)))
    for seq in range(seqs):
        d_start_ref[seq] = first[seq]
        d_conv_ref[seq, size:, :] = d_after_ref[seq]
    for copy in saved_copies[5:]:
        copy.wait()

    def send(chunk):
        slot = chunk ^ head
        pltpu.make_async_copy(d_all_ref.at[slot], d_all_out.at[slot], out_sem).start()

    def finish(turn, _):
        units = [
            (chunks - 1 - turn * BACKWARD_CHUNKS - back, seq)
            for back in range(BACKWARD_CHUNKS)
            for seq in range(seqs)
        ]

        @pl.when(turn > 0)
        def _():
            for back in range(BACKWARD_CHUNKS):
                send(chunks - 1 - (turn - 1) * BACKWARD_CHUNKS - back)

        for chunk, seq in units:
            unit = chunk * seqs + seq
            slope = slope_ref[unit]
            query = active_ref[unit, :, :DK]
            key = active_ref[unit, :, DK : 2 * DK]
            value = active_ref[unit, :, 2 * DK :]
            shrink = column_ref[unit, :, 0:1]
            beta = column_ref[unit, :, 1:2]
            decay_mat, growth, fade = decays(run_row_of(run_ref, chunk, seq, seqs), rows, cols)
            key_parts = parts(key)
            gram = mul_t(key_parts, key_parts) * decay_mat
            d_target = d_target_ref[chunk, seq]
            delta_parts = parts(delta_ref[chunk, seq])
            start_parts = parts(starts_ref[chunk, seq])
            both = parts(jnp.concatenate([d_target, d_headed_ref[chunk, seq]], 0))
            on_delta = mul_t(both, delta_parts)
            on_state = mul_t(both, start_parts)
            d_lower = jnp.where(rows > cols, -on_delta[:size], 0.0)
            d_scores = on_delta[size:] * decay_mat
            through = on_state[:size]
            d_gram = d_lower * decay_mat * beta
            d_query = growth * on_state[size:] + mul(parts(d_scores), key_parts)
            d_key = mul(parts(d_scores.T), parts(query))
            d_key = d_key + mul(parts(d_gram + d_gram.T), key_parts)
            d_key = d_key + fade * mul_t(delta_parts, parts(d_state_ref[chunk, seq]))
            d_key = d_key - (beta * growth) * through
            d_beta = (
                jnp.sum(d_target * value, axis=1, keepdims=True)
                - growth * jnp.sum(key * through, axis=1, keepdims=True)
                + jnp.sum(d_lower * gram, axis=1, keepdims=True)
            )
            d_raw = shrink * (d_key - key * jnp.sum(key * d_key, axis=1, keepdims=True))
            d_conv = jnp.concatenate([d_query, d_raw, beta * d_target], 1) * slope
            d_conv_ref[seq, :size, :] = d_conv
            d_in = None
            for tap in range(CONV):
                start = HALO - (CONV - 1) + tap
                grad_taps_ref[tap : tap + 1, :] += jnp.sum(
                    d_conv * rows_ref[unit, start : start + size, :], axis=0, keepdims=True
                )
                shift = CONV - 1 - tap
                term = d_conv_ref[seq, shift : shift + size, :] * taps_ref[tap : tap + 1, :]
                d_in = term if d_in is None else d_in + term
            d_conv_ref[seq, size:, :] = d_conv[:8, :]
            d_all_ref[chunk ^ head, seq, :, :WIDTH] = d_in.astype(bf16)
            d_logit = d_beta * beta * (1.0 - beta)
            d_all_ref[chunk ^ head, seq, :, WIDTH + DV :] = jnp.where(
                lane == 0, d_logit, 0.0
            ).astype(bf16)
        return 0

    lax.fori_loop(0, chunks // BACKWARD_CHUNKS, finish, 0)
    for seq in range(seqs):
        d_before_ref[seq] = d_conv_ref[seq, size:, :]
    for chunk in range(BACKWARD_CHUNKS):
        send(chunk)
    pltpu.make_async_copy(d_all_ref, d_all_out, out_sem).wait()


def whole(count):
    return [pl.BlockSpec(memory_space=pltpu.VMEM)] * count


def scalar():
    return [pl.BlockSpec(memory_space=pltpu.SMEM)]


shaped = jax.ShapeDtypeStruct


def cost(flops):
    return pl.CostEstimate(flops=flops, bytes_accessed=0, transcendentals=0)


def kernel_params():
    return pltpu.CompilerParams(vmem_limit_bytes=VMEM_LIMIT)


def own_columns_kernel(head_ref, *refs):
    out_ref = refs[-1]
    start = 0
    for ref in refs[:-1]:
        width = ref.shape[1]
        out_ref[:, start : start + width] = ref[...]
        start += width


def own_columns_rule(head, weights, widths):
    rows = weights[0].shape[0]
    total = sum(widths)
    return pl.pallas_call(
        own_columns_kernel,
        name="own_columns",
        grid_spec=pltpu.PrefetchScalarGridSpec(
            num_scalar_prefetch=1,
            grid=(1,),
            in_specs=[
                pl.BlockSpec((rows, width), lambda step, head_ref: (0, head_ref[0]))
                for width in widths
            ],
            out_specs=pl.BlockSpec((rows, total), lambda step, head_ref: (0, 0)),
        ),
        out_shape=shaped((rows, total), bf16),
        compiler_params=kernel_params(),
    )(head, *weights)


def anywhere(count):
    return [pl.BlockSpec(memory_space=pltpu.HBM)] * count


def forward_rule(head, blocks, own_decay, weight, beta_w, taps, gain, state, halo):
    rows, model = blocks[0].shape
    seqs = state.shape[0]
    size = rows // seqs
    lead = (H, seqs)
    held = [
        (lead + (size, DV), bf16),
        (lead + (size, WIDTH), bf16),
        (lead + (size, DV + 128), f32),
        (lead + (size, DV), f32),
        (lead + (size, 2 * size), bf16),
        (lead + (size, 2 * size), bf16),
        (lead + (size, DV), f32),
        (lead + (DK, DV), f32),
    ]
    return pl.pallas_call(
        forward_kernel,
        name="mixer_forward",
        out_shape=[shaped(*item) for item in held]
        + [shaped((H * seqs, size), f32), shaped((seqs, DK, DV), f32)],
        in_specs=scalar() + anywhere(H) + whole(1) + anywhere(1) + whole(5),
        out_specs=anywhere(8) + whole(2),
        scratch_shapes=[pltpu.VMEM(*item) for item in held]
        + [
            pltpu.VMEM((H, rows, model), bf16),
            pltpu.VMEM((model, WIDTH + DV), bf16),
            pltpu.VMEM((H * seqs, size), f32),
            pltpu.VMEM((FORWARD_CHUNKS * seqs, HALO + size, WIDTH), f32),
            pltpu.VMEM(lead + (size, 2 * DK), bf16),
            pltpu.VMEM(lead + (size, DV), f32),
            pltpu.VMEM(lead + (size, 2 * DK), bf16),
            pltpu.VMEM(lead + (DK, 2 * size), bf16),
            pltpu.VMEM(lead + (size, 2 * size), bf16),
            pltpu.SemaphoreType.DMA((H,)),
            pltpu.SemaphoreType.DMA,
            pltpu.SemaphoreType.DMA((8,)),
        ],
        compiler_params=kernel_params(),
    )(head, *blocks, own_decay, weight, beta_w, taps, gain, state, halo)


def backward_rule(head, branch, weight, saved, run, taps, gain, halo, d_end, d_after):
    rows, model = branch[0].shape
    seqs = d_end.shape[0]
    size = rows // seqs
    lead = (H, seqs)
    return pl.pallas_call(
        backward_kernel,
        name="mixer_backward",
        out_shape=(
            shaped(lead + (size, WIDTH + DV + 128), bf16),
            shaped((8, WIDTH), f32),
            shaped((1, DV), f32),
            shaped((seqs, DK, DV), f32),
            shaped((seqs, 8, WIDTH), f32),
        ),
        in_specs=scalar() + anywhere(H + 8) + whole(6),
        out_specs=tuple(anywhere(1) + whole(4)),
        scratch_shapes=[
            pltpu.VMEM((H, rows, model), bf16),
            pltpu.VMEM((model, DV), bf16),
        ]
        + [pltpu.VMEM(item.shape, item.dtype) for item in saved]
        + [
            pltpu.VMEM((H * seqs, HALO + size, WIDTH), f32),
            pltpu.VMEM(lead + (size, DV), f32),
            pltpu.VMEM(lead + (size, 2 * DK), bf16),
            pltpu.VMEM(lead + (DK, 2 * size), bf16),
            pltpu.VMEM(lead + (size, DV), f32),
            pltpu.VMEM(lead + (DK, DV), f32),
            pltpu.VMEM(lead + (size, DV), f32),
            pltpu.VMEM(lead + (DK, DV), f32),
            pltpu.VMEM((seqs, size + 8, WIDTH), f32),
            pltpu.VMEM(lead + (size, WIDTH + DV + 128), bf16),
            pltpu.VMEM((H * seqs, size, WIDTH), f32),
            pltpu.VMEM((H * seqs, size, WIDTH), f32),
            pltpu.VMEM((H * seqs, size, 128), f32),
            pltpu.SemaphoreType.DMA((H,)),
            pltpu.SemaphoreType.DMA,
            pltpu.SemaphoreType.DMA((7,)),
            pltpu.SemaphoreType.DMA,
        ],
        compiler_params=kernel_params(),
    )(head, *branch, weight, *saved, run, taps, gain, halo, d_end, d_after)


def out_kernel(head_ref, *refs):
    block_refs, refs = refs[:H], refs[H:]
    headed_ref, inputs_ref, gain_ref, residual_ref, normed_ref, weight_ref, sems = refs
    head = head_ref[0]

    def block_copy(source, slot):
        return pltpu.make_async_copy(source, weight_ref.at[slot], sems.at[slot])

    for slot in range(H):
        block_copy(block_refs[slot], slot).start()
    residual_ref[...] = inputs_ref[...].astype(f32)

    def add_heads(pair, _):
        slots = (2 * pair, 2 * pair + 1)
        for slot in slots:
            block_copy(block_refs[0], slot).wait()
        headed = jnp.concatenate([headed_ref[slot ^ head] for slot in slots], 1)
        weight = jnp.concatenate([weight_ref[slot] for slot in slots], 1)
        residual_ref[...] += contract_cols(headed, weight)
        return 0

    lax.fori_loop(0, H // 2, add_heads, 0)
    total = residual_ref[...]
    scale = lax.rsqrt(jnp.mean(total * total, axis=1, keepdims=True) + 1e-05)
    normed_ref[...] = (total * scale * gain_ref[...]).astype(bf16)


def out_rule(head, blocks, headed, inputs, gain):
    return pl.pallas_call(
        out_kernel,
        name="out_projection",
        out_shape=(shaped(inputs.shape, f32), shaped(inputs.shape, bf16)),
        in_specs=scalar() + anywhere(H) + whole(3),
        out_specs=tuple(whole(2)),
        scratch_shapes=[
            pltpu.VMEM((H,) + blocks[0].shape, bf16),
            pltpu.SemaphoreType.DMA((H,)),
        ],
        compiler_params=kernel_params(),
    )(head, *blocks, headed, inputs, gain)


PART = H // 2


def ffn_kernel(*refs):
    normed_refs, up_refs, refs = refs[:PART], refs[PART : 2 * PART], refs[2 * PART :]
    weight_in, d_both_ref, hidden_ref, d_even_ref, d_odd_ref, even_ref, odd_ref = refs[:7]
    normed_all_ref, up_all_ref, weight_ref, normed_sems, up_sems, weight_sem = refs[7:]
    share = weight_ref.shape[1] // 3
    step = pl.program_id(0)

    def copy_of(source, target, sems, slot):
        return pltpu.make_async_copy(source, target.at[slot], sems.at[slot])

    def start_slot(slot):
        copy_of(normed_refs[slot], normed_all_ref, normed_sems, slot).start()
        copy_of(up_refs[slot], up_all_ref, up_sems, slot).start()

    @pl.when(step == 0)
    def _():
        weight_copy = pltpu.make_async_copy(weight_in, weight_ref, weight_sem)
        weight_copy.start()
        start_slot(0)
        weight_copy.wait()

    for later in range(1, PART):

        @pl.when(step == later - 1)
        def _():
            start_slot(later)

    slot = step
    copy_of(normed_refs[0], normed_all_ref, normed_sems, slot).wait()
    copy_of(up_refs[0], up_all_ref, up_sems, slot).wait()
    both = product(normed_all_ref[slot], weight_ref[:, : 2 * share])
    d_hidden = product(up_all_ref[slot], weight_ref[:, 2 * share :])
    gate, up = both[:, :share], both[:, share:]
    logistic = jax.nn.sigmoid(gate)
    swish = gate * logistic
    hidden = (swish * up).astype(bf16)
    hidden_ref[0] = hidden
    d_gate = (d_hidden * up * logistic * (1.0 + gate * (1.0 - logistic))).astype(bf16)
    d_up = (d_hidden * swish).astype(bf16)
    d_both = jnp.concatenate([d_gate, d_up], 1)
    d_both_ref[0] = d_both
    d_in = contract_cols(d_both, weight_ref[:, : 2 * share]).astype(bf16)
    out = contract_cols(hidden, weight_ref[:, 2 * share :]).astype(bf16)
    for side, d_in_ref, out_ref in ((0, d_even_ref, even_ref), (1, d_odd_ref, odd_ref)):

        @pl.when(step % 2 == side)
        def _():
            d_in_ref[0] = d_in
            out_ref[0] = out


def ffn_rule(normed, upstream, weight):
    rows, model = normed[0].shape
    share = weight.shape[1] // 3

    def moving(width, steps):
        return pl.BlockSpec((1, rows, width), lambda step: (step // steps, 0, 0))

    return pl.pallas_call(
        ffn_kernel,
        name="feed_forward",
        grid=(PART,),
        in_specs=anywhere(2 * PART + 1),
        out_specs=[moving(2 * share, 1), moving(share, 1)] + [moving(model, 2)] * 4,
        out_shape=[shaped((PART, rows, 2 * share), bf16), shaped((PART, rows, share), bf16)]
        + [shaped((PART // 2, rows, model), bf16)] * 4,
        scratch_shapes=[pltpu.VMEM((PART, rows, model), bf16)] * 2
        + [
            pltpu.VMEM(weight.shape, bf16),
            pltpu.SemaphoreType.DMA((PART,)),
            pltpu.SemaphoreType.DMA((PART,)),
            pltpu.SemaphoreType.DMA,
        ],
        compiler_params=kernel_params(),
    )(*normed, *upstream, weight)


GRAD_TILE = 256


def ffn_grads_kernel(*refs):
    normed_refs, up_refs, refs = refs[:H], refs[H : 2 * H], refs[2 * H :]
    both_refs, hidden_refs, out_ref = refs[:2], refs[2:4], refs[4]
    wide = both_refs[0].shape[1]
    normed = jnp.concatenate([ref[...] for ref in normed_refs], 0)
    d_both = jnp.concatenate([ref[...] for ref in both_refs], 0)
    out_ref[:, :wide] = contract_rows(normed, d_both).astype(bf16)
    upstream = jnp.concatenate([ref[...] for ref in up_refs], 0)
    hidden = jnp.concatenate([ref[...] for ref in hidden_refs], 0)
    out_ref[:, wide:] = contract_rows(upstream, hidden).astype(bf16)


def ffn_grads_rule(normed, upstream, d_both, hidden):
    rows, model = normed[0].shape
    d_both = [part.reshape(PART * rows, -1) for part in d_both]
    hidden = [part.reshape(PART * rows, -1) for part in hidden]
    width = d_both[0].shape[1] + hidden[0].shape[1]
    columns = pl.BlockSpec((rows, GRAD_TILE), lambda step: (0, step))
    return pl.pallas_call(
        ffn_grads_kernel,
        name="feed_forward_grads",
        grid=(model // GRAD_TILE,),
        in_specs=[columns] * (2 * H)
        + [pl.BlockSpec(part.shape, lambda step: (0, 0)) for part in (*d_both, *hidden)],
        out_specs=pl.BlockSpec((GRAD_TILE, width), lambda step: (step, 0)),
        out_shape=shaped((model, width), bf16),
        compiler_params=kernel_params(),
    )(*normed, *upstream, *d_both, *hidden)


def mixer_grads_kernel(head_ref, *refs):
    normed_refs, branch_refs, refs = refs[:H], refs[H : 2 * H], refs[2 * H :]
    d_all_ref, headed_ref, weight_ref, beta_ref, out_ref, small_ref = refs
    head = head_ref[0]
    width = WIDTH + DV
    normed = jnp.concatenate([ref[...] for ref in normed_refs], 0)
    partial = contract_rows(normed, d_all_ref[:, :width])
    out_ref[:, :width] = partial.astype(bf16)
    beta = contract_rows(normed, d_all_ref[:, width:])
    branch = jnp.concatenate([ref[...] for ref in branch_refs], 0)
    headed = jnp.concatenate([headed_ref[slot ^ head] for slot in range(H)], 0)
    out_ref[:, width:] = contract_rows(branch, headed).astype(bf16)
    weighed = jnp.sum(partial * weight_ref[:, :width].astype(f32), axis=1, keepdims=True)
    weighed = weighed + beta[:, :1] * beta_ref[:, :1].astype(f32)
    lane = lax.broadcasted_iota(jnp.int32, beta.shape, 1)
    small_ref[...] = jnp.where(lane == 0, beta, jnp.where(lane == 1, weighed, 0.0))


def mixer_grads_rule(head, normed, branch, d_all, headed, weight, beta_w):
    rows, model = branch[0].shape
    width = WIDTH + 2 * DV
    columns = pl.BlockSpec((rows, GRAD_TILE), lambda step: (0, step))
    return pl.pallas_call(
        mixer_grads_kernel,
        name="mixer_grads",
        grid=(model // GRAD_TILE,),
        in_specs=scalar()
        + [columns] * (2 * H)
        + [
            pl.BlockSpec(d_all.shape, lambda step: (0, 0)),
            pl.BlockSpec(headed.shape, lambda step: (0, 0, 0)),
            pl.BlockSpec((GRAD_TILE, width), lambda step: (step, 0)),
            pl.BlockSpec((GRAD_TILE, 128), lambda step: (step, 0)),
        ],
        out_specs=[
            pl.BlockSpec((GRAD_TILE, width), lambda step: (step, 0)),
            pl.BlockSpec((GRAD_TILE, 128), lambda step: (step, 0)),
        ],
        out_shape=[shaped((model, width), bf16), shaped((model, 128), f32)],
        compiler_params=kernel_params(),
    )(head, *normed, *branch, d_all, headed, weight, beta_w)


def d_in_kernel(d_all_ref, weight_ref, beta_ref, even_ref, odd_ref):
    width = WIDTH + DV
    total = contract_cols(d_all_ref[0, :, :width], weight_ref[:, :width])
    total = (total + contract_cols(d_all_ref[0, :, width:], beta_ref[...])).astype(bf16)
    for side, out_ref in ((0, even_ref), (1, odd_ref)):

        @pl.when(pl.program_id(0) % 2 == side)
        def _():
            out_ref[0] = total


def d_in_rule(d_all, weight, beta_w):
    _, rows, width = d_all.shape
    model = weight.shape[0]
    out = pl.BlockSpec((1, rows, model), lambda step: (step // 2, 0, 0))
    return pl.pallas_call(
        d_in_kernel,
        name="mixer_d_in",
        grid=(H,),
        in_specs=[
            pl.BlockSpec((1, rows, width), lambda step: (step, 0, 0)),
            pl.BlockSpec(weight.shape, lambda step: (0, 0)),
            pl.BlockSpec(beta_w.shape, lambda step: (0, 0)),
        ],
        out_specs=[out, out],
        out_shape=[shaped((H // 2, rows, model), bf16)] * 2,
        compiler_params=kernel_params(),
    )(d_all, weight, beta_w)


JOIN_ROWS = 32


def join_kernel(spread_ref, *out_refs):
    start = 0
    for out_ref in out_refs:
        width = out_ref.shape[1] // H
        for peer in range(H):
            piece = spread_ref[peer, :, start : start + width]
            out_ref[:, peer * width : (peer + 1) * width] = piece.astype(f32)
        start += width


def join_rule(spread, widths):
    count, rows, width = spread.shape
    return pl.pallas_call(
        join_kernel,
        name="join_heads",
        grid=(rows // JOIN_ROWS,),
        in_specs=[pl.BlockSpec((count, JOIN_ROWS, width), lambda step: (0, step, 0))],
        out_specs=[pl.BlockSpec((JOIN_ROWS, count * width), lambda step: (step, 0)) for width in widths],
        out_shape=[shaped((rows, count * width), f32) for width in widths],
        compiler_params=kernel_params(),
    )(spread)


def join_hidden_kernel(spread_ref, *out_refs):
    count, _, width = spread_ref.shape
    share = width // len(out_refs)
    total = out_refs[0].shape[1]
    for index, out_ref in enumerate(out_refs):
        for peer in range(count):
            first = peer * share
            skip = first - min(first, total - share)
            piece = spread_ref[peer, :, index * share + skip : (index + 1) * share]
            out_ref[:, first : first + share - skip] = piece.astype(f32)


def join_hidden_rule(spread, total, pieces):
    count, rows, width = spread.shape
    return pl.pallas_call(
        join_hidden_kernel,
        name="join_hidden",
        grid=(rows // JOIN_ROWS,),
        in_specs=[pl.BlockSpec((count, JOIN_ROWS, width), lambda step: (0, step, 0))],
        out_specs=[pl.BlockSpec((JOIN_ROWS, total), lambda step: (step, 0))] * pieces,
        out_shape=[shaped((rows, total), f32)] * pieces,
        compiler_params=kernel_params(),
    )(spread)


def passed_along(array, axis, by):
    peers = lax.axis_size(axis)
    pairs = [(i, i + by) for i in range(peers) if 0 <= i + by < peers]
    return lax.ppermute(array, axis, pairs)


def swapped(array, axis, bits):
    return lax.ppermute(array, axis, [(i, i ^ bits) for i in range(lax.axis_size(axis))])


def neighbours(own):
    return [own] + [swapped(own, "seq", bits) for bits in range(2, H, 2)]


def with_siblings(blocks):
    return [each for block in blocks for each in (block, swapped(block, "seq", 1))]


def gather_blocks(own):
    return with_siblings(neighbours(own))


def pair_sums(even, handed):
    sums = [even[i].astype(f32) + handed[i].astype(f32) for i in range(even.shape[0])]
    return sums[0], [each.astype(bf16) for each in sums[1:]]


def exchanged(sums):
    return [swapped(sums[i - 1], "seq", 2 * i) for i in range(1, H // 2)]


def total_of(own, received):
    for piece in received:
        own = own + piece.astype(f32)
    return own


def rms_scale(values):
    return lax.rsqrt(jnp.mean(values * values, axis=-1, keepdims=True) + 1e-05)


def rms_back(values, gain, d_normed):
    scale = rms_scale(values)
    normed = values * scale
    pulled = d_normed * gain
    d_values = scale * (pulled - normed * jnp.mean(normed * pulled, axis=-1, keepdims=True))
    return d_values, jnp.sum(d_normed * normed, axis=0)


def shards(
    inputs,
    cotangent,
    decay,
    w_query,
    w_key,
    w_value,
    w_gate_out,
    w_out,
    w_ffn_gate,
    w_ffn_up,
    w_ffn_down,
    w_beta,
    conv_weight,
    norm_in,
    norm_mid,
    norm_head,
):
    seqs, size, model = inputs.shape
    rows = seqs * size
    peers = lax.axis_size("seq")
    stages = peers // H
    groups = None
    if stages > 1:
        groups = [[stage * H + head for head in range(H)] for stage in range(stages)]
    place = lax.axis_index("seq")
    head = lax.rem(place, H)
    head_arg = head.reshape(1)
    all_rows = H * rows
    hidden_all = w_ffn_gate.shape[1]
    share = -(-hidden_all // (H * 128)) * 128

    def gather_rows(local):
        return lax.all_gather(local, "seq", axis_index_groups=groups)

    def own_columns(weight, width):
        return lax.dynamic_slice_in_dim(weight, head * width, width, axis=1)

    def own_hidden(weight):
        start = jnp.minimum(head * share, hidden_all - share)
        piece = lax.dynamic_slice_in_dim(weight, start, share, axis=1)
        lane = lax.broadcasted_iota(jnp.int32, piece.shape, 1)
        return jnp.where(lane + start >= head * share, piece, jnp.zeros_like(piece))

    def gather_weight(local):
        return lax.all_gather(local, "wt", axis=0, tiled=True)

    mixer_w = gather_weight(
        own_columns_rule(
            head_arg, (w_query, w_key, w_value, w_gate_out, w_out), (DK, DK, DV, DV, DV)
        )
    )
    ffn_w_own = jnp.concatenate(
        [own_hidden(w_ffn_gate), own_hidden(w_ffn_up), own_hidden(w_ffn_down)], axis=1
    )

    def reduce_weight(partial):
        return lax.psum_scatter(partial, "wt", scatter_dimension=0, tiled=True)

    def spread_grads(summed):
        spread = lax.all_gather(summed, "seq")
        if stages > 1:
            spread = spread.reshape((stages, H) + summed.shape).astype(f32)
            spread = jnp.sum(spread, axis=0)
        return spread

    own_in = inputs.reshape(rows, model)
    flat_in = own_in.astype(f32)
    normed_own = (flat_in * rms_scale(flat_in) * norm_in).astype(bf16)
    upstream_own = cotangent.reshape(rows, model)
    decay_rows = decay.reshape(rows, H).T
    near_in = neighbours(normed_own)
    near_in, late_upstream, ffn_w_own = lax.optimization_barrier(
        (near_in, upstream_own, ffn_w_own)
    )
    up_near = neighbours(late_upstream)
    taps = jnp.concatenate(
        [
            own_columns(conv_weight[:, : H * DK], DK),
            own_columns(conv_weight[:, H * DK : 2 * H * DK], DK),
            own_columns(conv_weight[:, 2 * H * DK :], DV),
        ],
        axis=1,
    )
    taps = jnp.pad(taps, ((0, 8 - CONV), (0, 0)))
    beta_w = jnp.pad(own_columns(w_beta, 1), ((0, 0), (0, 127)))
    own_decay = lax.all_to_all(
        decay_rows, "seq", 0, 0, axis_index_groups=groups, tiled=True
    )
    own_decay, taps, beta_w, near_in = lax.optimization_barrier((own_decay, taps, beta_w, near_in))
    normed_in, mixer_w, up_sides = lax.optimization_barrier(
        (with_siblings(near_in), mixer_w, up_near[:3])
    )
    up_near = up_sides + up_near[3:]
    ffn_w = gather_weight(ffn_w_own)
    in_width = WIDTH + DV
    out_near = neighbours(mixer_w[:, in_width:])

    gain = norm_head[None, :]

    state = jnp.zeros((seqs, DK, DV), f32)
    halo = jnp.zeros((seqs, HALO, WIDTH), bf16)
    if stages > 1:
        edges = lax.all_gather(normed_own.reshape(seqs, size, model)[:, size - HALO :], "seq")
        before = lax.dynamic_index_in_dim(edges, jnp.maximum(place - head - 1, 0), keepdims=False)
        rolled = product(before.reshape(seqs * HALO, model), mixer_w[:, :WIDTH]).astype(bf16)
        halo = jnp.where(place >= H, rolled.reshape(halo.shape), halo)
    for stage in range(stages):
        headed, *saved, ending = forward_rule(
            head_arg, normed_in, own_decay, mixer_w, beta_w, taps, gain, state, halo
        )
        run = saved.pop()
        if stage < stages - 1:
            state = passed_along(ending, "seq", H)

    headed = headed.reshape(H, rows, DV)
    headed, up_near, out_near = lax.optimization_barrier((headed, up_near, out_near))
    upstream = with_siblings(up_near)
    own_headed = lax.all_to_all(headed, "seq", 0, 0, axis_index_groups=groups, tiled=True)
    residual, normed_own = out_rule(
        head_arg, with_siblings(out_near), own_headed, own_in, norm_mid[None, :]
    )
    across = swapped(normed_own, "seq", 6)
    near, far = swapped(normed_own, "seq", 2), swapped(normed_own, "seq", 4)
    mid_first = with_siblings([normed_own, across])
    up_first, up_last = upstream[:2] + upstream[6:], upstream[2:6]
    both_first, hidden_first, d_even, d_odd, even_first, odd_first = ffn_rule(
        mid_first, up_first, ffn_w
    )
    d_odd, near, far = lax.optimization_barrier((d_odd, near, far))
    own_pair = (d_even, swapped(d_odd, "seq", 1))
    across_sum = sum(each[1].astype(f32) for each in own_pair).astype(bf16)
    mid_last, across_sum = lax.optimization_barrier((with_siblings([near, far]), across_sum))
    across_sum = swapped(across_sum, "seq", 6)
    both_last, hidden_last, d_even, d_odd, even_last, odd_last = ffn_rule(
        mid_last, up_last, ffn_w
    )
    both_last, d_odd, across_sum = lax.optimization_barrier((both_last, d_odd, across_sum))
    ffn_partial = ffn_grads_rule(
        mid_first + mid_last,
        up_first + up_last,
        (both_first, both_last),
        (hidden_first, hidden_last),
    )
    handed, ffn_partial = lax.optimization_barrier((swapped(d_odd, "seq", 1), ffn_partial))
    ffn_summed = reduce_weight(ffn_partial)
    near_sum, far_sum = ((d_even[i].astype(f32) + handed[i].astype(f32)).astype(bf16) for i in (0, 1))
    received = [swapped(near_sum, "seq", 2), swapped(far_sum, "seq", 4), across_sum]
    ffn_own, ffn_across = pair_sums(even_first, swapped(odd_first, "seq", 1))
    ffn_handed = swapped(odd_last, "seq", 1)
    ffn_sums = [
        (even_last[i].astype(f32) + ffn_handed[i].astype(f32)).astype(bf16) for i in (0, 1)
    ] + ffn_across
    received, ffn_own, ffn_sums, own_pair = lax.optimization_barrier(
        (received, ffn_own, ffn_sums, own_pair)
    )
    own_sum = sum(each[0].astype(f32) for each in own_pair)
    d_normed_mid = total_of(own_sum, received)
    d_from_mid, grad_mid = rms_back(residual, norm_mid, d_normed_mid)
    d_residual = upstream_own.astype(f32) + d_from_mid
    branch, ffn_sums, ffn_summed = lax.optimization_barrier(
        (gather_blocks(d_residual.astype(bf16)), ffn_sums, ffn_summed)
    )
    ffn_received = exchanged(ffn_sums)
    ffn_spread = spread_grads(ffn_summed)

    d_end = jnp.zeros((seqs, DK, DV), f32)
    d_after = jnp.zeros((seqs, 8, WIDTH), f32)
    for stage in range(stages):
        d_all, grad_taps, grad_gain, d_start, d_before = backward_rule(
            head_arg, branch, mixer_w, saved, run, taps, gain, halo, d_end, d_after
        )
        if stage < stages - 1:
            d_end = passed_along(d_start, "seq", -H)
            d_after = passed_along(d_before, "seq", -H)
    d_all = d_all.reshape(H, rows, -1)

    mixer_partial, narrow = mixer_grads_rule(
        head_arg, normed_in, branch, d_all.reshape(all_rows, -1), headed, mixer_w, beta_w
    )
    mixer_partial, ffn_spread, ffn_received = lax.optimization_barrier(
        (mixer_partial, ffn_spread, ffn_received)
    )
    mixer_summed = reduce_weight(mixer_partial)
    ffn_grads = join_hidden_rule(ffn_spread, hidden_all, 3)

    d_even, d_odd = d_in_rule(d_all, mixer_w, beta_w)
    own_sum, sums = pair_sums(d_even, swapped(d_odd, "seq", 1))
    received, mixer_summed, narrow, ffn_grads = lax.optimization_barrier(
        (exchanged(sums), mixer_summed, narrow, ffn_grads)
    )
    layer_out = (residual + total_of(ffn_own, ffn_received)).astype(bf16).reshape(inputs.shape)
    mixer_grads = join_rule(spread_grads(mixer_summed), [DK, DK, DV, DV, DV])
    d_normed_in = total_of(own_sum, received)
    d_from_in, _ = rms_back(flat_in, norm_in, d_normed_in)
    grad_input = (d_residual + d_from_in).reshape(inputs.shape)

    small = jnp.concatenate(
        [
            grad_taps[:CONV].reshape(-1),
            narrow[:, 0],
            grad_gain[0],
            grad_mid,
            narrow[:, 1] / norm_in,
        ]
    ).reshape(-1, 128)
    step = 1
    while step < lax.axis_size("wt"):
        small = small + swapped(small, "wt", step)
        step *= 2
    step = H
    while step < peers:
        small = small + swapped(small, "seq", step)
        step *= 2
    small = small[None]
    for bits in (1, 2, 4):
        small = jnp.concatenate([small, swapped(small, "seq", bits)], axis=0)
    small = small[jnp.arange(H) ^ head].reshape(H, -1)
    ends = []
    for bound in (CONV * WIDTH, model, DV, model, model):
        ends.append(bound + (ends[-1] if ends else 0))
    taps_part = small[:, : ends[0]].reshape(H, CONV, WIDTH)

    def joined(pieces):
        return jnp.swapaxes(pieces, 0, 1).reshape(CONV, -1)

    grad_conv = jnp.concatenate(
        [
            joined(taps_part[:, :, :DK]),
            joined(taps_part[:, :, DK : 2 * DK]),
            joined(taps_part[:, :, 2 * DK :]),
        ],
        axis=1,
    )
    grad_beta = small[:, ends[0] : ends[1]].T
    shared = jnp.sum(small[:, ends[1] :], axis=0)
    return (
        layer_out,
        grad_input,
        *mixer_grads,
        *ffn_grads,
        grad_beta,
        grad_conv,
        shared[DV + model :],
        shared[DV : DV + model],
        shared[:DV],
    )


def solution(mesh):
    rows = P("wt", "seq", None)
    cut = P("wt", None)
    in_specs = (rows,) * 3 + (cut,) * 8 + (P(),) * 5
    out_specs = (rows,) * 2 + (cut,) * 8 + (P(),) * 5
    return jax.shard_map(shards, mesh=mesh, in_specs=in_specs, out_specs=out_specs, check_vma=False)
```

```python
import jax
import jax.numpy as jnp
from jax import lax
from jax.experimental import pallas as pl
from jax.experimental.pallas import tpu as pltpu
from jax.sharding import PartitionSpec as P

H = 8
DK = 128
DV = 256
CONV = 4
HALO = 16
WIDTH = 2 * DK + DV
VMEM_LIMIT = 60 * 1024 * 1024
bf16 = jnp.bfloat16
f32 = jnp.float32


def dot(left, right, dims):
    return lax.dot_general(left, right, (dims, ((), ())), preferred_element_type=f32)


def product(left, right):
    return dot(left, right, ((1,), (0,)))


def contract_rows(left, right):
    return dot(left, right, ((0,), (0,)))


def contract_cols(left, right):
    return dot(left, right, ((1,), (1,)))


def parts(values):
    high = values.astype(bf16)
    return high, (values - high.astype(f32)).astype(bf16)


def mul(left, right):
    (lh, ll), (rh, rl) = left, right
    wide = product(jnp.concatenate([lh, ll], 1), jnp.concatenate([rh, rh], 0))
    return wide + product(lh, rl)


def mul_t(left, right):
    (lh, ll), (rh, rl) = left, right
    wide = contract_cols(jnp.concatenate([lh, ll], 1), jnp.concatenate([rh, rh], 1))
    return wide + contract_cols(lh, rl)


def cat_parts(values):
    return jnp.concatenate(parts(values), 1)


def from_cat(both):
    half = both.shape[1] // 2
    return both[:, :half], both[:, half:]


def iotas(size):
    return (
        lax.broadcasted_iota(jnp.int32, (size, size), 0),
        lax.broadcasted_iota(jnp.int32, (size, size), 1),
    )


def unit_inverses(lowers, rows, cols):
    size = rows.shape[0]
    level = 0
    eye = jnp.where(rows == cols, 1.0, 0.0)
    inverses = [eye] * len(lowers)
    while (1 << level) < size:
        together = (rows >> (level + 1)) == (cols >> (level + 1))
        corner = together & (((rows >> level) & 1) == 1) & (((cols >> level) & 1) == 0)
        blocks = [jnp.where(corner, lower, 0.0) for lower in lowers]
        if level == 0:
            inverses = [inverse - block for inverse, block in zip(inverses, blocks)]
        elif (1 << level) >= 16:
            half = 1 << level
            starts = range(half, size, 2 * half)
            below = [jnp.concatenate([i[at : at + half] for at in starts], 0) for i in inverses]
            blocks = [jnp.concatenate([b[at : at + half] for at in starts], 0) for b in blocks]
            steps = [mul(parts(b), parts(i)) for b, i in zip(blocks, inverses)]
            gap = jnp.zeros((half, size), f32)
            spread = [
                jnp.concatenate(
                    [
                        piece
                        for index in range(len(starts))
                        for piece in (gap, step[index * half : (index + 1) * half])
                    ],
                    0,
                )
                for step in steps
            ]
            steps = [low - mul(parts(low), parts(wide)) for low, wide in zip(below, spread)]
            inverses = [
                jnp.concatenate(
                    [
                        piece
                        for index, at in enumerate(starts)
                        for piece in (
                            inverse[at - half : at], step[index * half : (index + 1) * half]
                        )
                    ],
                    0,
                )
                for inverse, step in zip(inverses, steps)
            ]
        else:
            wholes = [parts(inverse) for inverse in inverses]
            steps = [mul(parts(block), whole) for block, whole in zip(blocks, wholes)]
            steps = [mul(whole, parts(step)) for step, whole in zip(steps, wholes)]
            inverses = [inverse - step for inverse, step in zip(inverses, steps)]
        level += 1
    return inverses


def conv_rows(conv_ref, halo_ref, rows_ref, taps_ref, chunk, seq, slot):
    size = conv_ref.shape[2]
    before = conv_ref[jnp.maximum(chunk - 1, 0), seq, size - HALO :, :]
    before = jnp.where(chunk == 0, halo_ref[seq], before)
    rows_ref[slot, :HALO, :] = before.astype(f32)
    rows_ref[slot, HALO:, :] = conv_ref[chunk, seq].astype(f32)
    total = None
    for tap in range(CONV):
        start = HALO - (CONV - 1) + tap
        term = rows_ref[slot, start : start + size, :] * taps_ref[tap : tap + 1, :]
        total = term if total is None else total + term
    return total


def run_row_of(run_ref, chunk, seq, seqs):
    return run_ref[pl.ds(chunk * seqs + seq, 1), :]


def decays(run_row, rows, cols):
    size = rows.shape[0]
    run_col = jnp.sum(jnp.where(rows == cols, run_row, 0.0), axis=1, keepdims=True)
    spread = jnp.where(rows >= cols, run_col - run_row, 0.0)
    decay_mat = jnp.where(rows >= cols, jnp.exp(spread), 0.0)
    last = run_row[:, size - 1 : size]
    return decay_mat, jnp.exp(run_col), jnp.exp(last - run_col)


def running_sums(values, rows, cols):
    upper = jnp.where(rows <= cols, 1.0, 0.0).astype(bf16)
    total = None
    for _ in range(3):
        part = values.astype(bf16)
        values = values - part.astype(f32)
        term = product(part, upper)
        total = term if total is None else total + term
    return total


def units_of(first, count, seqs):
    return [(first + chunk, seq) for chunk in range(count) for seq in range(seqs)]


FORWARD_CHUNKS = 4


def forward_kernel(head_ref, *refs):
    block_refs, decay_ref, refs = refs[:H], refs[H], refs[H + 1 :]
    weight_in, beta_ref, taps_ref, gain_ref, state_ref, halo_ref = refs[:6]
    outs, (run_ref, end_ref), held, refs = refs[6:14], refs[14:16], refs[16:24], refs[24:]
    headed_ref, conv_ref, gate_ref, mixed_ref, inverse_ref, scores_ref, delta_ref, starts_ref = held
    (
        block_ref, weight_ref, log_ref, rows_ref, recall_ref, target_ref, query_ref, write_ref,
        plain_ref, block_sems, weight_sem, out_sems,
    ) = refs
    chunks, seqs, size, _ = conv_ref.shape
    rows, cols = iotas(size)
    head = head_ref[0]

    weight_copy = pltpu.make_async_copy(
        weight_in.at[:, pl.ds(0, WIDTH + DV)], weight_ref, weight_sem
    )
    weight_copy.start()
    def block_copy(source, slot):
        return pltpu.make_async_copy(source, block_ref.at[slot], block_sems.at[slot])

    for slot in range(H):
        block_copy(block_refs[slot], slot).start()
    logs = jnp.log(decay_ref[...])
    for chunk in range(chunks):
        for seq in range(seqs):
            row = chunk * seqs + seq
            log_ref[row : row + 1, :] = logs[chunk : chunk + 1, seq * size : (seq + 1) * size]
    run_ref[...] = running_sums(log_ref[...], rows, cols)

    weight_copy.wait()

    def project(slot, _):
        chunk = slot ^ head
        block_copy(block_refs[0], slot).wait()
        block = block_ref[slot]
        conv = product(block, weight_ref[:, :WIDTH]).astype(bf16)
        gate = product(block, weight_ref[:, WIDTH:])
        beta = product(block, beta_ref[...])
        for seq in range(seqs):
            span = slice(seq * size, (seq + 1) * size)
            conv_ref[chunk, seq] = conv[span]
            gate_ref[chunk, seq, :, :DV] = gate[span]
            gate_ref[chunk, seq, :, DV:] = beta[span]
        return 0

    lax.fori_loop(0, H, project, 0)

    def send(index, first, count):
        span = pl.ds(first, count)
        pltpu.make_async_copy(
            held[index].at[span], outs[index].at[span], out_sems.at[index]
        ).start()

    def prepare(turn, _):
        units = units_of(turn * FORWARD_CHUNKS, FORWARD_CHUNKS, seqs)
        lowers = []

        @pl.when(turn > 0)
        def _():
            for index in (1, 2, 4, 5):
                send(index, (turn - 1) * FORWARD_CHUNKS, FORWARD_CHUNKS)

        for slot, (chunk, seq) in enumerate(units):
            summed = conv_rows(conv_ref, halo_ref, rows_ref, taps_ref, chunk, seq, slot)
            active = summed * jax.nn.sigmoid(summed)
            query = active[:, :DK]
            key = active[:, DK : 2 * DK]
            key = key * lax.rsqrt(jnp.sum(key * key, axis=1, keepdims=True) + 1e-06)
            beta = jax.nn.sigmoid(gate_ref[chunk, seq, :, DV : DV + 1])
            decay_mat, growth, fade = decays(run_row_of(run_ref, chunk, seq, seqs), rows, cols)
            target_ref[chunk, seq] = beta * active[:, 2 * DK :]
            query_ref[chunk, seq] = cat_parts(growth * query)
            write_ref[chunk, seq] = cat_parts((fade * key).T)
            recall_ref[chunk, seq] = cat_parts(beta * growth * key)
            key_parts = parts(key)
            gram = mul_t(key_parts, key_parts)
            lowers.append(jnp.where(rows > cols, beta * gram * decay_mat, 0.0))
            scores = mul_t(parts(query), key_parts) * decay_mat
            plain_ref[chunk, seq] = cat_parts(scores)
            scores_ref[chunk, seq] = cat_parts(scores.T)
        inverses = unit_inverses(lowers, rows, cols)
        for (chunk, seq), inverse in zip(units, inverses):
            inverse_parts = parts(inverse)
            recall = mul(inverse_parts, from_cat(recall_ref[chunk, seq]))
            recall_ref[chunk, seq] = cat_parts(recall)
            target_ref[chunk, seq] = mul(inverse_parts, parts(target_ref[chunk, seq]))
            inverse_ref[chunk, seq] = cat_parts(inverse.T)
        return 0

    lax.fori_loop(0, chunks // FORWARD_CHUNKS, prepare, 0)

    def advance(chunk, states):
        following = []

        @pl.when(chunk == 0)
        def _():
            for index in (1, 2, 4, 5):
                send(index, chunks - FORWARD_CHUNKS, FORWARD_CHUNKS)

        @pl.when(chunk > 0)
        def _():
            for index in (0, 3, 6, 7):
                send(index, chunk - 1, 1)

        for seq in range(seqs):
            state = states[seq]
            starts_ref[chunk, seq] = state
            state_parts = parts(state)
            delta = target_ref[chunk, seq] - mul(from_cat(recall_ref[chunk, seq]), state_parts)
            delta_parts = parts(delta)
            total = jnp.exp(run_row_of(run_ref, chunk, seq, seqs)[:, size - 1 : size])
            following.append(
                total * state + mul(from_cat(write_ref[chunk, seq]), delta_parts)
            )
            delta_ref[chunk, seq] = delta
            read = mul(from_cat(query_ref[chunk, seq]), state_parts)
            read = read + mul(from_cat(plain_ref[chunk, seq]), delta_parts)
            mixed_ref[chunk, seq] = read
            scale = lax.rsqrt(jnp.mean(read * read, axis=1, keepdims=True) + 1e-05)
            gate = gate_ref[chunk, seq, :, :DV]
            headed = read * scale * gain_ref[...] * (gate * jax.nn.sigmoid(gate))
            headed_ref[chunk, seq] = headed.astype(bf16)
        return tuple(following)

    final = lax.fori_loop(0, chunks, advance, tuple(state_ref[seq] for seq in range(seqs)))
    for seq in range(seqs):
        end_ref[seq] = final[seq]
    for index in (0, 3, 6, 7):
        send(index, chunks - 1, 1)
    for index in range(len(held)):
        pltpu.make_async_copy(held[index], outs[index], out_sems.at[index]).wait()


BACKWARD_CHUNKS = 2


def backward_kernel(head_ref, *refs):
    branch_refs, weight_in, refs = refs[:H], refs[H], refs[H + 1 :]
    saved, refs = refs[:7], refs[7:]
    run_ref, taps_ref, gain_ref, halo_ref, d_end_ref, d_after_ref = refs[:6]
    d_all_out, grad_taps_ref, grad_gain_ref, d_start_ref, d_before_ref = refs[6:11]
    branch_ref, weight_ref, held, refs = refs[11], refs[12], refs[13:20], refs[20:]
    conv_ref, gate_ref, mixed_ref, inverse_ref, scores_ref, delta_ref, starts_ref = held
    (
        rows_ref, d_headed_ref, hold_ref, carry_ref, base_ref, back_ref, d_target_ref, d_state_ref,
        d_conv_ref, d_all_ref, slope_ref, active_ref, column_ref,
        block_sems, weight_sem, saved_sems, out_sem,
    ) = refs
    chunks, seqs, size, _ = conv_ref.shape
    rows, cols = iotas(size)
    head = head_ref[0]

    weight_copy = pltpu.make_async_copy(
        weight_in.at[:, pl.ds(WIDTH + DV, DV)], weight_ref, weight_sem
    )
    weight_copy.start()

    def block_copy(source, slot):
        return pltpu.make_async_copy(source, branch_ref.at[slot], block_sems.at[slot])

    for slot in range(H):
        block_copy(branch_refs[slot], slot).start()

    def saved_copy(index, first, count, turn):
        span = pl.ds(first, count)
        return pltpu.make_async_copy(
            saved[index].at[span], held[index].at[span], saved_sems.at[index, turn]
        )

    early = len(saved) - 2

    def turn_copy(index, turn):
        return saved_copy(index, turn * BACKWARD_CHUNKS, BACKWARD_CHUNKS, turn)


    lane = lax.broadcasted_iota(jnp.int32, (size, 128), 1)
    grad_gain_ref[...] = jnp.zeros_like(grad_gain_ref)
    grad_taps_ref[...] = jnp.zeros_like(grad_taps_ref)

    weight_copy.wait()

    def project(slot, _):
        @pl.when(slot == 1)
        def _():
            for turn in range(chunks // BACKWARD_CHUNKS):
                for index in range(early):
                    turn_copy(index, turn).start()

        block_copy(branch_refs[0], slot).wait()
        d_headed = product(branch_ref[slot], weight_ref[...])
        for seq in range(seqs):
            d_headed_ref[slot ^ head, seq] = d_headed[seq * size : (seq + 1) * size]
        return 0

    lax.fori_loop(0, H, project, 0)
    for index in range(early, len(saved)):
        saved_copy(index, 0, chunks, 0).start()

    def prepare(turn, _):
        units = units_of(turn * BACKWARD_CHUNKS, BACKWARD_CHUNKS, seqs)
        for index in range(early):
            turn_copy(index, turn).wait()
        for chunk, seq in units:
            unit = chunk * seqs + seq
            summed = conv_rows(conv_ref, halo_ref, rows_ref, taps_ref, chunk, seq, unit)
            logistic = jax.nn.sigmoid(summed)
            active = summed * logistic
            slope_ref[unit] = logistic * (1.0 + summed * (1.0 - logistic))
            query = active[:, :DK]
            raw = active[:, DK : 2 * DK]
            shrink = lax.rsqrt(jnp.sum(raw * raw, axis=1, keepdims=True) + 1e-06)
            key = raw * shrink
            active_ref[unit, :, :DK] = query
            active_ref[unit, :, DK : 2 * DK] = key
            active_ref[unit, :, 2 * DK :] = active[:, 2 * DK :]
            beta = jax.nn.sigmoid(gate_ref[chunk, seq, :, DV : DV + 1])
            column_ref[unit] = jnp.where(lane == 0, shrink, beta)
            _, growth, fade = decays(run_row_of(run_ref, chunk, seq, seqs), rows, cols)
            mixed = mixed_ref[chunk, seq]
            d_headed = d_headed_ref[chunk, seq]
            gate = gate_ref[chunk, seq, :, :DV]
            logistic = jax.nn.sigmoid(gate)
            scale = lax.rsqrt(jnp.mean(mixed * mixed, axis=1, keepdims=True) + 1e-05)
            normed = mixed * scale
            swish = gate * logistic
            inner = d_headed * gain_ref[...] * swish
            d_mixed = scale * (inner - normed * jnp.mean(normed * inner, axis=1, keepdims=True))
            grad_gain_ref[...] += jnp.sum(d_headed * normed * swish, axis=0, keepdims=True)
            d_gate = d_headed * gain_ref[...] * normed * logistic * (1.0 + gate * (1.0 - logistic))
            d_all_ref[chunk ^ head, seq, :, WIDTH : WIDTH + DV] = d_gate.astype(bf16)
            d_headed_ref[chunk, seq] = d_mixed
            d_mixed_parts = parts(d_mixed)
            inverse_parts = from_cat(inverse_ref[chunk, seq])
            scored = mul(from_cat(scores_ref[chunk, seq]), d_mixed_parts)
            base_ref[chunk, seq] = mul(inverse_parts, parts(scored))
            hold_ref[chunk, seq] = cat_parts(mul(inverse_parts, parts(fade * key)))
            back_ref[chunk, seq] = mul(parts((growth * query).T), d_mixed_parts)
            carry_ref[chunk, seq] = cat_parts((beta * growth * key).T)
        return 0

    lax.fori_loop(0, chunks // BACKWARD_CHUNKS, prepare, 0)

    def advance(step, d_states):
        chunk = chunks - 1 - step
        following = []
        for seq in range(seqs):
            d_state = d_states[seq]
            d_state_ref[chunk, seq] = d_state
            d_target = base_ref[chunk, seq] + mul(from_cat(hold_ref[chunk, seq]), parts(d_state))
            d_target_ref[chunk, seq] = d_target
            total = jnp.exp(run_row_of(run_ref, chunk, seq, seqs)[:, size - 1 : size])
            back = mul(from_cat(carry_ref[chunk, seq]), parts(d_target))
            following.append(total * d_state + back_ref[chunk, seq] - back)
        return tuple(following)

    first = lax.fori_loop(0, chunks, advance, tuple(d_end_ref[seq] for seq in range(seqs)))
    for seq in range(seqs):
        d_start_ref[seq] = first[seq]
        d_conv_ref[seq, size:, :] = d_after_ref[seq]
    for index in range(early, len(saved)):
        saved_copy(index, 0, chunks, 0).wait()

    def send(chunk):
        slot = chunk ^ head
        pltpu.make_async_copy(d_all_ref.at[slot], d_all_out.at[slot], out_sem).start()

    def finish(turn, _):
        units = [
            (chunks - 1 - turn * BACKWARD_CHUNKS - back, seq)
            for back in range(BACKWARD_CHUNKS)
            for seq in range(seqs)
        ]

        @pl.when(turn > 0)
        def _():
            for back in range(BACKWARD_CHUNKS):
                send(chunks - 1 - (turn - 1) * BACKWARD_CHUNKS - back)

        for chunk, seq in units:
            unit = chunk * seqs + seq
            slope = slope_ref[unit]
            query = active_ref[unit, :, :DK]
            key = active_ref[unit, :, DK : 2 * DK]
            value = active_ref[unit, :, 2 * DK :]
            shrink = column_ref[unit, :, 0:1]
            beta = column_ref[unit, :, 1:2]
            decay_mat, growth, fade = decays(run_row_of(run_ref, chunk, seq, seqs), rows, cols)
            key_parts = parts(key)
            gram = mul_t(key_parts, key_parts) * decay_mat
            d_target = d_target_ref[chunk, seq]
            delta_parts = parts(delta_ref[chunk, seq])
            start_parts = parts(starts_ref[chunk, seq])
            both = parts(jnp.concatenate([d_target, d_headed_ref[chunk, seq]], 0))
            on_delta = mul_t(both, delta_parts)
            on_state = mul_t(both, start_parts)
            d_lower = jnp.where(rows > cols, -on_delta[:size], 0.0)
            d_scores = on_delta[size:] * decay_mat
            through = on_state[:size]
            d_gram = d_lower * decay_mat * beta
            d_query = growth * on_state[size:] + mul(parts(d_scores), key_parts)
            d_key = mul(parts(d_scores.T), parts(query))
            d_key = d_key + mul(parts(d_gram + d_gram.T), key_parts)
            d_key = d_key + fade * mul_t(delta_parts, parts(d_state_ref[chunk, seq]))
            d_key = d_key - (beta * growth) * through
            d_beta = (
                jnp.sum(d_target * value, axis=1, keepdims=True)
                - growth * jnp.sum(key * through, axis=1, keepdims=True)
                + jnp.sum(d_lower * gram, axis=1, keepdims=True)
            )
            d_raw = shrink * (d_key - key * jnp.sum(key * d_key, axis=1, keepdims=True))
            d_conv = jnp.concatenate([d_query, d_raw, beta * d_target], 1) * slope
            d_conv_ref[seq, :size, :] = d_conv
            d_in = None
            for tap in range(CONV):
                start = HALO - (CONV - 1) + tap
                grad_taps_ref[tap : tap + 1, :] += jnp.sum(
                    d_conv * rows_ref[unit, start : start + size, :], axis=0, keepdims=True
                )
                shift = CONV - 1 - tap
                term = d_conv_ref[seq, shift : shift + size, :] * taps_ref[tap : tap + 1, :]
                d_in = term if d_in is None else d_in + term
            d_conv_ref[seq, size:, :] = d_conv[:8, :]
            d_all_ref[chunk ^ head, seq, :, :WIDTH] = d_in.astype(bf16)
            d_logit = d_beta * beta * (1.0 - beta)
            d_all_ref[chunk ^ head, seq, :, WIDTH + DV :] = jnp.where(
                lane == 0, d_logit, 0.0
            ).astype(bf16)
        return 0

    lax.fori_loop(0, chunks // BACKWARD_CHUNKS, finish, 0)
    for seq in range(seqs):
        d_before_ref[seq] = d_conv_ref[seq, size:, :]
    for chunk in range(BACKWARD_CHUNKS):
        send(chunk)
    pltpu.make_async_copy(d_all_ref, d_all_out, out_sem).wait()


def whole(count):
    return [pl.BlockSpec(memory_space=pltpu.VMEM)] * count


def scalar():
    return [pl.BlockSpec(memory_space=pltpu.SMEM)]


shaped = jax.ShapeDtypeStruct


def cost(flops):
    return pl.CostEstimate(flops=flops, bytes_accessed=0, transcendentals=0)


def kernel_params():
    return pltpu.CompilerParams(vmem_limit_bytes=VMEM_LIMIT)


def own_columns_kernel(head_ref, *refs):
    out_ref = refs[-1]
    start = 0
    for ref in refs[:-1]:
        width = ref.shape[1]
        out_ref[:, start : start + width] = ref[...]
        start += width


def own_columns_rule(head, weights, widths):
    rows = weights[0].shape[0]
    total = sum(widths)
    return pl.pallas_call(
        own_columns_kernel,
        name="own_columns",
        grid_spec=pltpu.PrefetchScalarGridSpec(
            num_scalar_prefetch=1,
            grid=(1,),
            in_specs=[
                pl.BlockSpec((rows, width), lambda step, head_ref: (0, head_ref[0]))
                for width in widths
            ],
            out_specs=pl.BlockSpec((rows, total), lambda step, head_ref: (0, 0)),
        ),
        out_shape=shaped((rows, total), bf16),
        compiler_params=kernel_params(),
    )(head, *weights)


def anywhere(count):
    return [pl.BlockSpec(memory_space=pltpu.HBM)] * count


def forward_rule(head, blocks, own_decay, weight, beta_w, taps, gain, state, halo):
    rows, model = blocks[0].shape
    seqs = state.shape[0]
    size = rows // seqs
    lead = (H, seqs)
    held = [
        (lead + (size, DV), bf16),
        (lead + (size, WIDTH), bf16),
        (lead + (size, DV + 128), f32),
        (lead + (size, DV), f32),
        (lead + (size, 2 * size), bf16),
        (lead + (size, 2 * size), bf16),
        (lead + (size, DV), f32),
        (lead + (DK, DV), f32),
    ]
    return pl.pallas_call(
        forward_kernel,
        name="mixer_forward",
        out_shape=[shaped(*item) for item in held]
        + [shaped((H * seqs, size), f32), shaped((seqs, DK, DV), f32)],
        in_specs=scalar() + anywhere(H) + whole(1) + anywhere(1) + whole(5),
        out_specs=anywhere(8) + whole(2),
        scratch_shapes=[pltpu.VMEM(*item) for item in held]
        + [
            pltpu.VMEM((H, rows, model), bf16),
            pltpu.VMEM((model, WIDTH + DV), bf16),
            pltpu.VMEM((H * seqs, size), f32),
            pltpu.VMEM((FORWARD_CHUNKS * seqs, HALO + size, WIDTH), f32),
            pltpu.VMEM(lead + (size, 2 * DK), bf16),
            pltpu.VMEM(lead + (size, DV), f32),
            pltpu.VMEM(lead + (size, 2 * DK), bf16),
            pltpu.VMEM(lead + (DK, 2 * size), bf16),
            pltpu.VMEM(lead + (size, 2 * size), bf16),
            pltpu.SemaphoreType.DMA((H,)),
            pltpu.SemaphoreType.DMA,
            pltpu.SemaphoreType.DMA((8,)),
        ],
        compiler_params=kernel_params(),
    )(head, *blocks, own_decay, weight, beta_w, taps, gain, state, halo)


def backward_rule(head, branch, weight, saved, run, taps, gain, halo, d_end, d_after):
    rows, model = branch[0].shape
    seqs = d_end.shape[0]
    size = rows // seqs
    lead = (H, seqs)
    return pl.pallas_call(
        backward_kernel,
        name="mixer_backward",
        out_shape=(
            shaped(lead + (size, WIDTH + DV + 128), bf16),
            shaped((8, WIDTH), f32),
            shaped((1, DV), f32),
            shaped((seqs, DK, DV), f32),
            shaped((seqs, 8, WIDTH), f32),
        ),
        in_specs=scalar() + anywhere(H + 8) + whole(6),
        out_specs=tuple(anywhere(1) + whole(4)),
        scratch_shapes=[
            pltpu.VMEM((H, rows, model), bf16),
            pltpu.VMEM((model, DV), bf16),
        ]
        + [pltpu.VMEM(item.shape, item.dtype) for item in saved]
        + [
            pltpu.VMEM((H * seqs, HALO + size, WIDTH), f32),
            pltpu.VMEM(lead + (size, DV), f32),
            pltpu.VMEM(lead + (size, 2 * DK), bf16),
            pltpu.VMEM(lead + (DK, 2 * size), bf16),
            pltpu.VMEM(lead + (size, DV), f32),
            pltpu.VMEM(lead + (DK, DV), f32),
            pltpu.VMEM(lead + (size, DV), f32),
            pltpu.VMEM(lead + (DK, DV), f32),
            pltpu.VMEM((seqs, size + 8, WIDTH), f32),
            pltpu.VMEM(lead + (size, WIDTH + DV + 128), bf16),
            pltpu.VMEM((H * seqs, size, WIDTH), f32),
            pltpu.VMEM((H * seqs, size, WIDTH), f32),
            pltpu.VMEM((H * seqs, size, 128), f32),
            pltpu.SemaphoreType.DMA((H,)),
            pltpu.SemaphoreType.DMA,
            pltpu.SemaphoreType.DMA((7, H // BACKWARD_CHUNKS)),
            pltpu.SemaphoreType.DMA,
        ],
        compiler_params=kernel_params(),
    )(head, *branch, weight, *saved, run, taps, gain, halo, d_end, d_after)


def out_kernel(head_ref, *refs):
    block_refs, refs = refs[:H], refs[H:]
    headed_ref, inputs_ref, gain_ref, residual_ref, normed_ref, weight_ref, sems = refs
    head = head_ref[0]

    def block_copy(source, slot):
        return pltpu.make_async_copy(source, weight_ref.at[slot], sems.at[slot])

    for slot in range(H):
        block_copy(block_refs[slot], slot).start()
    residual_ref[...] = inputs_ref[...].astype(f32)

    def add_heads(pair, _):
        slots = (2 * pair, 2 * pair + 1)
        for slot in slots:
            block_copy(block_refs[0], slot).wait()
        headed = jnp.concatenate([headed_ref[slot ^ head] for slot in slots], 1)
        weight = jnp.concatenate([weight_ref[slot] for slot in slots], 1)
        residual_ref[...] += contract_cols(headed, weight)
        return 0

    lax.fori_loop(0, H // 2, add_heads, 0)
    total = residual_ref[...]
    scale = lax.rsqrt(jnp.mean(total * total, axis=1, keepdims=True) + 1e-05)
    normed_ref[...] = (total * scale * gain_ref[...]).astype(bf16)


def out_rule(head, blocks, headed, inputs, gain):
    return pl.pallas_call(
        out_kernel,
        name="out_projection",
        out_shape=(shaped(inputs.shape, f32), shaped(inputs.shape, bf16)),
        in_specs=scalar() + anywhere(H) + whole(3),
        out_specs=tuple(whole(2)),
        scratch_shapes=[
            pltpu.VMEM((H,) + blocks[0].shape, bf16),
            pltpu.SemaphoreType.DMA((H,)),
        ],
        compiler_params=kernel_params(),
    )(head, *blocks, headed, inputs, gain)


PART = H // 2


def ffn_kernel(*refs):
    normed_refs, up_refs, refs = refs[:PART], refs[PART : 2 * PART], refs[2 * PART :]
    weight_in, d_both_ref, hidden_ref, d_even_ref, d_odd_ref, even_ref, odd_ref = refs[:7]
    normed_all_ref, up_all_ref, weight_ref, normed_sems, up_sems, weight_sem = refs[7:]
    share = weight_ref.shape[1] // 3
    step = pl.program_id(0)

    def copy_of(source, target, sems, slot):
        return pltpu.make_async_copy(source, target.at[slot], sems.at[slot])

    def start_slot(slot):
        copy_of(normed_refs[slot], normed_all_ref, normed_sems, slot).start()
        copy_of(up_refs[slot], up_all_ref, up_sems, slot).start()

    @pl.when(step == 0)
    def _():
        weight_copy = pltpu.make_async_copy(weight_in, weight_ref, weight_sem)
        weight_copy.start()
        start_slot(0)
        weight_copy.wait()

    for later in range(1, PART):

        @pl.when(step == later - 1)
        def _():
            start_slot(later)

    slot = step
    copy_of(normed_refs[0], normed_all_ref, normed_sems, slot).wait()
    copy_of(up_refs[0], up_all_ref, up_sems, slot).wait()
    both = product(normed_all_ref[slot], weight_ref[:, : 2 * share])
    d_hidden = product(up_all_ref[slot], weight_ref[:, 2 * share :])
    gate, up = both[:, :share], both[:, share:]
    logistic = jax.nn.sigmoid(gate)
    swish = gate * logistic
    hidden = (swish * up).astype(bf16)
    hidden_ref[0] = hidden
    d_gate = (d_hidden * up * logistic * (1.0 + gate * (1.0 - logistic))).astype(bf16)
    d_up = (d_hidden * swish).astype(bf16)
    d_both = jnp.concatenate([d_gate, d_up], 1)
    d_both_ref[0] = d_both
    d_in = contract_cols(d_both, weight_ref[:, : 2 * share]).astype(bf16)
    out = contract_cols(hidden, weight_ref[:, 2 * share :]).astype(bf16)
    for side, d_in_ref, out_ref in ((0, d_even_ref, even_ref), (1, d_odd_ref, odd_ref)):

        @pl.when(step % 2 == side)
        def _():
            d_in_ref[0] = d_in
            out_ref[0] = out


def ffn_rule(normed, upstream, weight):
    rows, model = normed[0].shape
    share = weight.shape[1] // 3

    def moving(width, steps):
        return pl.BlockSpec((1, rows, width), lambda step: (step // steps, 0, 0))

    return pl.pallas_call(
        ffn_kernel,
        name="feed_forward",
        grid=(PART,),
        in_specs=anywhere(2 * PART + 1),
        out_specs=[moving(2 * share, 1), moving(share, 1)] + [moving(model, 2)] * 4,
        out_shape=[shaped((PART, rows, 2 * share), bf16), shaped((PART, rows, share), bf16)]
        + [shaped((PART // 2, rows, model), bf16)] * 4,
        scratch_shapes=[pltpu.VMEM((PART, rows, model), bf16)] * 2
        + [
            pltpu.VMEM(weight.shape, bf16),
            pltpu.SemaphoreType.DMA((PART,)),
            pltpu.SemaphoreType.DMA((PART,)),
            pltpu.SemaphoreType.DMA,
        ],
        compiler_params=kernel_params(),
    )(*normed, *upstream, weight)


GRAD_TILE = 256


def ffn_grads_kernel(*refs):
    normed_refs, up_refs, refs = refs[:H], refs[H : 2 * H], refs[2 * H :]
    both_refs, hidden_refs, out_ref = refs[:2], refs[2:4], refs[4]
    wide = both_refs[0].shape[1]
    normed = jnp.concatenate([ref[...] for ref in normed_refs], 0)
    d_both = jnp.concatenate([ref[...] for ref in both_refs], 0)
    out_ref[:, :wide] = contract_rows(normed, d_both).astype(bf16)
    upstream = jnp.concatenate([ref[...] for ref in up_refs], 0)
    hidden = jnp.concatenate([ref[...] for ref in hidden_refs], 0)
    out_ref[:, wide:] = contract_rows(upstream, hidden).astype(bf16)


def ffn_grads_rule(normed, upstream, d_both, hidden):
    rows, model = normed[0].shape
    d_both = [part.reshape(PART * rows, -1) for part in d_both]
    hidden = [part.reshape(PART * rows, -1) for part in hidden]
    width = d_both[0].shape[1] + hidden[0].shape[1]
    columns = pl.BlockSpec((rows, GRAD_TILE), lambda step: (0, step))
    return pl.pallas_call(
        ffn_grads_kernel,
        name="feed_forward_grads",
        grid=(model // GRAD_TILE,),
        in_specs=[columns] * (2 * H)
        + [pl.BlockSpec(part.shape, lambda step: (0, 0)) for part in (*d_both, *hidden)],
        out_specs=pl.BlockSpec((GRAD_TILE, width), lambda step: (step, 0)),
        out_shape=shaped((model, width), bf16),
        compiler_params=kernel_params(),
    )(*normed, *upstream, *d_both, *hidden)


def mixer_grads_kernel(head_ref, *refs):
    normed_refs, branch_refs, refs = refs[:H], refs[H : 2 * H], refs[2 * H :]
    d_all_ref, headed_ref, weight_ref, beta_ref, out_ref, small_ref = refs
    head = head_ref[0]
    width = WIDTH + DV
    normed = jnp.concatenate([ref[...] for ref in normed_refs], 0)
    partial = contract_rows(normed, d_all_ref[:, :width])
    out_ref[:, :width] = partial.astype(bf16)
    beta = contract_rows(normed, d_all_ref[:, width:])
    branch = jnp.concatenate([ref[...] for ref in branch_refs], 0)
    headed = jnp.concatenate([headed_ref[slot ^ head] for slot in range(H)], 0)
    out_ref[:, width:] = contract_rows(branch, headed).astype(bf16)
    weighed = jnp.sum(partial * weight_ref[:, :width].astype(f32), axis=1, keepdims=True)
    weighed = weighed + beta[:, :1] * beta_ref[:, :1].astype(f32)
    lane = lax.broadcasted_iota(jnp.int32, beta.shape, 1)
    small_ref[...] = jnp.where(lane == 0, beta, jnp.where(lane == 1, weighed, 0.0))


def mixer_grads_rule(head, normed, branch, d_all, headed, weight, beta_w):
    rows, model = branch[0].shape
    width = WIDTH + 2 * DV
    columns = pl.BlockSpec((rows, GRAD_TILE), lambda step: (0, step))
    return pl.pallas_call(
        mixer_grads_kernel,
        name="mixer_grads",
        grid=(model // GRAD_TILE,),
        in_specs=scalar()
        + [columns] * (2 * H)
        + [
            pl.BlockSpec(d_all.shape, lambda step: (0, 0)),
            pl.BlockSpec(headed.shape, lambda step: (0, 0, 0)),
            pl.BlockSpec((GRAD_TILE, width), lambda step: (step, 0)),
            pl.BlockSpec((GRAD_TILE, 128), lambda step: (step, 0)),
        ],
        out_specs=[
            pl.BlockSpec((GRAD_TILE, width), lambda step: (step, 0)),
            pl.BlockSpec((GRAD_TILE, 128), lambda step: (step, 0)),
        ],
        out_shape=[shaped((model, width), bf16), shaped((model, 128), f32)],
        compiler_params=kernel_params(),
    )(head, *normed, *branch, d_all, headed, weight, beta_w)


def d_in_kernel(d_all_ref, weight_ref, beta_ref, even_ref, odd_ref):
    width = WIDTH + DV
    total = contract_cols(d_all_ref[0, :, :width], weight_ref[:, :width])
    total = (total + contract_cols(d_all_ref[0, :, width:], beta_ref[...])).astype(bf16)
    for side, out_ref in ((0, even_ref), (1, odd_ref)):

        @pl.when(pl.program_id(0) % 2 == side)
        def _():
            out_ref[0] = total


def d_in_rule(d_all, weight, beta_w):
    _, rows, width = d_all.shape
    model = weight.shape[0]
    out = pl.BlockSpec((1, rows, model), lambda step: (step // 2, 0, 0))
    return pl.pallas_call(
        d_in_kernel,
        name="mixer_d_in",
        grid=(H,),
        in_specs=[
            pl.BlockSpec((1, rows, width), lambda step: (step, 0, 0)),
            pl.BlockSpec(weight.shape, lambda step: (0, 0)),
            pl.BlockSpec(beta_w.shape, lambda step: (0, 0)),
        ],
        out_specs=[out, out],
        out_shape=[shaped((H // 2, rows, model), bf16)] * 2,
        compiler_params=kernel_params(),
    )(d_all, weight, beta_w)


JOIN_ROWS = 32


def join_kernel(spread_ref, *out_refs):
    start = 0
    for out_ref in out_refs:
        width = out_ref.shape[1] // H
        for peer in range(H):
            piece = spread_ref[peer, :, start : start + width]
            out_ref[:, peer * width : (peer + 1) * width] = piece.astype(f32)
        start += width


def join_rule(spread, widths):
    count, rows, width = spread.shape
    return pl.pallas_call(
        join_kernel,
        name="join_heads",
        grid=(rows // JOIN_ROWS,),
        in_specs=[pl.BlockSpec((count, JOIN_ROWS, width), lambda step: (0, step, 0))],
        out_specs=[pl.BlockSpec((JOIN_ROWS, count * width), lambda step: (step, 0)) for width in widths],
        out_shape=[shaped((rows, count * width), f32) for width in widths],
        compiler_params=kernel_params(),
    )(spread)


def join_hidden_kernel(spread_ref, *out_refs):
    count, _, width = spread_ref.shape
    share = width // len(out_refs)
    total = out_refs[0].shape[1]
    for index, out_ref in enumerate(out_refs):
        for peer in range(count):
            first = peer * share
            skip = first - min(first, total - share)
            piece = spread_ref[peer, :, index * share + skip : (index + 1) * share]
            out_ref[:, first : first + share - skip] = piece.astype(f32)


def join_hidden_rule(spread, total, pieces):
    count, rows, width = spread.shape
    return pl.pallas_call(
        join_hidden_kernel,
        name="join_hidden",
        grid=(rows // JOIN_ROWS,),
        in_specs=[pl.BlockSpec((count, JOIN_ROWS, width), lambda step: (0, step, 0))],
        out_specs=[pl.BlockSpec((JOIN_ROWS, total), lambda step: (step, 0))] * pieces,
        out_shape=[shaped((rows, total), f32)] * pieces,
        compiler_params=kernel_params(),
    )(spread)


def passed_along(array, axis, by):
    peers = lax.axis_size(axis)
    pairs = [(i, i + by) for i in range(peers) if 0 <= i + by < peers]
    return lax.ppermute(array, axis, pairs)


def swapped(array, axis, bits):
    return lax.ppermute(array, axis, [(i, i ^ bits) for i in range(lax.axis_size(axis))])


def neighbours(own):
    return [own] + [swapped(own, "seq", bits) for bits in range(2, H, 2)]


def with_siblings(blocks):
    return [each for block in blocks for each in (block, swapped(block, "seq", 1))]


def gather_blocks(own):
    return with_siblings(neighbours(own))


def pair_sums(even, handed):
    sums = [even[i].astype(f32) + handed[i].astype(f32) for i in range(even.shape[0])]
    return sums[0], [each.astype(bf16) for each in sums[1:]]


def exchanged(sums):
    return [swapped(sums[i - 1], "seq", 2 * i) for i in range(1, H // 2)]


def total_of(own, received):
    for piece in received:
        own = own + piece.astype(f32)
    return own


def rms_scale(values):
    return lax.rsqrt(jnp.mean(values * values, axis=-1, keepdims=True) + 1e-05)


def rms_back(values, gain, d_normed):
    scale = rms_scale(values)
    normed = values * scale
    pulled = d_normed * gain
    d_values = scale * (pulled - normed * jnp.mean(normed * pulled, axis=-1, keepdims=True))
    return d_values, jnp.sum(d_normed * normed, axis=0)


def shards(
    inputs,
    cotangent,
    decay,
    w_query,
    w_key,
    w_value,
    w_gate_out,
    w_out,
    w_ffn_gate,
    w_ffn_up,
    w_ffn_down,
    w_beta,
    conv_weight,
    norm_in,
    norm_mid,
    norm_head,
):
    seqs, size, model = inputs.shape
    rows = seqs * size
    peers = lax.axis_size("seq")
    stages = peers // H
    groups = None
    if stages > 1:
        groups = [[stage * H + head for head in range(H)] for stage in range(stages)]
    place = lax.axis_index("seq")
    head = lax.rem(place, H)
    head_arg = head.reshape(1)
    all_rows = H * rows
    hidden_all = w_ffn_gate.shape[1]
    share = -(-hidden_all // (H * 128)) * 128

    def gather_rows(local):
        return lax.all_gather(local, "seq", axis_index_groups=groups)

    def own_columns(weight, width):
        return lax.dynamic_slice_in_dim(weight, head * width, width, axis=1)

    def own_hidden(weight):
        start = jnp.minimum(head * share, hidden_all - share)
        piece = lax.dynamic_slice_in_dim(weight, start, share, axis=1)
        lane = lax.broadcasted_iota(jnp.int32, piece.shape, 1)
        return jnp.where(lane + start >= head * share, piece, jnp.zeros_like(piece))

    def gather_weight(local):
        return lax.all_gather(local, "wt", axis=0, tiled=True)

    mixer_w = gather_weight(
        own_columns_rule(
            head_arg, (w_query, w_key, w_value, w_gate_out, w_out), (DK, DK, DV, DV, DV)
        )
    )
    ffn_w_own = jnp.concatenate(
        [own_hidden(w_ffn_gate), own_hidden(w_ffn_up), own_hidden(w_ffn_down)], axis=1
    )

    def reduce_weight(partial):
        return lax.psum_scatter(partial, "wt", scatter_dimension=0, tiled=True)

    def spread_grads(summed):
        spread = lax.all_gather(summed, "seq")
        if stages > 1:
            spread = spread.reshape((stages, H) + summed.shape).astype(f32)
            spread = jnp.sum(spread, axis=0)
        return spread

    own_in = inputs.reshape(rows, model)
    flat_in = own_in.astype(f32)
    normed_own = (flat_in * rms_scale(flat_in) * norm_in).astype(bf16)
    upstream_own = cotangent.reshape(rows, model)
    decay_rows = decay.reshape(rows, H).T
    near_in = neighbours(normed_own)
    near_in, late_upstream, ffn_w_own = lax.optimization_barrier(
        (near_in, upstream_own, ffn_w_own)
    )
    up_near = neighbours(late_upstream)
    taps = jnp.concatenate(
        [
            own_columns(conv_weight[:, : H * DK], DK),
            own_columns(conv_weight[:, H * DK : 2 * H * DK], DK),
            own_columns(conv_weight[:, 2 * H * DK :], DV),
        ],
        axis=1,
    )
    taps = jnp.pad(taps, ((0, 8 - CONV), (0, 0)))
    beta_w = jnp.pad(own_columns(w_beta, 1), ((0, 0), (0, 127)))
    own_decay = lax.all_to_all(
        decay_rows, "seq", 0, 0, axis_index_groups=groups, tiled=True
    )
    own_decay, taps, beta_w, near_in = lax.optimization_barrier((own_decay, taps, beta_w, near_in))
    normed_in, mixer_w, up_sides = lax.optimization_barrier(
        (with_siblings(near_in), mixer_w, up_near[:3])
    )
    up_near = up_sides + up_near[3:]
    ffn_w = gather_weight(ffn_w_own)
    in_width = WIDTH + DV
    out_near = neighbours(mixer_w[:, in_width:])

    gain = norm_head[None, :]

    state = jnp.zeros((seqs, DK, DV), f32)
    halo = jnp.zeros((seqs, HALO, WIDTH), bf16)
    if stages > 1:
        edges = lax.all_gather(normed_own.reshape(seqs, size, model)[:, size - HALO :], "seq")
        before = lax.dynamic_index_in_dim(edges, jnp.maximum(place - head - 1, 0), keepdims=False)
        rolled = product(before.reshape(seqs * HALO, model), mixer_w[:, :WIDTH]).astype(bf16)
        halo = jnp.where(place >= H, rolled.reshape(halo.shape), halo)
    for stage in range(stages):
        headed, *saved, ending = forward_rule(
            head_arg, normed_in, own_decay, mixer_w, beta_w, taps, gain, state, halo
        )
        run = saved.pop()
        if stage < stages - 1:
            state = passed_along(ending, "seq", H)

    headed = headed.reshape(H, rows, DV)
    headed, up_near, out_near = lax.optimization_barrier((headed, up_near, out_near))
    upstream = with_siblings(up_near)
    own_headed = lax.all_to_all(headed, "seq", 0, 0, axis_index_groups=groups, tiled=True)
    residual, normed_own = out_rule(
        head_arg, with_siblings(out_near), own_headed, own_in, norm_mid[None, :]
    )
    across = swapped(normed_own, "seq", 6)
    near, far = swapped(normed_own, "seq", 2), swapped(normed_own, "seq", 4)
    mid_first = with_siblings([normed_own, across])
    up_first, up_last = upstream[:2] + upstream[6:], upstream[2:6]
    both_first, hidden_first, d_even, d_odd, even_first, odd_first = ffn_rule(
        mid_first, up_first, ffn_w
    )
    d_odd, near, far = lax.optimization_barrier((d_odd, near, far))
    own_pair = (d_even, swapped(d_odd, "seq", 1))
    across_sum = sum(each[1].astype(f32) for each in own_pair).astype(bf16)
    mid_last, across_sum = lax.optimization_barrier((with_siblings([near, far]), across_sum))
    across_sum = swapped(across_sum, "seq", 6)
    both_last, hidden_last, d_even, d_odd, even_last, odd_last = ffn_rule(
        mid_last, up_last, ffn_w
    )
    both_last, d_odd, across_sum = lax.optimization_barrier((both_last, d_odd, across_sum))
    ffn_partial = ffn_grads_rule(
        mid_first + mid_last,
        up_first + up_last,
        (both_first, both_last),
        (hidden_first, hidden_last),
    )
    handed, ffn_partial = lax.optimization_barrier((swapped(d_odd, "seq", 1), ffn_partial))
    ffn_summed = reduce_weight(ffn_partial)
    near_sum, far_sum = ((d_even[i].astype(f32) + handed[i].astype(f32)).astype(bf16) for i in (0, 1))
    received = [swapped(near_sum, "seq", 2), swapped(far_sum, "seq", 4), across_sum]
    ffn_own, ffn_across = pair_sums(even_first, swapped(odd_first, "seq", 1))
    ffn_handed = swapped(odd_last, "seq", 1)
    ffn_sums = [
        (even_last[i].astype(f32) + ffn_handed[i].astype(f32)).astype(bf16) for i in (0, 1)
    ] + ffn_across
    received, ffn_own, ffn_sums, own_pair = lax.optimization_barrier(
        (received, ffn_own, ffn_sums, own_pair)
    )
    own_sum = sum(each[0].astype(f32) for each in own_pair)
    d_normed_mid = total_of(own_sum, received)
    d_from_mid, grad_mid = rms_back(residual, norm_mid, d_normed_mid)
    d_residual = upstream_own.astype(f32) + d_from_mid
    branch, ffn_sums, ffn_summed = lax.optimization_barrier(
        (gather_blocks(d_residual.astype(bf16)), ffn_sums, ffn_summed)
    )
    ffn_received = exchanged(ffn_sums)
    ffn_spread = spread_grads(ffn_summed)

    d_end = jnp.zeros((seqs, DK, DV), f32)
    d_after = jnp.zeros((seqs, 8, WIDTH), f32)
    for stage in range(stages):
        d_all, grad_taps, grad_gain, d_start, d_before = backward_rule(
            head_arg, branch, mixer_w, saved, run, taps, gain, halo, d_end, d_after
        )
        if stage < stages - 1:
            d_end = passed_along(d_start, "seq", -H)
            d_after = passed_along(d_before, "seq", -H)
    d_all = d_all.reshape(H, rows, -1)

    mixer_partial, narrow = mixer_grads_rule(
        head_arg, normed_in, branch, d_all.reshape(all_rows, -1), headed, mixer_w, beta_w
    )
    mixer_partial, ffn_spread, ffn_received = lax.optimization_barrier(
        (mixer_partial, ffn_spread, ffn_received)
    )
    mixer_summed = reduce_weight(mixer_partial)
    ffn_grads = join_hidden_rule(ffn_spread, hidden_all, 3)

    d_even, d_odd = d_in_rule(d_all, mixer_w, beta_w)
    own_sum, sums = pair_sums(d_even, swapped(d_odd, "seq", 1))
    received, mixer_summed, narrow, ffn_grads = lax.optimization_barrier(
        (exchanged(sums), mixer_summed, narrow, ffn_grads)
    )
    layer_out = (residual + total_of(ffn_own, ffn_received)).astype(bf16).reshape(inputs.shape)
    mixer_grads = join_rule(spread_grads(mixer_summed), [DK, DK, DV, DV, DV])
    d_normed_in = total_of(own_sum, received)
    d_from_in, _ = rms_back(flat_in, norm_in, d_normed_in)
    grad_input = (d_residual + d_from_in).reshape(inputs.shape)

    small = jnp.concatenate(
        [
            grad_taps[:CONV].reshape(-1),
            narrow[:, 0],
            grad_gain[0],
            grad_mid,
            narrow[:, 1] / norm_in,
        ]
    ).reshape(-1, 128)
    step = 1
    while step < lax.axis_size("wt"):
        small = small + swapped(small, "wt", step)
        step *= 2
    step = H
    while step < peers:
        small = small + swapped(small, "seq", step)
        step *= 2
    small = small[None]
    for bits in (1, 2, 4):
        small = jnp.concatenate([small, swapped(small, "seq", bits)], axis=0)
    small = small[jnp.arange(H) ^ head].reshape(H, -1)
    ends = []
    for bound in (CONV * WIDTH, model, DV, model, model):
        ends.append(bound + (ends[-1] if ends else 0))
    taps_part = small[:, : ends[0]].reshape(H, CONV, WIDTH)

    def joined(pieces):
        return jnp.swapaxes(pieces, 0, 1).reshape(CONV, -1)

    grad_conv = jnp.concatenate(
        [
            joined(taps_part[:, :, :DK]),
            joined(taps_part[:, :, DK : 2 * DK]),
            joined(taps_part[:, :, 2 * DK :]),
        ],
        axis=1,
    )
    grad_beta = small[:, ends[0] : ends[1]].T
    shared = jnp.sum(small[:, ends[1] :], axis=0)
    return (
        layer_out,
        grad_input,
        *mixer_grads,
        *ffn_grads,
        grad_beta,
        grad_conv,
        shared[DV + model :],
        shared[DV : DV + model],
        shared[:DV],
    )


def solution(mesh):
    rows = P("wt", "seq", None)
    cut = P("wt", None)
    in_specs = (rows,) * 3 + (cut,) * 8 + (P(),) * 5
    out_specs = (rows,) * 2 + (cut,) * 8 + (P(),) * 5
    return jax.shard_map(shards, mesh=mesh, in_specs=in_specs, out_specs=out_specs, check_vma=False)
```
